256 devices in a mesh: batch: 16 (over y, x_hi, core), feat: 16 (over z, x_lo).
Axes of the slice: x: 4 (x_hi: 2, x_lo: 2; x = x_hi * 2 + x_lo), y: 4, z: 8, core: 2. Of those that a mesh axis runs over, the one named last changes fastest.
Arguments:
- embedding: bfloat16 [1024, 131072], P('feat', 'batch'), may hold values from -6 to 6
- self_weight: bfloat16 [1024, 128], P('feat'), may hold values from -0.1875 to 0.1875
- neighbor_weight: bfloat16 [1024, 128], P('feat'), may hold values from -0.1875 to 0.1875
- up_weight: bfloat16 [128, 1024], replicated, may hold values from -0.5 to 0.5
- down_weight: bfloat16 [1024, 128], replicated, may hold values from -0.1875 to 0.1875
- source_tiles: int32 [2, 8, 64], P(None, None, 'batch'), may hold values from 0 to 7
- neighbor_rows: int32 [2, 8, 16, 16384], P(None, None, None, 'batch'), may hold values from 0 to 1023
- slot_mask: int32 [2, 8, 16384], P(None, None, 'batch'), may hold values 0 or 1
- dest_rows: int32 [2, 16384], P(None, 'batch'), may hold values from 0 to 8191
- owner_order: int32 [2, 16, 1024], P(None, 'batch'), may hold values from 0 to 1023, each once within a row
- output_grad: bfloat16 [2, 16384, 128], P(None, ('batch', 'feat')), may hold values from -16 to 16
Outputs:
- embedding_grad: float32 [1024, 131072], P('feat', 'batch')
- self_grad: float32 [1024, 128], P('feat')
- neighbor_grad: float32 [1024, 128], P('feat')
- up_grad: float32 [128, 1024], replicated
- down_grad: float32 [1024, 128], replicated
The draws below stay inside these ranges and needn't reach their ends.
Inputs may be any that keep to these rules, and one draw needn't show every extreme that they name: `source_tiles`: numbers of tiles within the group's own 8 source tiles. `neighbor_rows`: rows within the slot's source tile. `dest_rows`: rows within the group's own table. `owner_order`: each of a group's 1024 destinations once per microbatch.
All inputs are finite; a program needn't handle non-finite values. No bound on the sum of `slot_mask` on one device may be relied on, other than what follows from the above.
Results may differ from the reference program's by a relative error of at most 0.006.
Values may be sent and summed in bfloat16 or wider, within the bound.
A program may use at most 128 MiB of HBM per device.

```python
import math
import jax
import jax.numpy as jnp
from jax import lax

F = 1024
H = 128
FF = 1024
DST = 1024
NSRC_T = 8
M = 2
TD = 256
TS = 1024
K = 8
NB = 16
NT = 4
SRC_G = 8192
N_BATCH = 16


def plant(entries, own_key, low, top_value):
    shape = entries.shape
    place = [jax.random.randint(jax.random.fold_in(own_key, axis), (), 0, shape[axis]) for axis in range(len(shape))]
    entries = entries.at[tuple(place)].set(low)
    longest = shape.index(max(shape))
    place[longest] = (place[longest] + 1) % shape[longest]
    return entries.at[tuple(place)].set(top_value)


def level_of(own_key, shape, split, smallest, high):
    def one(position, parts):
        heights = jax.random.uniform(jax.random.fold_in(jax.random.fold_in(own_key, 6), position), (parts,), jnp.float32, smallest / len(split), high / len(split))
        return jnp.repeat(jnp.exp(heights), shape[position] // parts).reshape((-1,) + (1,) * (len(shape) - position - 1))

    loudness = one(*split[0])
    for cut in split[1:]:
        loudness = loudness * one(*cut)
    return loudness


def noise(own_key, extent, scale, limit, cuts=(), held_as=jnp.bfloat16):
    values = scale * jax.random.normal(own_key, extent, jnp.float32)
    if cuts:
        values = values * level_of(own_key, extent, cuts, -0.22, 0.18)
    return jnp.clip(values, -limit, limit).astype(held_as)


def setup_inputs(seed: int = 0) -> dict:
    streams_of = jax.random.split(jax.random.key(seed), 12)
    embedding = noise(streams_of[0], (F, SRC_G * N_BATCH), 1.0, 6.0, ((0, 16), (1, 16)))
    self_weight = noise(streams_of[1], (F, H), F ** -0.5, 0.1875, ((0, 16),))
    neighbor_weight = noise(streams_of[2], (F, H), F ** -0.5, 0.1875, ((0, 16),))
    up_weight = noise(streams_of[3], (H, FF), H ** -0.5, 0.5)
    down_weight = noise(streams_of[4], (FF, H), FF ** -0.5, 0.1875)
    source_tiles = plant(jax.random.randint(streams_of[5], (M, K, NT * N_BATCH), 0, NSRC_T), jax.random.fold_in(streams_of[5], 1), 0, NSRC_T - 1).astype(jnp.int32)
    neighbor_rows = plant(jax.random.randint(streams_of[6], (M, K, NB, DST * N_BATCH), 0, TS), jax.random.fold_in(streams_of[6], 1), 0, TS - 1).astype(jnp.int32)
    slot_mask = plant((jax.random.randint(streams_of[7], (M, K, DST * N_BATCH), 0, 4) < 3).astype(jnp.int32), jax.random.fold_in(streams_of[7], 1), 0, 1)
    dest_rows = plant(jax.random.randint(streams_of[8], (M, DST * N_BATCH), 0, NSRC_T * TS), jax.random.fold_in(streams_of[8], 1), 0, (NSRC_T * TS) - 1).astype(jnp.int32)
    owner_order = jax.vmap(lambda own: jax.random.permutation(own, DST))(jax.random.split(streams_of[9], M * N_BATCH)).reshape((M, N_BATCH, DST)).astype(jnp.int32)
    output_grad = noise(streams_of[10], (M, DST * N_BATCH, H), 4.0, 16.0, ((1, 256),))
    return {"embedding": embedding, "self_weight": self_weight, "neighbor_weight": neighbor_weight, "up_weight": up_weight, "down_weight": down_weight, "source_tiles": source_tiles, "neighbor_rows": neighbor_rows, "slot_mask": slot_mask, "dest_rows": dest_rows, "owner_order": owner_order, "output_grad": output_grad}


def gelu_slope(values):
    result, pullback = jax.vjp(jax.nn.gelu, values)
    return (result, pullback(jnp.ones_like(values))[0])

def adjacency(rows_block, valid_block):
    row_total = rows_block.shape[2]
    slot_index = jnp.broadcast_to(jnp.arange(K, dtype=jnp.int32)[:, None, None], rows_block.shape)
    dest_index = jnp.broadcast_to(jnp.arange(row_total, dtype=jnp.int32)[None, None, :], rows_block.shape)
    weights = jnp.broadcast_to(valid_block[:, None, :], rows_block.shape).astype(jnp.bfloat16)
    zero_tiles = jnp.zeros((K, row_total, TS), jnp.bfloat16)
    return zero_tiles.at[slot_index, dest_index, rows_block.astype(jnp.int32)].add(weights)

def mlp_pass(hidden, target, up_weight, down_weight):
    first_value, first_slope = gelu_slope(hidden)
    first_act = first_value.astype(jnp.bfloat16)
    inner_pre = jnp.dot(first_act, up_weight, preferred_element_type=jnp.float32)
    inner_value, inner_slope = gelu_slope(inner_pre)
    inner_act = inner_value.astype(jnp.bfloat16)
    down_part = jnp.dot(inner_act.T, target, preferred_element_type=jnp.float32)
    inner_grad = (jnp.dot(target, down_weight.T, preferred_element_type=jnp.float32) * inner_slope).astype(jnp.bfloat16)
    up_part = jnp.dot(first_act.T, inner_grad, preferred_element_type=jnp.float32)
    hidden_grad = (jnp.dot(inner_grad, up_weight.T, preferred_element_type=jnp.float32) * first_slope).astype(jnp.bfloat16)
    return (hidden_grad, up_part, down_part)

def reference(embedding, self_weight, neighbor_weight, up_weight, down_weight, source_tiles, neighbor_rows, slot_mask, dest_rows, owner_order, output_grad):
    agg_scale = 1.0 / math.sqrt(K * NB)
    norm_factor = 1.0 / math.sqrt(M * DST * N_BATCH)
    tables = embedding.T.reshape(N_BATCH, SRC_G, F)
    tiles_all = source_tiles.reshape(M, K, N_BATCH, NT).transpose(2, 0, 1, 3)
    rows_all = neighbor_rows.reshape(M, K, NB, N_BATCH, DST).transpose(3, 0, 1, 2, 4)
    valid_all = slot_mask.reshape(M, K, N_BATCH, DST).transpose(2, 0, 1, 3)
    dest_all = dest_rows.reshape(M, N_BATCH, DST).transpose(1, 0, 2)
    order_all = owner_order.transpose(1, 0, 2)
    grad_all = output_grad.reshape(M, N_BATCH, DST, H).transpose(1, 0, 2, 3)

    def group_step(totals, group_data):
        self_sum, neighbor_sum, up_sum, down_sum = totals
        table_rows, tile_group, rows_group, valid_group, dest_group, order_group, grad_group = group_data
        table_grad = jnp.zeros((SRC_G, F), jnp.float32)
        for micro_index in range(M):
            tile_ids = tile_group[micro_index]
            counts = adjacency(rows_group[micro_index], valid_group[micro_index]).reshape(K, NT, TD, TS)
            pieces = table_rows.reshape(NSRC_T, TS, F)[tile_ids]
            summed = jnp.einsum('ktds,ktsf->tdf', counts.astype(jnp.float32), pieces.astype(jnp.float32))
            gathered = (summed * agg_scale).reshape(DST, F).astype(jnp.bfloat16)
            own_rows = table_rows[dest_group[micro_index]]
            hidden = jnp.dot(own_rows, self_weight, preferred_element_type=jnp.float32) + jnp.dot(gathered, neighbor_weight, preferred_element_type=jnp.float32)
            row_order = order_group[micro_index]
            ordered_grad, up_part, down_part = mlp_pass(hidden[row_order], grad_group[micro_index], up_weight, down_weight)
            up_sum = up_sum + up_part
            down_sum = down_sum + down_part
            hidden_grad = jnp.zeros((DST, H), jnp.bfloat16).at[row_order].set(ordered_grad)
            self_sum = self_sum + jnp.dot(own_rows.T, hidden_grad, preferred_element_type=jnp.float32)
            neighbor_sum = neighbor_sum + jnp.dot(gathered.T, hidden_grad, preferred_element_type=jnp.float32)
            table_grad = table_grad.at[dest_group[micro_index]].add(jnp.dot(hidden_grad, self_weight.T, preferred_element_type=jnp.float32))
            back_grad = jnp.dot(hidden_grad, neighbor_weight.T, preferred_element_type=jnp.float32).astype(jnp.bfloat16).reshape(NT, TD, F)
            spread = jnp.einsum('ktds,tdf->ktsf', counts.astype(jnp.float32), back_grad.astype(jnp.float32)) * agg_scale
            table_grad = table_grad.reshape(NSRC_T, TS, F).at[tile_ids].add(spread).reshape(SRC_G, F)
        return ((self_sum, neighbor_sum, up_sum, down_sum), table_grad)
    start_sums = (jnp.zeros((F, H), jnp.float32), jnp.zeros((F, H), jnp.float32), jnp.zeros((H, FF), jnp.float32), jnp.zeros((FF, H), jnp.float32))
    sums_out, grads_out = lax.scan(group_step, start_sums, (tables, tiles_all, rows_all, valid_all, dest_all, order_all, grad_all))
    self_sum, neighbor_sum, up_sum, down_sum = sums_out
    embedding_grad = grads_out.reshape(N_BATCH * SRC_G, F).T
    return (embedding_grad, self_sum * norm_factor, neighbor_sum * norm_factor, up_sum * norm_factor, down_sum * norm_factor)
```

```python
import functools
import math

import jax
import jax.numpy as jnp
from jax import lax
from jax.experimental import pallas as pl
from jax.experimental.pallas import tpu as pltpu
from jax.sharding import PartitionSpec as P

H = 128
TD = 256
TS = 1024
K = 8
NB = 16
CS = 64


def gelu_slope(values):
    result, pullback = jax.vjp(jax.nn.gelu, values)
    return (result, pullback(jnp.ones_like(values))[0])


def mlp_pass(hidden, target, up_weight, down_weight):
    first_value, first_slope = gelu_slope(hidden)
    first_act = first_value.astype(jnp.bfloat16)
    inner_pre = jnp.dot(first_act, up_weight, preferred_element_type=jnp.float32)
    inner_value, inner_slope = gelu_slope(inner_pre)
    inner_act = inner_value.astype(jnp.bfloat16)
    down_part = jnp.dot(inner_act.T, target, preferred_element_type=jnp.float32)
    inner_grad = (
        jnp.dot(target, down_weight.T, preferred_element_type=jnp.float32) * inner_slope
    ).astype(jnp.bfloat16)
    up_part = jnp.dot(first_act.T, inner_grad, preferred_element_type=jnp.float32)
    hidden_grad = (
        jnp.dot(inner_grad, up_weight.T, preferred_element_type=jnp.float32) * first_slope
    ).astype(jnp.bfloat16)
    return (hidden_grad, up_part, down_part)


def agg_kernel(agg_scale, k_total, nt, tiles_ref, emb_ref, rows_ref, mask_ref, counts_ref, agg_ref, acc_ref):
    k = pl.program_id(2)

    @pl.when(k == 0)
    def _():
        acc_ref[...] = jnp.zeros_like(acc_ref)

    msk = mask_ref[0, 0]

    def chunk(c, carry):
        start = pl.multiple_of(c * CS, CS)
        iota = lax.broadcasted_iota(jnp.int32, (CS, TD), 0) + start
        cnt = jnp.zeros((CS, TD), jnp.int32)
        for j in range(NB):
            cnt = cnt + (rows_ref[0, 0, j : j + 1, :] == iota).astype(jnp.int32)
        counts_ref[0, 0, 0, pl.ds(start, CS), :] = (cnt * msk).astype(jnp.bfloat16)
        return carry

    lax.fori_loop(0, TS // CS, chunk, 0)
    acc_ref[...] += jnp.dot(emb_ref[...], counts_ref[0, 0, 0], preferred_element_type=jnp.float32)

    @pl.when(k == k_total - 1)
    def _():
        agg_ref[0] = (acc_ref[...] * agg_scale).astype(jnp.bfloat16)


def aggregate(embedding, tiles_flat, neighbor_rows, slot_mask, agg_scale):
    columns = embedding.shape[0]
    micro_total, k_total, nb, dest_total = neighbor_rows.shape
    nt = dest_total // TD
    mask4 = slot_mask.reshape(micro_total, k_total, 1, dest_total)
    grid_spec = pltpu.PrefetchScalarGridSpec(
        num_scalar_prefetch=1,
        grid=(micro_total, nt, k_total),
        in_specs=[
            pl.BlockSpec((columns, TS), lambda m, t, k, tiles: (0, tiles[(m * k_total + k) * nt + t])),
            pl.BlockSpec((1, 1, nb, TD), lambda m, t, k, tiles: (m, k, 0, t)),
            pl.BlockSpec((1, 1, 1, TD), lambda m, t, k, tiles: (m, k, 0, t)),
        ],
        out_specs=[
            pl.BlockSpec((1, 1, 1, TS, TD), lambda m, t, k, tiles: (m, k, t, 0, 0)),
            pl.BlockSpec((1, columns, TD), lambda m, t, k, tiles: (m, 0, t)),
        ],
        scratch_shapes=[pltpu.VMEM((columns, TD), jnp.float32)],
    )
    return pl.pallas_call(
        functools.partial(agg_kernel, agg_scale, k_total, nt),
        grid_spec=grid_spec,
        out_shape=[
            jax.ShapeDtypeStruct((micro_total, k_total, nt, TS, TD), jnp.bfloat16),
            jax.ShapeDtypeStruct((micro_total, columns, dest_total), jnp.bfloat16),
        ],
        compiler_params=pltpu.CompilerParams(
            dimension_semantics=("arbitrary", "arbitrary", "arbitrary")
        ),
    )(tiles_flat, embedding, neighbor_rows, mask4)


def spread_kernel(agg_scale, k_total, nt, tiles_ref, counts_ref, back_ref, tg_ref):
    m = pl.program_id(0)
    t = pl.program_id(1)
    k = pl.program_id(2)

    @pl.when((m == 0) & (t == 0) & (k == 0))
    def _():
        tg_ref[...] = jnp.zeros_like(tg_ref)

    tile = tiles_ref[(m * k_total + k) * nt + t]
    start = pl.multiple_of(tile * TS, TS)
    part = jnp.dot(counts_ref[0, 0, 0], back_ref[0], preferred_element_type=jnp.float32)
    tg_ref[pl.ds(start, TS), :] += part * agg_scale


def spread(counts, back, tiles_flat, source_total, agg_scale):
    micro_total, k_total, nt = counts.shape[:3]
    columns = back.shape[2]
    grid_spec = pltpu.PrefetchScalarGridSpec(
        num_scalar_prefetch=1,
        grid=(micro_total, nt, k_total),
        in_specs=[
            pl.BlockSpec((1, 1, 1, TS, TD), lambda m, t, k, tiles: (m, k, t, 0, 0)),
            pl.BlockSpec((1, TD, columns), lambda m, t, k, tiles: (m, t, 0)),
        ],
        out_specs=pl.BlockSpec((source_total, columns), lambda m, t, k, tiles: (0, 0)),
    )
    return pl.pallas_call(
        functools.partial(spread_kernel, agg_scale, k_total, nt),
        grid_spec=grid_spec,
        out_shape=jax.ShapeDtypeStruct((source_total, columns), jnp.float32),
        compiler_params=pltpu.CompilerParams(
            dimension_semantics=("arbitrary", "arbitrary", "arbitrary"),
            vmem_limit_bytes=48 * 1024 * 1024,
        ),
    )(tiles_flat, counts, back)


def local(
    embedding,
    self_weight,
    neighbor_weight,
    up_weight,
    down_weight,
    source_tiles,
    neighbor_rows,
    slot_mask,
    dest_rows,
    owner_order,
    output_grad,
):
    batch_total = lax.axis_size("batch")
    columns, source_total = embedding.shape
    micro_total = source_tiles.shape[0]
    dest_total = dest_rows.shape[1]
    agg_scale = 1.0 / math.sqrt(K * NB)
    norm_factor = 1.0 / math.sqrt(micro_total * dest_total * batch_total)
    tiles_flat = source_tiles.reshape(-1)

    target_all = lax.all_gather(output_grad, "feat", axis=1, tiled=True)
    counts, agg_t = aggregate(embedding, tiles_flat, neighbor_rows, slot_mask, agg_scale)
    table = embedding.T
    own_all = [table[dest_rows[m]] for m in range(micro_total)]
    partial = jnp.stack(
        [
            jnp.dot(own_all[m], self_weight, preferred_element_type=jnp.float32)
            + lax.dot_general(
                agg_t[m], neighbor_weight, (((0,), (0,)), ((), ())),
                preferred_element_type=jnp.float32,
            )
            for m in range(micro_total)
        ]
    )
    hidden_all = lax.psum(partial, "feat")

    up_sum = jnp.zeros(up_weight.shape, jnp.float32)
    down_sum = jnp.zeros(down_weight.shape, jnp.float32)
    self_sum = jnp.zeros((columns, H), jnp.float32)
    neighbor_sum = jnp.zeros((columns, H), jnp.float32)
    backs = []
    own_grads = []
    for m in range(micro_total):
        row_order = owner_order[m, 0]
        target = jnp.zeros(target_all.shape[1:], target_all.dtype).at[row_order].set(target_all[m])
        hidden_grad, up_part, down_part = mlp_pass(hidden_all[m], target, up_weight, down_weight)
        up_sum = up_sum + up_part
        down_sum = down_sum + down_part
        self_sum = self_sum + jnp.dot(own_all[m].T, hidden_grad, preferred_element_type=jnp.float32)
        neighbor_sum = neighbor_sum + jnp.dot(agg_t[m], hidden_grad, preferred_element_type=jnp.float32)
        backs.append(
            jnp.dot(hidden_grad, neighbor_weight.T, preferred_element_type=jnp.float32).astype(jnp.bfloat16)
        )
        own_grads.append(jnp.dot(hidden_grad, self_weight.T, preferred_element_type=jnp.float32))

    sizes = [up_sum.size, down_sum.size, self_sum.size, neighbor_sum.size]
    line = jnp.concatenate([up_sum.ravel(), down_sum.ravel(), self_sum.ravel(), neighbor_sum.ravel()])
    line = lax.psum(line, "batch")
    ends = [0]
    for s in sizes:
        ends.append(ends[-1] + s)
    up_sum = line[ends[0] : ends[1]].reshape(up_weight.shape)
    down_sum = line[ends[1] : ends[2]].reshape(down_weight.shape)
    self_sum = line[ends[2] : ends[3]].reshape(columns, H)
    neighbor_sum = line[ends[3] : ends[4]].reshape(columns, H)

    table_grad = spread(jnp.asarray(counts), jnp.stack(backs), tiles_flat, source_total, agg_scale)
    for m in range(micro_total):
        table_grad = table_grad.at[dest_rows[m]].add(own_grads[m])
    return (
        table_grad.T,
        self_sum * norm_factor,
        neighbor_sum * norm_factor,
        up_sum * norm_factor,
        down_sum * norm_factor,
    )


def solution(mesh):
    in_specs = (
        P("feat", "batch"),
        P("feat", None),
        P("feat", None),
        P(),
        P(),
        P(None, None, "batch"),
        P(None, None, None, "batch"),
        P(None, None, "batch"),
        P(None, "batch"),
        P(None, "batch", None),
        P(None, ("batch", "feat"), None),
    )
    out_specs = (P("feat", "batch"), P("feat", None), P("feat", None), P(), P())
    return jax.shard_map(local, mesh=mesh, in_specs=in_specs, out_specs=out_specs, check_vma=False)
```

```python
import functools
import math

import jax
import jax.numpy as jnp
from jax import lax
from jax.experimental import pallas as pl
from jax.experimental.pallas import tpu as pltpu
from jax.sharding import PartitionSpec as P

H = 128
TD = 256
TS = 1024
K = 8
NB = 16
CS = 64


def gelu_slope(values):
    result, pullback = jax.vjp(jax.nn.gelu, values)
    return (result, pullback(jnp.ones_like(values))[0])


def mlp_pass(hidden, target, up_weight, down_weight):
    first_value, first_slope = gelu_slope(hidden)
    first_act = first_value.astype(jnp.bfloat16)
    inner_pre = jnp.dot(first_act, up_weight, preferred_element_type=jnp.float32)
    inner_value, inner_slope = gelu_slope(inner_pre)
    inner_act = inner_value.astype(jnp.bfloat16)
    down_part = jnp.dot(inner_act.T, target, preferred_element_type=jnp.float32)
    inner_grad = (
        jnp.dot(target, down_weight.T, preferred_element_type=jnp.float32) * inner_slope
    ).astype(jnp.bfloat16)
    up_part = jnp.dot(first_act.T, inner_grad, preferred_element_type=jnp.float32)
    hidden_grad = (
        jnp.dot(inner_grad, up_weight.T, preferred_element_type=jnp.float32) * first_slope
    ).astype(jnp.bfloat16)
    return (hidden_grad, up_part, down_part)


def summed_over(x, axis):
    n = lax.axis_size(axis)
    flat = x.reshape(n, -1)
    mine = lax.all_to_all(flat, axis, 0, 0, tiled=True).reshape(n, -1).sum(axis=0)
    spread_back = lax.all_to_all(jnp.broadcast_to(mine[None], (n, mine.size)), axis, 0, 0, tiled=True)
    return spread_back.reshape(x.shape)


def gathered_over(x, axis, dim):
    n = lax.axis_size(axis)
    pieces = lax.all_to_all(jnp.broadcast_to(x[None], (n, *x.shape)), axis, 0, 0, tiled=True)
    pieces = jnp.moveaxis(pieces, 0, dim)
    shape = pieces.shape
    return pieces.reshape(*shape[:dim], shape[dim] * shape[dim + 1], *shape[dim + 2 :])


def agg_kernel(agg_scale, k_total, nt, tiles_ref, emb_ref, rows_ref, mask_ref, counts_ref, agg_ref, acc_ref):
    k = pl.program_id(2)

    @pl.when(k == 0)
    def _():
        acc_ref[...] = jnp.zeros_like(acc_ref)

    msk = mask_ref[0, 0]

    def chunk(c, carry):
        start = pl.multiple_of(c * CS, CS)
        iota = lax.broadcasted_iota(jnp.int32, (CS, TD), 0) + start
        cnt = jnp.zeros((CS, TD), jnp.int32)
        for j in range(NB):
            cnt = cnt + (rows_ref[0, 0, j : j + 1, :] == iota).astype(jnp.int32)
        counts_ref[0, 0, 0, pl.ds(start, CS), :] = (cnt * msk).astype(jnp.bfloat16)
        return carry

    lax.fori_loop(0, TS // CS, chunk, 0)
    acc_ref[...] += jnp.dot(emb_ref[...], counts_ref[0, 0, 0], preferred_element_type=jnp.float32)

    @pl.when(k == k_total - 1)
    def _():
        agg_ref[0] = (acc_ref[...] * agg_scale).astype(jnp.bfloat16)


def aggregate(embedding, tiles_flat, neighbor_rows, slot_mask, agg_scale):
    columns = embedding.shape[0]
    micro_total, k_total, nb, dest_total = neighbor_rows.shape
    nt = dest_total // TD
    mask4 = slot_mask.reshape(micro_total, k_total, 1, dest_total)
    grid_spec = pltpu.PrefetchScalarGridSpec(
        num_scalar_prefetch=1,
        grid=(micro_total, nt, k_total),
        in_specs=[
            pl.BlockSpec((columns, TS), lambda m, t, k, tiles: (0, tiles[(m * k_total + k) * nt + t])),
            pl.BlockSpec((1, 1, nb, TD), lambda m, t, k, tiles: (m, k, 0, t)),
            pl.BlockSpec((1, 1, 1, TD), lambda m, t, k, tiles: (m, k, 0, t)),
        ],
        out_specs=[
            pl.BlockSpec((1, 1, 1, TS, TD), lambda m, t, k, tiles: (m, k, t, 0, 0)),
            pl.BlockSpec((1, columns, TD), lambda m, t, k, tiles: (m, 0, t)),
        ],
        scratch_shapes=[pltpu.VMEM((columns, TD), jnp.float32)],
    )
    return pl.pallas_call(
        functools.partial(agg_kernel, agg_scale, k_total, nt),
        grid_spec=grid_spec,
        out_shape=[
            jax.ShapeDtypeStruct((micro_total, k_total, nt, TS, TD), jnp.bfloat16),
            jax.ShapeDtypeStruct((micro_total, columns, dest_total), jnp.bfloat16),
        ],
        compiler_params=pltpu.CompilerParams(
            dimension_semantics=("arbitrary", "arbitrary", "arbitrary")
        ),
    )(tiles_flat, embedding, neighbor_rows, mask4)


def spread_kernel(agg_scale, k_total, nt, tiles_ref, counts_ref, back_ref, tg_ref):
    m = pl.program_id(0)
    t = pl.program_id(1)
    k = pl.program_id(2)

    @pl.when((m == 0) & (t == 0) & (k == 0))
    def _():
        tg_ref[...] = jnp.zeros_like(tg_ref)

    tile = tiles_ref[(m * k_total + k) * nt + t]
    start = pl.multiple_of(tile * TS, TS)
    part = jnp.dot(counts_ref[0, 0, 0], back_ref[0], preferred_element_type=jnp.float32)
    tg_ref[pl.ds(start, TS), :] += part * agg_scale


def spread(counts, back, tiles_flat, source_total, agg_scale):
    micro_total, k_total, nt = counts.shape[:3]
    columns = back.shape[2]
    grid_spec = pltpu.PrefetchScalarGridSpec(
        num_scalar_prefetch=1,
        grid=(micro_total, nt, k_total),
        in_specs=[
            pl.BlockSpec((1, 1, 1, TS, TD), lambda m, t, k, tiles: (m, k, t, 0, 0)),
            pl.BlockSpec((1, TD, columns), lambda m, t, k, tiles: (m, t, 0)),
        ],
        out_specs=pl.BlockSpec((source_total, columns), lambda m, t, k, tiles: (0, 0)),
    )
    return pl.pallas_call(
        functools.partial(spread_kernel, agg_scale, k_total, nt),
        grid_spec=grid_spec,
        out_shape=jax.ShapeDtypeStruct((source_total, columns), jnp.float32),
        compiler_params=pltpu.CompilerParams(
            dimension_semantics=("arbitrary", "arbitrary", "arbitrary"),
            vmem_limit_bytes=48 * 1024 * 1024,
        ),
    )(tiles_flat, counts, back)


def local(
    embedding,
    self_weight,
    neighbor_weight,
    up_weight,
    down_weight,
    source_tiles,
    neighbor_rows,
    slot_mask,
    dest_rows,
    owner_order,
    output_grad,
):
    batch_total = lax.axis_size("batch")
    columns, source_total = embedding.shape
    micro_total = source_tiles.shape[0]
    dest_total = dest_rows.shape[1]
    agg_scale = 1.0 / math.sqrt(K * NB)
    norm_factor = 1.0 / math.sqrt(micro_total * dest_total * batch_total)
    tiles_flat = source_tiles.reshape(-1)

    target_all = gathered_over(output_grad, "feat", 1)
    counts, agg_t = aggregate(embedding, tiles_flat, neighbor_rows, slot_mask, agg_scale)
    table = embedding.T
    own_all = [table[dest_rows[m]] for m in range(micro_total)]
    partial = jnp.stack(
        [
            jnp.dot(own_all[m], self_weight, preferred_element_type=jnp.float32)
            + lax.dot_general(
                agg_t[m], neighbor_weight, (((0,), (0,)), ((), ())),
                preferred_element_type=jnp.float32,
            )
            for m in range(micro_total)
        ]
    )
    hidden_all = summed_over(partial, "feat")

    up_sum = jnp.zeros(up_weight.shape, jnp.float32)
    down_sum = jnp.zeros(down_weight.shape, jnp.float32)
    self_sum = jnp.zeros((columns, H), jnp.float32)
    neighbor_sum = jnp.zeros((columns, H), jnp.float32)
    backs = []
    own_grads = []
    for m in range(micro_total):
        row_order = owner_order[m, 0]
        target = jnp.zeros(target_all.shape[1:], target_all.dtype).at[row_order].set(target_all[m])
        hidden_grad, up_part, down_part = mlp_pass(hidden_all[m], target, up_weight, down_weight)
        up_sum = up_sum + up_part
        down_sum = down_sum + down_part
        self_sum = self_sum + jnp.dot(own_all[m].T, hidden_grad, preferred_element_type=jnp.float32)
        neighbor_sum = neighbor_sum + jnp.dot(agg_t[m], hidden_grad, preferred_element_type=jnp.float32)
        backs.append(
            jnp.dot(hidden_grad, neighbor_weight.T, preferred_element_type=jnp.float32).astype(jnp.bfloat16)
        )
        own_grads.append(jnp.dot(hidden_grad, self_weight.T, preferred_element_type=jnp.float32))

    sizes = [up_sum.size, down_sum.size, self_sum.size, neighbor_sum.size]
    line = jnp.concatenate([up_sum.ravel(), down_sum.ravel(), self_sum.ravel(), neighbor_sum.ravel()])
    line = summed_over(line, "batch")
    ends = [0]
    for s in sizes:
        ends.append(ends[-1] + s)
    up_sum = line[ends[0] : ends[1]].reshape(up_weight.shape)
    down_sum = line[ends[1] : ends[2]].reshape(down_weight.shape)
    self_sum = line[ends[2] : ends[3]].reshape(columns, H)
    neighbor_sum = line[ends[3] : ends[4]].reshape(columns, H)

    table_grad = spread(jnp.asarray(counts), jnp.stack(backs), tiles_flat, source_total, agg_scale)
    for m in range(micro_total):
        table_grad = table_grad.at[dest_rows[m]].add(own_grads[m])
    return (
        table_grad.T,
        self_sum * norm_factor,
        neighbor_sum * norm_factor,
        up_sum * norm_factor,
        down_sum * norm_factor,
    )


def solution(mesh):
    in_specs = (
        P("feat", "batch"),
        P("feat", None),
        P("feat", None),
        P(),
        P(),
        P(None, None, "batch"),
        P(None, None, None, "batch"),
        P(None, None, "batch"),
        P(None, "batch"),
        P(None, "batch", None),
        P(None, ("batch", "feat"), None),
    )
    out_specs = (P("feat", "batch"), P("feat", None), P("feat", None), P(), P())
    return jax.shard_map(local, mesh=mesh, in_specs=in_specs, out_specs=out_specs, check_vma=False)
```

```python
import functools
import math

import jax
import jax.numpy as jnp
from jax import lax
from jax.experimental import pallas as pl
from jax.experimental.pallas import tpu as pltpu
from jax.sharding import PartitionSpec as P

H = 128
TD = 256
TS = 1024
K = 8
NB = 16
CS = 128


def gelu_slope(values):
    result, pullback = jax.vjp(jax.nn.gelu, values)
    return (result, pullback(jnp.ones_like(values))[0])


def mlp_pass(hidden, target, up_weight, down_weight):
    first_value, first_slope = gelu_slope(hidden)
    first_act = first_value.astype(jnp.bfloat16)
    inner_pre = jnp.dot(first_act, up_weight, preferred_element_type=jnp.float32)
    inner_value, inner_slope = gelu_slope(inner_pre)
    inner_act = inner_value.astype(jnp.bfloat16)
    down_part = jnp.dot(inner_act.T, target, preferred_element_type=jnp.float32)
    inner_grad = (
        jnp.dot(target, down_weight.T, preferred_element_type=jnp.float32) * inner_slope
    ).astype(jnp.bfloat16)
    up_part = jnp.dot(first_act.T, inner_grad, preferred_element_type=jnp.float32)
    hidden_grad = (
        jnp.dot(inner_grad, up_weight.T, preferred_element_type=jnp.float32) * first_slope
    ).astype(jnp.bfloat16)
    return (hidden_grad, up_part, down_part)


def summed_over(x, axis):
    n = lax.axis_size(axis)
    flat = x.reshape(n, -1)
    mine = lax.all_to_all(flat, axis, 0, 0, tiled=True).reshape(n, -1).sum(axis=0)
    spread_back = lax.all_to_all(jnp.broadcast_to(mine[None], (n, mine.size)), axis, 0, 0, tiled=True)
    return spread_back.reshape(x.shape)


def gathered_over(x, axis, dim):
    n = lax.axis_size(axis)
    pieces = lax.all_to_all(jnp.broadcast_to(x[None], (n, *x.shape)), axis, 0, 0, tiled=True)
    pieces = jnp.moveaxis(pieces, 0, dim)
    shape = pieces.shape
    return pieces.reshape(*shape[:dim], shape[dim] * shape[dim + 1], *shape[dim + 2 :])


def agg_kernel(agg_scale, k_total, nt, tiles_ref, emb_ref, rows_ref, mask_ref, counts_ref, agg_ref, acc_ref):
    k = pl.program_id(1)

    @pl.when(k == 0)
    def _():
        acc_ref[...] = jnp.zeros_like(acc_ref)

    msk = mask_ref[0, 0].astype(jnp.bfloat16)
    rows = rows_ref[0, 0]
    local_iota = lax.broadcasted_iota(jnp.int32, (CS, TD), 0).astype(jnp.bfloat16)
    one = jnp.ones((CS, TD), jnp.bfloat16)
    zero = jnp.zeros((CS, TD), jnp.bfloat16)

    def chunk(c, carry):
        start = pl.multiple_of(c * CS, CS)
        local = (rows - start).astype(jnp.float32)
        cnt = zero
        for j in range(NB):
            here = local[j : j + 1, :].astype(jnp.bfloat16)
            cnt = cnt + jnp.where(here == local_iota, one, zero)
        counts_ref[0, 0, pl.ds(start, CS), :] = cnt * msk
        return carry

    lax.fori_loop(0, TS // CS, chunk, 0)
    acc_ref[...] += jnp.dot(emb_ref[...], counts_ref[0, 0], preferred_element_type=jnp.float32)

    @pl.when(k == k_total - 1)
    def _():
        agg_ref[...] = (acc_ref[...] * agg_scale).astype(jnp.bfloat16)


def aggregate(embedding, tiles_flat, neighbor_rows, slot_mask, agg_scale):
    columns, source_total = embedding.shape
    k_total, nb, dest_total = neighbor_rows.shape
    nt = dest_total // TD
    mask4 = slot_mask.reshape(k_total, 1, 1, dest_total)
    rows4 = neighbor_rows.reshape(k_total, 1, nb, dest_total)
    grid_spec = pltpu.PrefetchScalarGridSpec(
        num_scalar_prefetch=1,
        grid=(nt, k_total),
        in_specs=[
            pl.BlockSpec((columns, TS), lambda t, k, tiles: (0, tiles[k * nt + t])),
            pl.BlockSpec((1, 1, nb, TD), lambda t, k, tiles: (k, 0, 0, t)),
            pl.BlockSpec((1, 1, 1, TD), lambda t, k, tiles: (k, 0, 0, t)),
        ],
        out_specs=[
            pl.BlockSpec((1, 1, TS, TD), lambda t, k, tiles: (k, t, 0, 0)),
            pl.BlockSpec((columns, TD), lambda t, k, tiles: (0, t)),
        ],
        scratch_shapes=[pltpu.VMEM((columns, TD), jnp.float32)],
    )
    work = k_total * dest_total * TS
    return pl.pallas_call(
        functools.partial(agg_kernel, agg_scale, k_total, nt),
        grid_spec=grid_spec,
        out_shape=[
            jax.ShapeDtypeStruct((k_total, nt, TS, TD), jnp.bfloat16),
            jax.ShapeDtypeStruct((columns, dest_total), jnp.bfloat16),
        ],
        compiler_params=pltpu.CompilerParams(dimension_semantics=("arbitrary", "arbitrary")),
        cost_estimate=pl.CostEstimate(
            flops=2 * columns * work + 4 * nb * work,
            bytes_accessed=2 * work + 2 * columns * source_total,
            transcendentals=0,
        ),
    )(tiles_flat, embedding, rows4, mask4)


def spread_kernel(agg_scale, k_total, nt, tiles_ref, counts_ref, back_ref, tg_in_ref, tg_ref):
    t = pl.program_id(0)
    k = pl.program_id(1)

    @pl.when((t == 0) & (k == 0))
    def _():
        tg_ref[...] = tg_in_ref[...]

    tile = tiles_ref[k * nt + t]
    start = pl.multiple_of(tile * TS, TS)
    part = jnp.dot(counts_ref[0, 0], back_ref[...], preferred_element_type=jnp.float32)
    tg_ref[pl.ds(start, TS), :] += part * agg_scale


def spread(counts, back, tiles_flat, table_grad, agg_scale):
    k_total, nt = counts.shape[:2]
    source_total, columns = table_grad.shape
    grid_spec = pltpu.PrefetchScalarGridSpec(
        num_scalar_prefetch=1,
        grid=(nt, k_total),
        in_specs=[
            pl.BlockSpec((1, 1, TS, TD), lambda t, k, tiles: (k, t, 0, 0)),
            pl.BlockSpec((TD, columns), lambda t, k, tiles: (t, 0)),
            pl.BlockSpec((source_total, columns), lambda t, k, tiles: (0, 0)),
        ],
        out_specs=pl.BlockSpec((source_total, columns), lambda t, k, tiles: (0, 0)),
    )
    work = k_total * nt * TD * TS
    return pl.pallas_call(
        functools.partial(spread_kernel, agg_scale, k_total, nt),
        grid_spec=grid_spec,
        out_shape=jax.ShapeDtypeStruct((source_total, columns), jnp.float32),
        input_output_aliases={3: 0},
        compiler_params=pltpu.CompilerParams(
            dimension_semantics=("arbitrary", "arbitrary"),
            vmem_limit_bytes=48 * 1024 * 1024,
        ),
        cost_estimate=pl.CostEstimate(
            flops=2 * columns * work,
            bytes_accessed=2 * work + 8 * source_total * columns,
            transcendentals=0,
        ),
    )(tiles_flat, counts, back, table_grad)


def local(
    embedding,
    self_weight,
    neighbor_weight,
    up_weight,
    down_weight,
    source_tiles,
    neighbor_rows,
    slot_mask,
    dest_rows,
    owner_order,
    output_grad,
):
    batch_total = lax.axis_size("batch")
    columns, source_total = embedding.shape
    micro_total = source_tiles.shape[0]
    dest_total = dest_rows.shape[1]
    agg_scale = 1.0 / math.sqrt(K * NB)
    norm_factor = 1.0 / math.sqrt(micro_total * dest_total * batch_total)
    tiles_all = source_tiles.reshape(micro_total, -1)

    target_all = gathered_over(output_grad, "feat", 1)
    table = embedding.T
    counts_all, own_all, hidden_all = [], [], []
    for m in range(micro_total):
        counts, agg_t = aggregate(embedding, tiles_all[m], neighbor_rows[m], slot_mask[m], agg_scale)
        own = table[dest_rows[m]]
        partial = jnp.dot(own, self_weight, preferred_element_type=jnp.float32) + lax.dot_general(
            agg_t, neighbor_weight, (((0,), (0,)), ((), ())), preferred_element_type=jnp.float32
        )
        counts_all.append((counts, agg_t))
        own_all.append(own)
        hidden_all.append(summed_over(partial, "feat"))

    up_sum = jnp.zeros(up_weight.shape, jnp.float32)
    down_sum = jnp.zeros(down_weight.shape, jnp.float32)
    self_sum = jnp.zeros((columns, H), jnp.float32)
    neighbor_sum = jnp.zeros((columns, H), jnp.float32)
    backs = []
    own_grads = []
    for m in range(micro_total):
        agg_t = counts_all[m][1]
        row_order = owner_order[m, 0]
        target = jnp.zeros(target_all.shape[1:], target_all.dtype).at[row_order].set(target_all[m])
        hidden_grad, up_part, down_part = mlp_pass(hidden_all[m], target, up_weight, down_weight)
        up_sum = up_sum + up_part
        down_sum = down_sum + down_part
        self_sum = self_sum + jnp.dot(own_all[m].T, hidden_grad, preferred_element_type=jnp.float32)
        neighbor_sum = neighbor_sum + jnp.dot(agg_t, hidden_grad, preferred_element_type=jnp.float32)
        backs.append(
            jnp.dot(hidden_grad, neighbor_weight.T, preferred_element_type=jnp.float32).astype(jnp.bfloat16)
        )
        own_grads.append(jnp.dot(hidden_grad, self_weight.T, preferred_element_type=jnp.float32))

    sizes = [up_sum.size, down_sum.size, self_sum.size, neighbor_sum.size]
    line = jnp.concatenate([up_sum.ravel(), down_sum.ravel(), self_sum.ravel(), neighbor_sum.ravel()])
    line = summed_over(line, "batch")
    ends = [0]
    for s in sizes:
        ends.append(ends[-1] + s)
    up_sum = line[ends[0] : ends[1]].reshape(up_weight.shape)
    down_sum = line[ends[1] : ends[2]].reshape(down_weight.shape)
    self_sum = line[ends[2] : ends[3]].reshape(columns, H)
    neighbor_sum = line[ends[3] : ends[4]].reshape(columns, H)

    table_grad = jnp.zeros((source_total, columns), jnp.float32)
    for m in range(micro_total):
        table_grad = table_grad.at[dest_rows[m]].add(own_grads[m])
    for m in range(micro_total):
        table_grad = spread(counts_all[m][0], backs[m], tiles_all[m], table_grad, agg_scale)
    return (
        table_grad.T,
        self_sum * norm_factor,
        neighbor_sum * norm_factor,
        up_sum * norm_factor,
        down_sum * norm_factor,
    )


def solution(mesh):
    in_specs = (
        P("feat", "batch"),
        P("feat", None),
        P("feat", None),
        P(),
        P(),
        P(None, None, "batch"),
        P(None, None, None, "batch"),
        P(None, None, "batch"),
        P(None, "batch"),
        P(None, "batch", None),
        P(None, ("batch", "feat"), None),
    )
    out_specs = (P("feat", "batch"), P("feat", None), P("feat", None), P(), P())
    return jax.shard_map(local, mesh=mesh, in_specs=in_specs, out_specs=out_specs, check_vma=False)
```

```python
import functools
import math

import jax
import jax.numpy as jnp
from jax import lax
from jax.experimental import pallas as pl
from jax.experimental.pallas import tpu as pltpu
from jax.sharding import PartitionSpec as P

H = 128
TD = 256
TS = 1024
K = 8
NB = 16
CS = 256


def gelu_slope(values):
    result, pullback = jax.vjp(jax.nn.gelu, values)
    return (result, pullback(jnp.ones_like(values))[0])


def mlp_pass(hidden, target, up_weight, down_weight):
    first_value, first_slope = gelu_slope(hidden)
    first_act = first_value.astype(jnp.bfloat16)
    inner_pre = jnp.dot(first_act, up_weight, preferred_element_type=jnp.float32)
    inner_value, inner_slope = gelu_slope(inner_pre)
    inner_act = inner_value.astype(jnp.bfloat16)
    down_part = jnp.dot(inner_act.T, target, preferred_element_type=jnp.float32)
    inner_grad = (
        jnp.dot(target, down_weight.T, preferred_element_type=jnp.float32) * inner_slope
    ).astype(jnp.bfloat16)
    up_part = jnp.dot(first_act.T, inner_grad, preferred_element_type=jnp.float32)
    hidden_grad = (
        jnp.dot(inner_grad, up_weight.T, preferred_element_type=jnp.float32) * first_slope
    ).astype(jnp.bfloat16)
    return (hidden_grad, up_part, down_part)


def summed_over(x, axis):
    n = lax.axis_size(axis)
    flat = x.reshape(n, -1)
    mine = lax.all_to_all(flat, axis, 0, 0, tiled=True).reshape(n, -1).sum(axis=0)
    spread_back = lax.all_to_all(jnp.broadcast_to(mine[None], (n, mine.size)), axis, 0, 0, tiled=True)
    return spread_back.reshape(x.shape)


def gathered_over(x, axis, dim):
    n = lax.axis_size(axis)
    pieces = lax.all_to_all(jnp.broadcast_to(x[None], (n, *x.shape)), axis, 0, 0, tiled=True)
    pieces = jnp.moveaxis(pieces, 0, dim)
    shape = pieces.shape
    return pieces.reshape(*shape[:dim], shape[dim] * shape[dim + 1], *shape[dim + 2 :])


def agg_kernel(agg_scale, k_total, nt, tiles_ref, emb_ref, rows_ref, mask_ref, counts_ref, agg_ref, acc_ref):
    k = pl.program_id(1)

    @pl.when(k == 0)
    def _():
        acc_ref[...] = jnp.zeros_like(acc_ref)

    msk = mask_ref[0, 0].astype(jnp.bfloat16)
    rows = rows_ref[0, 0]
    local_iota = lax.broadcasted_iota(jnp.int32, (CS, TD), 0).astype(jnp.bfloat16)
    one = jnp.ones((CS, TD), jnp.bfloat16)
    zero = jnp.zeros((CS, TD), jnp.bfloat16)

    def chunk(c, carry):
        start = pl.multiple_of(c * CS, CS)
        local = (rows - start).astype(jnp.float32)
        cnt = zero
        for j in range(NB):
            here = local[j : j + 1, :].astype(jnp.bfloat16)
            cnt = cnt + jnp.where(here == local_iota, one, zero)
        cnt = cnt * msk
        counts_ref[0, 0, pl.ds(start, CS), :] = cnt
        acc_ref[...] += jnp.dot(emb_ref[:, pl.ds(start, CS)], cnt, preferred_element_type=jnp.float32)
        return carry

    lax.fori_loop(0, TS // CS, chunk, 0)

    @pl.when(k == k_total - 1)
    def _():
        agg_ref[...] = (acc_ref[...] * agg_scale).astype(jnp.bfloat16)


def aggregate(embedding, tiles_flat, neighbor_rows, slot_mask, agg_scale):
    columns, source_total = embedding.shape
    k_total, nb, dest_total = neighbor_rows.shape
    nt = dest_total // TD
    mask4 = slot_mask.reshape(k_total, 1, 1, dest_total)
    rows4 = neighbor_rows.reshape(k_total, 1, nb, dest_total)
    grid_spec = pltpu.PrefetchScalarGridSpec(
        num_scalar_prefetch=1,
        grid=(nt, k_total),
        in_specs=[
            pl.BlockSpec((columns, TS), lambda t, k, tiles: (0, tiles[k * nt + t])),
            pl.BlockSpec((1, 1, nb, TD), lambda t, k, tiles: (k, 0, 0, t)),
            pl.BlockSpec((1, 1, 1, TD), lambda t, k, tiles: (k, 0, 0, t)),
        ],
        out_specs=[
            pl.BlockSpec((1, 1, TS, TD), lambda t, k, tiles: (k, t, 0, 0)),
            pl.BlockSpec((columns, TD), lambda t, k, tiles: (0, t)),
        ],
        scratch_shapes=[pltpu.VMEM((columns, TD), jnp.float32)],
    )
    work = k_total * dest_total * TS
    return pl.pallas_call(
        functools.partial(agg_kernel, agg_scale, k_total, nt),
        grid_spec=grid_spec,
        out_shape=[
            jax.ShapeDtypeStruct((k_total, nt, TS, TD), jnp.bfloat16),
            jax.ShapeDtypeStruct((columns, dest_total), jnp.bfloat16),
        ],
        compiler_params=pltpu.CompilerParams(dimension_semantics=("arbitrary", "arbitrary")),
        cost_estimate=pl.CostEstimate(
            flops=2 * columns * work + 4 * nb * work,
            bytes_accessed=2 * work + 2 * columns * source_total,
            transcendentals=0,
        ),
    )(tiles_flat, embedding, rows4, mask4)


def spread_kernel(agg_scale, k_total, nt, tiles_ref, counts_ref, back_ref, tg_in_ref, tg_ref):
    t = pl.program_id(0)
    k = pl.program_id(1)

    @pl.when((t == 0) & (k == 0))
    def _():
        tg_ref[...] = tg_in_ref[...]

    tile = tiles_ref[k * nt + t]
    start = pl.multiple_of(tile * TS, TS)
    part = jnp.dot(counts_ref[0, 0], back_ref[...], preferred_element_type=jnp.float32)
    tg_ref[pl.ds(start, TS), :] += part * agg_scale


def spread(counts, back, tiles_flat, table_grad, agg_scale):
    k_total, nt = counts.shape[:2]
    source_total, columns = table_grad.shape
    grid_spec = pltpu.PrefetchScalarGridSpec(
        num_scalar_prefetch=1,
        grid=(nt, k_total),
        in_specs=[
            pl.BlockSpec((1, 1, TS, TD), lambda t, k, tiles: (k, t, 0, 0)),
            pl.BlockSpec((TD, columns), lambda t, k, tiles: (t, 0)),
            pl.BlockSpec((source_total, columns), lambda t, k, tiles: (0, 0)),
        ],
        out_specs=pl.BlockSpec((source_total, columns), lambda t, k, tiles: (0, 0)),
    )
    work = k_total * nt * TD * TS
    return pl.pallas_call(
        functools.partial(spread_kernel, agg_scale, k_total, nt),
        grid_spec=grid_spec,
        out_shape=jax.ShapeDtypeStruct((source_total, columns), jnp.float32),
        input_output_aliases={3: 0},
        compiler_params=pltpu.CompilerParams(
            dimension_semantics=("arbitrary", "arbitrary"),
            vmem_limit_bytes=48 * 1024 * 1024,
        ),
        cost_estimate=pl.CostEstimate(
            flops=2 * columns * work,
            bytes_accessed=2 * work + 8 * source_total * columns,
            transcendentals=0,
        ),
    )(tiles_flat, counts, back, table_grad)


def local(
    embedding,
    self_weight,
    neighbor_weight,
    up_weight,
    down_weight,
    source_tiles,
    neighbor_rows,
    slot_mask,
    dest_rows,
    owner_order,
    output_grad,
):
    batch_total = lax.axis_size("batch")
    columns, source_total = embedding.shape
    micro_total = source_tiles.shape[0]
    dest_total = dest_rows.shape[1]
    agg_scale = 1.0 / math.sqrt(K * NB)
    norm_factor = 1.0 / math.sqrt(micro_total * dest_total * batch_total)
    tiles_all = source_tiles.reshape(micro_total, -1)

    target_all = gathered_over(output_grad, "feat", 1)
    table = embedding.T
    counts_all, own_all, hidden_all = [], [], []
    for m in range(micro_total):
        counts, agg_t = aggregate(embedding, tiles_all[m], neighbor_rows[m], slot_mask[m], agg_scale)
        own = table[dest_rows[m]]
        partial = jnp.dot(own, self_weight, preferred_element_type=jnp.float32) + lax.dot_general(
            agg_t, neighbor_weight, (((0,), (0,)), ((), ())), preferred_element_type=jnp.float32
        )
        counts_all.append((counts, agg_t))
        own_all.append(own)
        hidden_all.append(summed_over(partial, "feat"))

    up_sum = jnp.zeros(up_weight.shape, jnp.float32)
    down_sum = jnp.zeros(down_weight.shape, jnp.float32)
    self_sum = jnp.zeros((columns, H), jnp.float32)
    neighbor_sum = jnp.zeros((columns, H), jnp.float32)
    table_grad = jnp.zeros((source_total, columns), jnp.float32)
    pending = []
    for m in range(micro_total):
        hidden = hidden_all[m]
        if m > 0:
            hidden, table_grad = lax.optimization_barrier((hidden, table_grad))
        agg_t = counts_all[m][1]
        row_order = owner_order[m, 0]
        target = jnp.zeros(target_all.shape[1:], target_all.dtype).at[row_order].set(target_all[m])
        hidden_grad, up_part, down_part = mlp_pass(hidden, target, up_weight, down_weight)
        up_sum = up_sum + up_part
        down_sum = down_sum + down_part
        self_sum = self_sum + jnp.dot(own_all[m].T, hidden_grad, preferred_element_type=jnp.float32)
        neighbor_sum = neighbor_sum + jnp.dot(agg_t, hidden_grad, preferred_element_type=jnp.float32)
        back = jnp.dot(hidden_grad, neighbor_weight.T, preferred_element_type=jnp.float32).astype(jnp.bfloat16)
        own_grad = jnp.dot(hidden_grad, self_weight.T, preferred_element_type=jnp.float32)
        if m + 1 < micro_total:
            table_grad = spread(counts_all[m][0], back, tiles_all[m], table_grad, agg_scale)
            table_grad = table_grad.at[dest_rows[m]].add(own_grad)
        else:
            pending.append((m, back, own_grad))

    sizes = [up_sum.size, down_sum.size, self_sum.size, neighbor_sum.size]
    line = jnp.concatenate([up_sum.ravel(), down_sum.ravel(), self_sum.ravel(), neighbor_sum.ravel()])
    line = summed_over(line, "batch")
    ends = [0]
    for s in sizes:
        ends.append(ends[-1] + s)
    up_sum = line[ends[0] : ends[1]].reshape(up_weight.shape)
    down_sum = line[ends[1] : ends[2]].reshape(down_weight.shape)
    self_sum = line[ends[2] : ends[3]].reshape(columns, H)
    neighbor_sum = line[ends[3] : ends[4]].reshape(columns, H)

    for m, back, own_grad in pending:
        table_grad = spread(counts_all[m][0], back, tiles_all[m], table_grad, agg_scale)
        table_grad = table_grad.at[dest_rows[m]].add(own_grad)
    return (
        table_grad.T,
        self_sum * norm_factor,
        neighbor_sum * norm_factor,
        up_sum * norm_factor,
        down_sum * norm_factor,
    )


def solution(mesh):
    in_specs = (
        P("feat", "batch"),
        P("feat", None),
        P("feat", None),
        P(),
        P(),
        P(None, None, "batch"),
        P(None, None, None, "batch"),
        P(None, None, "batch"),
        P(None, "batch"),
        P(None, "batch", None),
        P(None, ("batch", "feat"), None),
    )
    out_specs = (P("feat", "batch"), P("feat", None), P("feat", None), P(), P())
    return jax.shard_map(local, mesh=mesh, in_specs=in_specs, out_specs=out_specs, check_vma=False)
```

```python
import functools
import math

import jax
import jax.numpy as jnp
from jax import lax
from jax.experimental import pallas as pl
from jax.experimental.pallas import tpu as pltpu
from jax.sharding import PartitionSpec as P

H = 128
TD = 256
TS = 1024
K = 8
NB = 16
CS = 128


def gelu_slope(values):
    result, pullback = jax.vjp(jax.nn.gelu, values)
    return (result, pullback(jnp.ones_like(values))[0])


def mlp_pass(hidden, target, up_weight, down_weight):
    first_value, first_slope = gelu_slope(hidden)
    first_act = first_value.astype(jnp.bfloat16)
    inner_pre = jnp.dot(first_act, up_weight, preferred_element_type=jnp.float32)
    inner_value, inner_slope = gelu_slope(inner_pre)
    inner_act = inner_value.astype(jnp.bfloat16)
    down_part = jnp.dot(inner_act.T, target, preferred_element_type=jnp.float32)
    inner_grad = (
        jnp.dot(target, down_weight.T, preferred_element_type=jnp.float32) * inner_slope
    ).astype(jnp.bfloat16)
    up_part = jnp.dot(first_act.T, inner_grad, preferred_element_type=jnp.float32)
    hidden_grad = (
        jnp.dot(inner_grad, up_weight.T, preferred_element_type=jnp.float32) * first_slope
    ).astype(jnp.bfloat16)
    return (hidden_grad, up_part, down_part)


def summed_over(x, axis):
    n = lax.axis_size(axis)
    flat = x.reshape(n, -1)
    mine = lax.all_to_all(flat, axis, 0, 0, tiled=True).reshape(n, -1).sum(axis=0)
    spread_back = lax.all_to_all(jnp.broadcast_to(mine[None], (n, mine.size)), axis, 0, 0, tiled=True)
    return spread_back.reshape(x.shape)


def gathered_over(x, axis, dim):
    n = lax.axis_size(axis)
    pieces = lax.all_to_all(jnp.broadcast_to(x[None], (n, *x.shape)), axis, 0, 0, tiled=True)
    pieces = jnp.moveaxis(pieces, 0, dim)
    shape = pieces.shape
    return pieces.reshape(*shape[:dim], shape[dim] * shape[dim + 1], *shape[dim + 2 :])


def agg_kernel(agg_scale, k_total, nt, tiles_ref, emb_ref, rows_ref, mask_ref, counts_ref, agg_ref, acc_ref):
    k = pl.program_id(1)

    @pl.when(k == 0)
    def _():
        acc_ref[...] = jnp.zeros_like(acc_ref)

    msk = mask_ref[0, 0].astype(jnp.bfloat16)
    rows = rows_ref[0, 0]
    local_iota = lax.broadcasted_iota(jnp.int32, (CS, TD), 0).astype(jnp.bfloat16)
    one = jnp.ones((CS, TD), jnp.bfloat16)
    zero = jnp.zeros((CS, TD), jnp.bfloat16)

    def chunk(c, carry):
        start = pl.multiple_of(c * CS, CS)
        local = (rows - start).astype(jnp.float32)
        cnt = zero
        for j in range(NB):
            here = local[j : j + 1, :].astype(jnp.bfloat16)
            cnt = cnt + jnp.where(here == local_iota, one, zero)
        counts_ref[0, 0, pl.ds(start, CS), :] = cnt * msk
        return carry

    lax.fori_loop(0, TS // CS, chunk, 0)
    acc_ref[...] += jnp.dot(emb_ref[...], counts_ref[0, 0], preferred_element_type=jnp.float32)

    @pl.when(k == k_total - 1)
    def _():
        agg_ref[...] = (acc_ref[...] * agg_scale).astype(jnp.bfloat16)


def aggregate(embedding, tiles_flat, neighbor_rows, slot_mask, agg_scale, t0, t_count):
    columns, source_total = embedding.shape
    k_total, nb, dest_total = neighbor_rows.shape
    nt = dest_total // TD
    mask4 = slot_mask.reshape(k_total, 1, 1, dest_total)
    rows4 = neighbor_rows.reshape(k_total, 1, nb, dest_total)
    grid_spec = pltpu.PrefetchScalarGridSpec(
        num_scalar_prefetch=1,
        grid=(t_count, k_total),
        in_specs=[
            pl.BlockSpec((columns, TS), lambda t, k, tiles: (0, tiles[k * nt + t0 + t])),
            pl.BlockSpec((1, 1, nb, TD), lambda t, k, tiles: (k, 0, 0, t0 + t)),
            pl.BlockSpec((1, 1, 1, TD), lambda t, k, tiles: (k, 0, 0, t0 + t)),
        ],
        out_specs=[
            pl.BlockSpec((1, 1, TS, TD), lambda t, k, tiles: (k, t, 0, 0)),
            pl.BlockSpec((columns, TD), lambda t, k, tiles: (0, t)),
        ],
        scratch_shapes=[pltpu.VMEM((columns, TD), jnp.float32)],
    )
    work = k_total * t_count * TD * TS
    return pl.pallas_call(
        functools.partial(agg_kernel, agg_scale, k_total, nt),
        grid_spec=grid_spec,
        out_shape=[
            jax.ShapeDtypeStruct((k_total, t_count, TS, TD), jnp.bfloat16),
            jax.ShapeDtypeStruct((columns, t_count * TD), jnp.bfloat16),
        ],
        compiler_params=pltpu.CompilerParams(dimension_semantics=("arbitrary", "arbitrary")),
        cost_estimate=pl.CostEstimate(
            flops=2 * columns * work + 4 * nb * work,
            bytes_accessed=2 * work + 2 * columns * source_total,
            transcendentals=0,
        ),
    )(tiles_flat, embedding, rows4, mask4)


def spread_kernel(agg_scale, k_total, nt, t0, tiles_ref, counts_ref, back_ref, tg_in_ref, tg_ref):
    t = pl.program_id(0)
    k = pl.program_id(1)

    @pl.when((t == 0) & (k == 0))
    def _():
        tg_ref[...] = tg_in_ref[...]

    tile = tiles_ref[k * nt + t0 + t]
    start = pl.multiple_of(tile * TS, TS)
    part = jnp.dot(counts_ref[0, 0], back_ref[...], preferred_element_type=jnp.float32)
    tg_ref[pl.ds(start, TS), :] += part * agg_scale


def spread(counts, back, tiles_flat, table_grad, agg_scale, t0, nt):
    k_total, t_count = counts.shape[:2]
    source_total, columns = table_grad.shape
    grid_spec = pltpu.PrefetchScalarGridSpec(
        num_scalar_prefetch=1,
        grid=(t_count, k_total),
        in_specs=[
            pl.BlockSpec((1, 1, TS, TD), lambda t, k, tiles: (k, t, 0, 0)),
            pl.BlockSpec((TD, columns), lambda t, k, tiles: (t, 0)),
            pl.BlockSpec((source_total, columns), lambda t, k, tiles: (0, 0)),
        ],
        out_specs=pl.BlockSpec((source_total, columns), lambda t, k, tiles: (0, 0)),
    )
    work = k_total * t_count * TD * TS
    return pl.pallas_call(
        functools.partial(spread_kernel, agg_scale, k_total, nt, t0),
        grid_spec=grid_spec,
        out_shape=jax.ShapeDtypeStruct((source_total, columns), jnp.float32),
        input_output_aliases={3: 0},
        compiler_params=pltpu.CompilerParams(
            dimension_semantics=("arbitrary", "arbitrary"),
            vmem_limit_bytes=48 * 1024 * 1024,
        ),
        cost_estimate=pl.CostEstimate(
            flops=2 * columns * work,
            bytes_accessed=2 * work + 8 * source_total * columns,
            transcendentals=0,
        ),
    )(tiles_flat, counts, back, table_grad)


def local(
    embedding,
    self_weight,
    neighbor_weight,
    up_weight,
    down_weight,
    source_tiles,
    neighbor_rows,
    slot_mask,
    dest_rows,
    owner_order,
    output_grad,
):
    batch_total = lax.axis_size("batch")
    columns, source_total = embedding.shape
    micro_total = source_tiles.shape[0]
    dest_total = dest_rows.shape[1]
    agg_scale = 1.0 / math.sqrt(K * NB)
    norm_factor = 1.0 / math.sqrt(micro_total * dest_total * batch_total)
    tiles_all = source_tiles.reshape(micro_total, -1)
    nt = dest_total // TD
    halves = 2
    tc = nt // halves
    rows_c = tc * TD

    target_all = gathered_over(output_grad, "feat", 1)
    table = embedding.T
    chunks = []
    for m in range(micro_total):
        for h in range(halves):
            t0 = h * tc
            counts, agg_t = aggregate(
                embedding, tiles_all[m], neighbor_rows[m], slot_mask[m], agg_scale, t0, tc
            )
            dest_c = dest_rows[m, h * rows_c : (h + 1) * rows_c]
            own = table[dest_c]
            partial = jnp.dot(own, self_weight, preferred_element_type=jnp.float32) + lax.dot_general(
                agg_t, neighbor_weight, (((0,), (0,)), ((), ())), preferred_element_type=jnp.float32
            )
            chunks.append((m, h, t0, counts, agg_t, own, dest_c, summed_over(partial, "feat")))

    targets = []
    for m in range(micro_total):
        row_order = owner_order[m, 0]
        targets.append(jnp.zeros(target_all.shape[1:], target_all.dtype).at[row_order].set(target_all[m]))

    up_sum = jnp.zeros(up_weight.shape, jnp.float32)
    down_sum = jnp.zeros(down_weight.shape, jnp.float32)
    self_sum = jnp.zeros((columns, H), jnp.float32)
    neighbor_sum = jnp.zeros((columns, H), jnp.float32)
    table_grad = jnp.zeros((source_total, columns), jnp.float32)
    pending = []
    for i, (m, h, t0, counts, agg_t, own, dest_c, hidden) in enumerate(chunks):
        if i > 0:
            hidden, table_grad = lax.optimization_barrier((hidden, table_grad))
        target = targets[m][h * rows_c : (h + 1) * rows_c]
        hidden_grad, up_part, down_part = mlp_pass(hidden, target, up_weight, down_weight)
        up_sum = up_sum + up_part
        down_sum = down_sum + down_part
        self_sum = self_sum + jnp.dot(own.T, hidden_grad, preferred_element_type=jnp.float32)
        neighbor_sum = neighbor_sum + jnp.dot(agg_t, hidden_grad, preferred_element_type=jnp.float32)
        back = jnp.dot(hidden_grad, neighbor_weight.T, preferred_element_type=jnp.float32).astype(jnp.bfloat16)
        own_grad = jnp.dot(hidden_grad, self_weight.T, preferred_element_type=jnp.float32)
        if i + 1 < len(chunks):
            table_grad = spread(counts, back, tiles_all[m], table_grad, agg_scale, t0, nt)
            table_grad = table_grad.at[dest_c].add(own_grad)
        else:
            pending.append((counts, back, tiles_all[m], t0, dest_c, own_grad))

    sizes = [up_sum.size, down_sum.size, self_sum.size, neighbor_sum.size]
    line = jnp.concatenate([up_sum.ravel(), down_sum.ravel(), self_sum.ravel(), neighbor_sum.ravel()])
    line = summed_over(line, "batch")
    ends = [0]
    for s in sizes:
        ends.append(ends[-1] + s)
    up_sum = line[ends[0] : ends[1]].reshape(up_weight.shape)
    down_sum = line[ends[1] : ends[2]].reshape(down_weight.shape)
    self_sum = line[ends[2] : ends[3]].reshape(columns, H)
    neighbor_sum = line[ends[3] : ends[4]].reshape(columns, H)

    for counts, back, tiles, t0, dest_c, own_grad in pending:
        table_grad = spread(counts, back, tiles, table_grad, agg_scale, t0, nt)
        table_grad = table_grad.at[dest_c].add(own_grad)
    return (
        table_grad.T,
        self_sum * norm_factor,
        neighbor_sum * norm_factor,
        up_sum * norm_factor,
        down_sum * norm_factor,
    )


def solution(mesh):
    in_specs = (
        P("feat", "batch"),
        P("feat", None),
        P("feat", None),
        P(),
        P(),
        P(None, None, "batch"),
        P(None, None, None, "batch"),
        P(None, None, "batch"),
        P(None, "batch"),
        P(None, "batch", None),
        P(None, ("batch", "feat"), None),
    )
    out_specs = (P("feat", "batch"), P("feat", None), P("feat", None), P(), P())
    return jax.shard_map(local, mesh=mesh, in_specs=in_specs, out_specs=out_specs, check_vma=False)
```

```python
import functools
import math

import jax
import jax.numpy as jnp
from jax import lax
from jax.experimental import pallas as pl
from jax.experimental.pallas import tpu as pltpu
from jax.sharding import PartitionSpec as P

H = 128
TD = 256
TS = 1024
K = 8
NB = 16
CS = 128


def gelu_slope(values):
    result, pullback = jax.vjp(jax.nn.gelu, values)
    return (result, pullback(jnp.ones_like(values))[0])


def mlp_pass(hidden, target, up_weight, down_weight):
    first_value, first_slope = gelu_slope(hidden)
    first_act = first_value.astype(jnp.bfloat16)
    inner_pre = jnp.dot(first_act, up_weight, preferred_element_type=jnp.float32)
    inner_value, inner_slope = gelu_slope(inner_pre)
    inner_act = inner_value.astype(jnp.bfloat16)
    down_part = jnp.dot(inner_act.T, target, preferred_element_type=jnp.float32)
    inner_grad = (
        jnp.dot(target, down_weight.T, preferred_element_type=jnp.float32) * inner_slope
    ).astype(jnp.bfloat16)
    up_part = jnp.dot(first_act.T, inner_grad, preferred_element_type=jnp.float32)
    hidden_grad = (
        jnp.dot(inner_grad, up_weight.T, preferred_element_type=jnp.float32) * first_slope
    ).astype(jnp.bfloat16)
    return (hidden_grad, up_part, down_part)


def summed_over(x, axis):
    n = lax.axis_size(axis)
    flat = x.reshape(n, -1)
    mine = lax.all_to_all(flat, axis, 0, 0, tiled=True).reshape(n, -1).sum(axis=0)
    spread_back = lax.all_to_all(jnp.broadcast_to(mine[None], (n, mine.size)), axis, 0, 0, tiled=True)
    return spread_back.reshape(x.shape)


def gathered_over(x, axis, dim):
    n = lax.axis_size(axis)
    pieces = lax.all_to_all(jnp.broadcast_to(x[None], (n, *x.shape)), axis, 0, 0, tiled=True)
    pieces = jnp.moveaxis(pieces, 0, dim)
    shape = pieces.shape
    return pieces.reshape(*shape[:dim], shape[dim] * shape[dim + 1], *shape[dim + 2 :])


def agg_kernel(agg_scale, k_total, nt, tiles_ref, emb_ref, rows_ref, mask_ref, counts_ref, agg_ref, acc_ref):
    k = pl.program_id(1)

    @pl.when(k == 0)
    def _():
        acc_ref[...] = jnp.zeros_like(acc_ref)

    msk = mask_ref[0, 0].astype(jnp.bfloat16)
    rows = rows_ref[0, 0]
    local_iota = lax.broadcasted_iota(jnp.int32, (CS, TD), 0).astype(jnp.bfloat16)
    one = jnp.ones((CS, TD), jnp.bfloat16)
    zero = jnp.zeros((CS, TD), jnp.bfloat16)

    def chunk(c, carry):
        start = pl.multiple_of(c * CS, CS)
        local = (rows - start).astype(jnp.float32)
        cnt = zero
        for j in range(NB):
            here = local[j : j + 1, :].astype(jnp.bfloat16)
            cnt = cnt + jnp.where(here == local_iota, one, zero)
        counts_ref[0, 0, pl.ds(start, CS), :] = cnt * msk
        return carry

    lax.fori_loop(0, TS // CS, chunk, 0)
    acc_ref[...] += jnp.dot(emb_ref[...], counts_ref[0, 0], preferred_element_type=jnp.float32)

    @pl.when(k == k_total - 1)
    def _():
        agg_ref[...] = (acc_ref[...] * agg_scale).astype(jnp.bfloat16)


def aggregate(embedding, tiles_flat, neighbor_rows, slot_mask, agg_scale):
    columns, source_total = embedding.shape
    k_total, nb, dest_total = neighbor_rows.shape
    nt = dest_total // TD
    mask4 = slot_mask.reshape(k_total, 1, 1, dest_total)
    rows4 = neighbor_rows.reshape(k_total, 1, nb, dest_total)
    grid_spec = pltpu.PrefetchScalarGridSpec(
        num_scalar_prefetch=1,
        grid=(nt, k_total),
        in_specs=[
            pl.BlockSpec((columns, TS), lambda t, k, tiles: (0, tiles[k * nt + t])),
            pl.BlockSpec((1, 1, nb, TD), lambda t, k, tiles: (k, 0, 0, t)),
            pl.BlockSpec((1, 1, 1, TD), lambda t, k, tiles: (k, 0, 0, t)),
        ],
        out_specs=[
            pl.BlockSpec((1, 1, TS, TD), lambda t, k, tiles: (k, t, 0, 0)),
            pl.BlockSpec((columns, TD), lambda t, k, tiles: (0, t)),
        ],
        scratch_shapes=[pltpu.VMEM((columns, TD), jnp.float32)],
    )
    work = k_total * dest_total * TS
    return pl.pallas_call(
        functools.partial(agg_kernel, agg_scale, k_total, nt),
        grid_spec=grid_spec,
        out_shape=[
            jax.ShapeDtypeStruct((k_total, nt, TS, TD), jnp.bfloat16),
            jax.ShapeDtypeStruct((columns, dest_total), jnp.bfloat16),
        ],
        compiler_params=pltpu.CompilerParams(dimension_semantics=("arbitrary", "arbitrary")),
        cost_estimate=pl.CostEstimate(
            flops=2 * columns * work + 4 * nb * work,
            bytes_accessed=2 * work + 2 * columns * source_total,
            transcendentals=0,
        ),
    )(tiles_flat, embedding, rows4, mask4)


def spread_kernel(agg_scale, k_total, nt, tiles_ref, counts_ref, back_ref, tg_in_ref, tg_ref):
    t = pl.program_id(0)
    k = pl.program_id(1)

    @pl.when((t == 0) & (k == 0))
    def _():
        tg_ref[...] = tg_in_ref[...]

    tile = tiles_ref[k * nt + t]
    start = pl.multiple_of(tile * TS, TS)
    part = jnp.dot(counts_ref[0, 0], back_ref[...], preferred_element_type=jnp.float32)
    tg_ref[pl.ds(start, TS), :] += part * agg_scale


def spread(counts, back, tiles_flat, table_grad, agg_scale):
    k_total, nt = counts.shape[:2]
    source_total, columns = table_grad.shape
    grid_spec = pltpu.PrefetchScalarGridSpec(
        num_scalar_prefetch=1,
        grid=(nt, k_total),
        in_specs=[
            pl.BlockSpec((1, 1, TS, TD), lambda t, k, tiles: (k, t, 0, 0)),
            pl.BlockSpec((TD, columns), lambda t, k, tiles: (t, 0)),
            pl.BlockSpec((source_total, columns), lambda t, k, tiles: (0, 0)),
        ],
        out_specs=pl.BlockSpec((source_total, columns), lambda t, k, tiles: (0, 0)),
    )
    work = k_total * nt * TD * TS
    return pl.pallas_call(
        functools.partial(spread_kernel, agg_scale, k_total, nt),
        grid_spec=grid_spec,
        out_shape=jax.ShapeDtypeStruct((source_total, columns), jnp.float32),
        input_output_aliases={3: 0},
        compiler_params=pltpu.CompilerParams(
            dimension_semantics=("arbitrary", "arbitrary"),
            vmem_limit_bytes=48 * 1024 * 1024,
        ),
        cost_estimate=pl.CostEstimate(
            flops=2 * columns * work,
            bytes_accessed=2 * work + 8 * source_total * columns,
            transcendentals=0,
        ),
    )(tiles_flat, counts, back, table_grad)


def local(
    embedding,
    self_weight,
    neighbor_weight,
    up_weight,
    down_weight,
    source_tiles,
    neighbor_rows,
    slot_mask,
    dest_rows,
    owner_order,
    output_grad,
):
    batch_total = lax.axis_size("batch")
    columns, source_total = embedding.shape
    micro_total = source_tiles.shape[0]
    dest_total = dest_rows.shape[1]
    agg_scale = 1.0 / math.sqrt(K * NB)
    norm_factor = 1.0 / math.sqrt(micro_total * dest_total * batch_total)
    tiles_all = source_tiles.reshape(micro_total, -1)

    target_all = gathered_over(output_grad, "feat", 1)
    table = embedding.T
    counts_all, own_all, hidden_all = [], [], []
    for m in range(micro_total):
        counts, agg_t = aggregate(embedding, tiles_all[m], neighbor_rows[m], slot_mask[m], agg_scale)
        own = table[dest_rows[m]]
        partial = jnp.dot(own, self_weight, preferred_element_type=jnp.float32) + lax.dot_general(
            agg_t, neighbor_weight, (((0,), (0,)), ((), ())), preferred_element_type=jnp.float32
        )
        counts_all.append((counts, agg_t))
        own_all.append(own)
        hidden_all.append(summed_over(partial, "feat"))

    up_sum = jnp.zeros(up_weight.shape, jnp.float32)
    down_sum = jnp.zeros(down_weight.shape, jnp.float32)
    self_sum = jnp.zeros((columns, H), jnp.float32)
    neighbor_sum = jnp.zeros((columns, H), jnp.float32)
    table_grad = jnp.zeros((source_total, columns), jnp.float32)
    pending = []
    for m in range(micro_total):
        hidden = hidden_all[m]
        if m > 0:
            hidden, table_grad = lax.optimization_barrier((hidden, table_grad))
        agg_t = counts_all[m][1]
        row_order = owner_order[m, 0]
        target = jnp.zeros(target_all.shape[1:], target_all.dtype).at[row_order].set(target_all[m])
        hidden_grad, up_part, down_part = mlp_pass(hidden, target, up_weight, down_weight)
        up_sum = up_sum + up_part
        down_sum = down_sum + down_part
        self_sum = self_sum + jnp.dot(own_all[m].T, hidden_grad, preferred_element_type=jnp.float32)
        neighbor_sum = neighbor_sum + jnp.dot(agg_t, hidden_grad, preferred_element_type=jnp.float32)
        back = jnp.dot(hidden_grad, neighbor_weight.T, preferred_element_type=jnp.float32).astype(jnp.bfloat16)
        own_grad = jnp.dot(hidden_grad, self_weight.T, preferred_element_type=jnp.float32)
        if m + 1 < micro_total:
            table_grad = spread(counts_all[m][0], back, tiles_all[m], table_grad, agg_scale)
            table_grad = table_grad.at[dest_rows[m]].add(own_grad)
        else:
            pending.append((m, back, own_grad))

    sizes = [up_sum.size, down_sum.size, self_sum.size, neighbor_sum.size]
    line = jnp.concatenate([up_sum.ravel(), down_sum.ravel(), self_sum.ravel(), neighbor_sum.ravel()])
    line = summed_over(line, "batch")
    ends = [0]
    for s in sizes:
        ends.append(ends[-1] + s)
    up_sum = line[ends[0] : ends[1]].reshape(up_weight.shape)
    down_sum = line[ends[1] : ends[2]].reshape(down_weight.shape)
    self_sum = line[ends[2] : ends[3]].reshape(columns, H)
    neighbor_sum = line[ends[3] : ends[4]].reshape(columns, H)

    for m, back, own_grad in pending:
        table_grad = spread(counts_all[m][0], back, tiles_all[m], table_grad, agg_scale)
        table_grad = table_grad.at[dest_rows[m]].add(own_grad)
    return (
        table_grad.T,
        self_sum * norm_factor,
        neighbor_sum * norm_factor,
        up_sum * norm_factor,
        down_sum * norm_factor,
    )


def solution(mesh):
    in_specs = (
        P("feat", "batch"),
        P("feat", None),
        P("feat", None),
        P(),
        P(),
        P(None, None, "batch"),
        P(None, None, None, "batch"),
        P(None, None, "batch"),
        P(None, "batch"),
        P(None, "batch", None),
        P(None, ("batch", "feat"), None),
    )
    out_specs = (P("feat", "batch"), P("feat", None), P("feat", None), P(), P())
    return jax.shard_map(local, mesh=mesh, in_specs=in_specs, out_specs=out_specs, check_vma=False)
```

```python
import functools
import math

import jax
import jax.numpy as jnp
from jax import lax
from jax.experimental import pallas as pl
from jax.experimental.pallas import tpu as pltpu
from jax.sharding import PartitionSpec as P

H = 128
TD = 256
TS = 1024
K = 8
NB = 16
CS = 128
MESH = pl.DeviceIdType.MESH


def gelu_slope(values):
    result, pullback = jax.vjp(jax.nn.gelu, values)
    return (result, pullback(jnp.ones_like(values))[0])


def mlp_pass(hidden, target, up_weight, down_weight):
    first_value, first_slope = gelu_slope(hidden)
    first_act = first_value.astype(jnp.bfloat16)
    inner_pre = jnp.dot(first_act, up_weight, preferred_element_type=jnp.float32)
    inner_value, inner_slope = gelu_slope(inner_pre)
    inner_act = inner_value.astype(jnp.bfloat16)
    down_part = jnp.dot(inner_act.T, target, preferred_element_type=jnp.float32)
    inner_grad = (
        jnp.dot(target, down_weight.T, preferred_element_type=jnp.float32) * inner_slope
    ).astype(jnp.bfloat16)
    up_part = jnp.dot(first_act.T, inner_grad, preferred_element_type=jnp.float32)
    hidden_grad = (
        jnp.dot(inner_grad, up_weight.T, preferred_element_type=jnp.float32) * first_slope
    ).astype(jnp.bfloat16)
    return (hidden_grad, up_part, down_part)


def summed_over(x, axis):
    n = lax.axis_size(axis)
    flat = x.reshape(n, -1)
    mine = lax.all_to_all(flat, axis, 0, 0, tiled=True).reshape(n, -1).sum(axis=0)
    spread_back = lax.all_to_all(jnp.broadcast_to(mine[None], (n, mine.size)), axis, 0, 0, tiled=True)
    return spread_back.reshape(x.shape)


def exchange_kernel(axis, n, x_ref, out_ref, recv_ref, send1, recv1, send2, recv2):
    me = lax.axis_index(axis)
    other = lax.axis_index("feat" if axis == "batch" else "batch")

    def dev(j):
        return (j, other) if axis == "batch" else (other, j)

    barrier = pltpu.get_barrier_semaphore()
    for d in range(1, n):
        pl.semaphore_signal(barrier, inc=1, device_id=dev(lax.rem(me + d, n)), device_id_type=MESH)
    pl.semaphore_wait(barrier, n - 1)

    def link(src, dst, send, recv, peer):
        return pltpu.make_async_remote_copy(
            src_ref=src, dst_ref=dst, send_sem=send, recv_sem=recv, device_id=dev(peer), device_id_type=MESH
        )

    for d in range(1, n):
        peer = lax.rem(me + d, n)
        link(x_ref.at[peer], recv_ref.at[me], send1.at[d], recv1.at[me], peer).start()
    for d in range(1, n):
        peer = lax.rem(me + d, n)
        src = lax.rem(me + n - d, n)
        link(x_ref.at[peer], recv_ref.at[me], send1.at[d], recv1.at[me], peer).wait_send()
        link(x_ref.at[src], recv_ref.at[src], send1.at[d], recv1.at[src], src).wait_recv()
    acc = x_ref[me]
    for d in range(1, n):
        acc = acc + recv_ref[lax.rem(me + n - d, n)]
    out_ref[me] = acc
    for d in range(1, n):
        peer = lax.rem(me + d, n)
        link(out_ref.at[me], out_ref.at[me], send2.at[d], recv2.at[me], peer).start()
    for d in range(1, n):
        peer = lax.rem(me + d, n)
        src = lax.rem(me + n - d, n)
        link(out_ref.at[me], out_ref.at[me], send2.at[d], recv2.at[me], peer).wait_send()
        link(out_ref.at[src], out_ref.at[src], send2.at[d], recv2.at[src], src).wait_recv()


def summed_by_kernel(x, axis, collective_id):
    n = lax.axis_size(axis)
    pieces = x.reshape(n, -1, 128)
    out = pl.pallas_call(
        functools.partial(exchange_kernel, axis, n),
        out_shape=jax.ShapeDtypeStruct(pieces.shape, pieces.dtype),
        in_specs=[pl.BlockSpec(memory_space=pltpu.VMEM)],
        out_specs=pl.BlockSpec(memory_space=pltpu.VMEM),
        scratch_shapes=[
            pltpu.VMEM(pieces.shape, pieces.dtype),
            pltpu.SemaphoreType.DMA((n,)),
            pltpu.SemaphoreType.DMA((n,)),
            pltpu.SemaphoreType.DMA((n,)),
            pltpu.SemaphoreType.DMA((n,)),
        ],
        compiler_params=pltpu.CompilerParams(collective_id=collective_id, has_side_effects=True),
    )(pieces)
    return out.reshape(x.shape)


def gathered_over(x, axis, dim):
    n = lax.axis_size(axis)
    pieces = lax.all_to_all(jnp.broadcast_to(x[None], (n, *x.shape)), axis, 0, 0, tiled=True)
    pieces = jnp.moveaxis(pieces, 0, dim)
    shape = pieces.shape
    return pieces.reshape(*shape[:dim], shape[dim] * shape[dim + 1], *shape[dim + 2 :])


def agg_kernel(agg_scale, k_total, nt, tiles_ref, emb_ref, rows_ref, mask_ref, counts_ref, agg_ref, acc_ref):
    k = pl.program_id(1)

    @pl.when(k == 0)
    def _():
        acc_ref[...] = jnp.zeros_like(acc_ref)

    msk = mask_ref[0, 0].astype(jnp.bfloat16)
    rows = rows_ref[0, 0]
    local_iota = lax.broadcasted_iota(jnp.int32, (CS, TD), 0).astype(jnp.bfloat16)
    one = jnp.ones((CS, TD), jnp.bfloat16)
    zero = jnp.zeros((CS, TD), jnp.bfloat16)

    def chunk(c, carry):
        start = pl.multiple_of(c * CS, CS)
        local = (rows - start).astype(jnp.float32)
        cnt = zero
        for j in range(NB):
            here = local[j : j + 1, :].astype(jnp.bfloat16)
            cnt = cnt + jnp.where(here == local_iota, one, zero)
        counts_ref[0, 0, pl.ds(start, CS), :] = cnt * msk
        return carry

    lax.fori_loop(0, TS // CS, chunk, 0)
    acc_ref[...] += jnp.dot(emb_ref[...], counts_ref[0, 0], preferred_element_type=jnp.float32)

    @pl.when(k == k_total - 1)
    def _():
        agg_ref[...] = (acc_ref[...] * agg_scale).astype(jnp.bfloat16)


def aggregate(embedding, tiles_flat, neighbor_rows, slot_mask, agg_scale):
    columns, source_total = embedding.shape
    k_total, nb, dest_total = neighbor_rows.shape
    nt = dest_total // TD
    mask4 = slot_mask.reshape(k_total, 1, 1, dest_total)
    rows4 = neighbor_rows.reshape(k_total, 1, nb, dest_total)
    grid_spec = pltpu.PrefetchScalarGridSpec(
        num_scalar_prefetch=1,
        grid=(nt, k_total),
        in_specs=[
            pl.BlockSpec((columns, TS), lambda t, k, tiles: (0, tiles[k * nt + t])),
            pl.BlockSpec((1, 1, nb, TD), lambda t, k, tiles: (k, 0, 0, t)),
            pl.BlockSpec((1, 1, 1, TD), lambda t, k, tiles: (k, 0, 0, t)),
        ],
        out_specs=[
            pl.BlockSpec((1, 1, TS, TD), lambda t, k, tiles: (k, t, 0, 0)),
            pl.BlockSpec((columns, TD), lambda t, k, tiles: (0, t)),
        ],
        scratch_shapes=[pltpu.VMEM((columns, TD), jnp.float32)],
    )
    work = k_total * dest_total * TS
    return pl.pallas_call(
        functools.partial(agg_kernel, agg_scale, k_total, nt),
        grid_spec=grid_spec,
        out_shape=[
            jax.ShapeDtypeStruct((k_total, nt, TS, TD), jnp.bfloat16),
            jax.ShapeDtypeStruct((columns, dest_total), jnp.bfloat16),
        ],
        compiler_params=pltpu.CompilerParams(dimension_semantics=("arbitrary", "arbitrary")),
        cost_estimate=pl.CostEstimate(
            flops=2 * columns * work + 4 * nb * work,
            bytes_accessed=2 * work + 2 * columns * source_total,
            transcendentals=0,
        ),
    )(tiles_flat, embedding, rows4, mask4)


def spread_kernel(agg_scale, k_total, nt, tiles_ref, counts_ref, back_ref, tg_in_ref, tg_ref):
    t = pl.program_id(0)
    k = pl.program_id(1)

    @pl.when((t == 0) & (k == 0))
    def _():
        tg_ref[...] = tg_in_ref[...]

    tile = tiles_ref[k * nt + t]
    start = pl.multiple_of(tile * TS, TS)
    part = jnp.dot(counts_ref[0, 0], back_ref[...], preferred_element_type=jnp.float32)
    tg_ref[pl.ds(start, TS), :] += part * agg_scale


def spread(counts, back, tiles_flat, table_grad, agg_scale):
    k_total, nt = counts.shape[:2]
    source_total, columns = table_grad.shape
    grid_spec = pltpu.PrefetchScalarGridSpec(
        num_scalar_prefetch=1,
        grid=(nt, k_total),
        in_specs=[
            pl.BlockSpec((1, 1, TS, TD), lambda t, k, tiles: (k, t, 0, 0)),
            pl.BlockSpec((TD, columns), lambda t, k, tiles: (t, 0)),
            pl.BlockSpec((source_total, columns), lambda t, k, tiles: (0, 0)),
        ],
        out_specs=pl.BlockSpec((source_total, columns), lambda t, k, tiles: (0, 0)),
    )
    work = k_total * nt * TD * TS
    return pl.pallas_call(
        functools.partial(spread_kernel, agg_scale, k_total, nt),
        grid_spec=grid_spec,
        out_shape=jax.ShapeDtypeStruct((source_total, columns), jnp.float32),
        input_output_aliases={3: 0},
        compiler_params=pltpu.CompilerParams(
            dimension_semantics=("arbitrary", "arbitrary"),
            vmem_limit_bytes=48 * 1024 * 1024,
        ),
        cost_estimate=pl.CostEstimate(
            flops=2 * columns * work,
            bytes_accessed=2 * work + 8 * source_total * columns,
            transcendentals=0,
        ),
    )(tiles_flat, counts, back, table_grad)


def local(
    embedding,
    self_weight,
    neighbor_weight,
    up_weight,
    down_weight,
    source_tiles,
    neighbor_rows,
    slot_mask,
    dest_rows,
    owner_order,
    output_grad,
):
    batch_total = lax.axis_size("batch")
    columns, source_total = embedding.shape
    micro_total = source_tiles.shape[0]
    dest_total = dest_rows.shape[1]
    agg_scale = 1.0 / math.sqrt(K * NB)
    norm_factor = 1.0 / math.sqrt(micro_total * dest_total * batch_total)
    tiles_all = source_tiles.reshape(micro_total, -1)

    target_all = gathered_over(output_grad, "feat", 1)
    table = embedding.T
    counts_all, own_all, hidden_all = [], [], []
    for m in range(micro_total):
        counts, agg_t = aggregate(embedding, tiles_all[m], neighbor_rows[m], slot_mask[m], agg_scale)
        own = table[dest_rows[m]]
        partial = jnp.dot(own, self_weight, preferred_element_type=jnp.float32) + lax.dot_general(
            agg_t, neighbor_weight, (((0,), (0,)), ((), ())), preferred_element_type=jnp.float32
        )
        counts_all.append((counts, agg_t))
        own_all.append(own)
        hidden_all.append(summed_over(partial, "feat"))

    up_sum = jnp.zeros(up_weight.shape, jnp.float32)
    down_sum = jnp.zeros(down_weight.shape, jnp.float32)
    self_sum = jnp.zeros((columns, H), jnp.float32)
    neighbor_sum = jnp.zeros((columns, H), jnp.float32)
    table_grad = jnp.zeros((source_total, columns), jnp.float32)
    pending = []
    for m in range(micro_total):
        hidden = hidden_all[m]
        if m > 0:
            hidden, table_grad = lax.optimization_barrier((hidden, table_grad))
        agg_t = counts_all[m][1]
        row_order = owner_order[m, 0]
        target = jnp.zeros(target_all.shape[1:], target_all.dtype).at[row_order].set(target_all[m])
        hidden_grad, up_part, down_part = mlp_pass(hidden, target, up_weight, down_weight)
        up_sum = up_sum + up_part
        down_sum = down_sum + down_part
        self_sum = self_sum + jnp.dot(own_all[m].T, hidden_grad, preferred_element_type=jnp.float32)
        neighbor_sum = neighbor_sum + jnp.dot(agg_t, hidden_grad, preferred_element_type=jnp.float32)
        back = jnp.dot(hidden_grad, neighbor_weight.T, preferred_element_type=jnp.float32).astype(jnp.bfloat16)
        own_grad = jnp.dot(hidden_grad, self_weight.T, preferred_element_type=jnp.float32)
        if m + 1 < micro_total:
            table_grad = spread(counts_all[m][0], back, tiles_all[m], table_grad, agg_scale)
            table_grad = table_grad.at[dest_rows[m]].add(own_grad)
        else:
            pending.append((m, back, own_grad))

    sizes = [up_sum.size, down_sum.size, self_sum.size, neighbor_sum.size]
    line = jnp.concatenate([up_sum.ravel(), down_sum.ravel(), self_sum.ravel(), neighbor_sum.ravel()])
    line = summed_by_kernel(line, "batch", 0)
    ends = [0]
    for s in sizes:
        ends.append(ends[-1] + s)
    up_sum = line[ends[0] : ends[1]].reshape(up_weight.shape)
    down_sum = line[ends[1] : ends[2]].reshape(down_weight.shape)
    self_sum = line[ends[2] : ends[3]].reshape(columns, H)
    neighbor_sum = line[ends[3] : ends[4]].reshape(columns, H)

    for m, back, own_grad in pending:
        table_grad = spread(counts_all[m][0], back, tiles_all[m], table_grad, agg_scale)
        table_grad = table_grad.at[dest_rows[m]].add(own_grad)
    return (
        table_grad.T,
        self_sum * norm_factor,
        neighbor_sum * norm_factor,
        up_sum * norm_factor,
        down_sum * norm_factor,
    )


def solution(mesh):
    in_specs = (
        P("feat", "batch"),
        P("feat", None),
        P("feat", None),
        P(),
        P(),
        P(None, None, "batch"),
        P(None, None, None, "batch"),
        P(None, None, "batch"),
        P(None, "batch"),
        P(None, "batch", None),
        P(None, ("batch", "feat"), None),
    )
    out_specs = (P("feat", "batch"), P("feat", None), P("feat", None), P(), P())
    return jax.shard_map(local, mesh=mesh, in_specs=in_specs, out_specs=out_specs, check_vma=False)
```

```python
import functools
import math

import jax
import jax.numpy as jnp
from jax import lax
from jax.experimental import pallas as pl
from jax.experimental.pallas import tpu as pltpu
from jax.sharding import PartitionSpec as P

H = 128
TD = 256
TS = 1024
K = 8
NB = 16
CS = 128


def gelu_slope(values):
    result, pullback = jax.vjp(jax.nn.gelu, values)
    return (result, pullback(jnp.ones_like(values))[0])


def mlp_pass(hidden, target, up_weight, down_weight):
    first_value, first_slope = gelu_slope(hidden)
    first_act = first_value.astype(jnp.bfloat16)
    inner_pre = jnp.dot(first_act, up_weight, preferred_element_type=jnp.float32)
    inner_value, inner_slope = gelu_slope(inner_pre)
    inner_act = inner_value.astype(jnp.bfloat16)
    down_part = jnp.dot(inner_act.T, target, preferred_element_type=jnp.float32)
    inner_grad = (
        jnp.dot(target, down_weight.T, preferred_element_type=jnp.float32) * inner_slope
    ).astype(jnp.bfloat16)
    up_part = jnp.dot(first_act.T, inner_grad, preferred_element_type=jnp.float32)
    hidden_grad = (
        jnp.dot(inner_grad, up_weight.T, preferred_element_type=jnp.float32) * first_slope
    ).astype(jnp.bfloat16)
    return (hidden_grad, up_part, down_part)


def reduced_piece(x, axis):
    n = lax.axis_size(axis)
    flat = x.reshape(n, -1)
    return lax.all_to_all(flat, axis, 0, 0, tiled=True).reshape(n, -1).sum(axis=0)


def spread_piece(mine, axis, shape):
    n = lax.axis_size(axis)
    return lax.all_to_all(jnp.broadcast_to(mine[None], (n, mine.size)), axis, 0, 0, tiled=True).reshape(shape)


def summed_over(x, axis):
    return spread_piece(reduced_piece(x, axis), axis, x.shape)


def gathered_over(x, axis, dim):
    n = lax.axis_size(axis)
    pieces = lax.all_to_all(jnp.broadcast_to(x[None], (n, *x.shape)), axis, 0, 0, tiled=True)
    pieces = jnp.moveaxis(pieces, 0, dim)
    shape = pieces.shape
    return pieces.reshape(*shape[:dim], shape[dim] * shape[dim + 1], *shape[dim + 2 :])


def agg_kernel(agg_scale, k_total, nt, *refs):
    tiles_ref, emb_ref, rows_ref, mask_ref = refs[:4]
    counts_ref, agg_ref, acc_ref = refs[-3:]
    k = pl.program_id(1)

    @pl.when(k == 0)
    def _():
        acc_ref[...] = jnp.zeros_like(acc_ref)

    msk = mask_ref[0, 0].astype(jnp.bfloat16)
    rows = rows_ref[0, 0]
    local_iota = lax.broadcasted_iota(jnp.int32, (CS, TD), 0).astype(jnp.bfloat16)
    one = jnp.ones((CS, TD), jnp.bfloat16)
    zero = jnp.zeros((CS, TD), jnp.bfloat16)

    def chunk(c, carry):
        start = pl.multiple_of(c * CS, CS)
        local = (rows - start).astype(jnp.float32)
        cnt = zero
        for j in range(NB):
            here = local[j : j + 1, :].astype(jnp.bfloat16)
            cnt = cnt + jnp.where(here == local_iota, one, zero)
        counts_ref[0, 0, pl.ds(start, CS), :] = cnt * msk
        return carry

    lax.fori_loop(0, TS // CS, chunk, 0)
    acc_ref[...] += jnp.dot(emb_ref[...], counts_ref[0, 0], preferred_element_type=jnp.float32)

    @pl.when(k == k_total - 1)
    def _():
        agg_ref[...] = (acc_ref[...] * agg_scale).astype(jnp.bfloat16)


def aggregate(embedding, tiles_flat, neighbor_rows, slot_mask, agg_scale, t0, t_count, into=None):
    columns, source_total = embedding.shape
    k_total, nb, dest_total = neighbor_rows.shape
    nt = dest_total // TD
    mask4 = slot_mask.reshape(k_total, 1, 1, dest_total)
    rows4 = neighbor_rows.reshape(k_total, 1, nb, dest_total)
    prefetch = jnp.concatenate([jnp.full((1,), t0, jnp.int32), tiles_flat])
    in_specs = [
        pl.BlockSpec((columns, TS), lambda t, k, tiles: (0, tiles[1 + k * nt + tiles[0] + t])),
        pl.BlockSpec((1, 1, nb, TD), lambda t, k, tiles: (k, 0, 0, tiles[0] + t)),
        pl.BlockSpec((1, 1, 1, TD), lambda t, k, tiles: (k, 0, 0, tiles[0] + t)),
    ]
    operands = [prefetch, embedding, rows4, mask4]
    aliases = {}
    if into is not None:
        in_specs += [pl.BlockSpec(memory_space=pl.ANY), pl.BlockSpec(memory_space=pl.ANY)]
        operands += list(into)
        aliases = {4: 0, 5: 1}
    grid_spec = pltpu.PrefetchScalarGridSpec(
        num_scalar_prefetch=1,
        grid=(t_count, k_total),
        in_specs=in_specs,
        out_specs=[
            pl.BlockSpec((1, 1, TS, TD), lambda t, k, tiles: (k, tiles[0] + t, 0, 0)),
            pl.BlockSpec((columns, TD), lambda t, k, tiles: (0, tiles[0] + t)),
        ],
        scratch_shapes=[pltpu.VMEM((columns, TD), jnp.float32)],
    )
    work = k_total * t_count * TD * TS
    return pl.pallas_call(
        functools.partial(agg_kernel, agg_scale, k_total, nt),
        grid_spec=grid_spec,
        out_shape=[
            jax.ShapeDtypeStruct((k_total, nt, TS, TD), jnp.bfloat16),
            jax.ShapeDtypeStruct((columns, dest_total), jnp.bfloat16),
        ],
        input_output_aliases=aliases,
        compiler_params=pltpu.CompilerParams(dimension_semantics=("arbitrary", "arbitrary")),
        cost_estimate=pl.CostEstimate(
            flops=2 * columns * work + 4 * nb * work,
            bytes_accessed=2 * work + 2 * columns * source_total,
            transcendentals=0,
        ),
    )(*operands)


def spread_kernel(agg_scale, k_total, nt, tiles_ref, counts_ref, back_ref, tg_in_ref, tg_ref):
    t = pl.program_id(0)
    k = pl.program_id(1)

    @pl.when((t == 0) & (k == 0))
    def _():
        tg_ref[...] = tg_in_ref[...]

    tile = tiles_ref[k * nt + t]
    start = pl.multiple_of(tile * TS, TS)
    part = jnp.dot(counts_ref[0, 0], back_ref[...], preferred_element_type=jnp.float32)
    tg_ref[pl.ds(start, TS), :] += part * agg_scale


def spread(counts, back, tiles_flat, table_grad, agg_scale):
    k_total, nt = counts.shape[:2]
    source_total, columns = table_grad.shape
    grid_spec = pltpu.PrefetchScalarGridSpec(
        num_scalar_prefetch=1,
        grid=(nt, k_total),
        in_specs=[
            pl.BlockSpec((1, 1, TS, TD), lambda t, k, tiles: (k, t, 0, 0)),
            pl.BlockSpec((TD, columns), lambda t, k, tiles: (t, 0)),
            pl.BlockSpec((source_total, columns), lambda t, k, tiles: (0, 0)),
        ],
        out_specs=pl.BlockSpec((source_total, columns), lambda t, k, tiles: (0, 0)),
    )
    work = k_total * nt * TD * TS
    return pl.pallas_call(
        functools.partial(spread_kernel, agg_scale, k_total, nt),
        grid_spec=grid_spec,
        out_shape=jax.ShapeDtypeStruct((source_total, columns), jnp.float32),
        input_output_aliases={3: 0},
        compiler_params=pltpu.CompilerParams(
            dimension_semantics=("arbitrary", "arbitrary"),
            vmem_limit_bytes=48 * 1024 * 1024,
        ),
        cost_estimate=pl.CostEstimate(
            flops=2 * columns * work,
            bytes_accessed=2 * work + 8 * source_total * columns,
            transcendentals=0,
        ),
    )(tiles_flat, counts, back, table_grad)


def local(
    embedding,
    self_weight,
    neighbor_weight,
    up_weight,
    down_weight,
    source_tiles,
    neighbor_rows,
    slot_mask,
    dest_rows,
    owner_order,
    output_grad,
):
    batch_total = lax.axis_size("batch")
    columns, source_total = embedding.shape
    micro_total = source_tiles.shape[0]
    dest_total = dest_rows.shape[1]
    agg_scale = 1.0 / math.sqrt(K * NB)
    norm_factor = 1.0 / math.sqrt(micro_total * dest_total * batch_total)
    tiles_all = source_tiles.reshape(micro_total, -1)

    target_all = gathered_over(output_grad, "feat", 1)
    table = embedding.T
    nt = dest_total // TD
    half = nt // 2
    counts_all, own_all, pieces = [], [], []
    for m in range(micro_total):
        first = aggregate(embedding, tiles_all[m], neighbor_rows[m], slot_mask[m], agg_scale, 0, half)
        if m > 0:
            first_counts, first_agg, pieces[m - 1] = lax.optimization_barrier(
                (first[0], first[1], pieces[m - 1])
            )
            first = (first_counts, first_agg)
        counts, agg_t = aggregate(
            embedding, tiles_all[m], neighbor_rows[m], slot_mask[m], agg_scale, half, nt - half, into=first
        )
        own = table[dest_rows[m]]
        partial = jnp.dot(own, self_weight, preferred_element_type=jnp.float32) + lax.dot_general(
            agg_t, neighbor_weight, (((0,), (0,)), ((), ())), preferred_element_type=jnp.float32
        )
        counts_all.append((counts, agg_t))
        own_all.append(own)
        pieces.append(reduced_piece(partial, "feat"))
    hidden_all = [spread_piece(p, "feat", (dest_total, H)) for p in pieces]

    up_sum = jnp.zeros(up_weight.shape, jnp.float32)
    down_sum = jnp.zeros(down_weight.shape, jnp.float32)
    self_sum = jnp.zeros((columns, H), jnp.float32)
    neighbor_sum = jnp.zeros((columns, H), jnp.float32)
    table_grad = jnp.zeros((source_total, columns), jnp.float32)
    pending = []
    for m in range(micro_total):
        hidden = hidden_all[m]
        if m > 0:
            hidden, table_grad = lax.optimization_barrier((hidden, table_grad))
        agg_t = counts_all[m][1]
        row_order = owner_order[m, 0]
        target = jnp.zeros(target_all.shape[1:], target_all.dtype).at[row_order].set(target_all[m])
        hidden_grad, up_part, down_part = mlp_pass(hidden, target, up_weight, down_weight)
        up_sum = up_sum + up_part
        down_sum = down_sum + down_part
        self_sum = self_sum + jnp.dot(own_all[m].T, hidden_grad, preferred_element_type=jnp.float32)
        neighbor_sum = neighbor_sum + jnp.dot(agg_t, hidden_grad, preferred_element_type=jnp.float32)
        back = jnp.dot(hidden_grad, neighbor_weight.T, preferred_element_type=jnp.float32).astype(jnp.bfloat16)
        own_grad = jnp.dot(hidden_grad, self_weight.T, preferred_element_type=jnp.float32)
        if m + 1 < micro_total:
            table_grad = spread(counts_all[m][0], back, tiles_all[m], table_grad, agg_scale)
            table_grad = table_grad.at[dest_rows[m]].add(own_grad)
        else:
            pending.append((m, back, own_grad))

    sizes = [up_sum.size, down_sum.size, self_sum.size, neighbor_sum.size]
    line = jnp.concatenate([up_sum.ravel(), down_sum.ravel(), self_sum.ravel(), neighbor_sum.ravel()])
    line = summed_over(line, "batch")
    ends = [0]
    for s in sizes:
        ends.append(ends[-1] + s)
    up_sum = line[ends[0] : ends[1]].reshape(up_weight.shape)
    down_sum = line[ends[1] : ends[2]].reshape(down_weight.shape)
    self_sum = line[ends[2] : ends[3]].reshape(columns, H)
    neighbor_sum = line[ends[3] : ends[4]].reshape(columns, H)

    for m, back, own_grad in pending:
        table_grad = spread(counts_all[m][0], back, tiles_all[m], table_grad, agg_scale)
        table_grad = table_grad.at[dest_rows[m]].add(own_grad)
    return (
        table_grad.T,
        self_sum * norm_factor,
        neighbor_sum * norm_factor,
        up_sum * norm_factor,
        down_sum * norm_factor,
    )


def solution(mesh):
    in_specs = (
        P("feat", "batch"),
        P("feat", None),
        P("feat", None),
        P(),
        P(),
        P(None, None, "batch"),
        P(None, None, None, "batch"),
        P(None, None, "batch"),
        P(None, "batch"),
        P(None, "batch", None),
        P(None, ("batch", "feat"), None),
    )
    out_specs = (P("feat", "batch"), P("feat", None), P("feat", None), P(), P())
    return jax.shard_map(local, mesh=mesh, in_specs=in_specs, out_specs=out_specs, check_vma=False)
```

```python
import functools
import math

import jax
import jax.numpy as jnp
from jax import lax
from jax.experimental import pallas as pl
from jax.experimental.pallas import tpu as pltpu
from jax.sharding import PartitionSpec as P

H = 128
TD = 256
TS = 1024
K = 8
NB = 16
CS = 256


def gelu_slope(values):
    result, pullback = jax.vjp(jax.nn.gelu, values)
    return (result, pullback(jnp.ones_like(values))[0])


def mlp_pass(hidden, target, up_weight, down_weight):
    first_value, first_slope = gelu_slope(hidden)
    first_act = first_value.astype(jnp.bfloat16)
    inner_pre = jnp.dot(first_act, up_weight, preferred_element_type=jnp.float32)
    inner_value, inner_slope = gelu_slope(inner_pre)
    inner_act = inner_value.astype(jnp.bfloat16)
    down_part = jnp.dot(inner_act.T, target, preferred_element_type=jnp.float32)
    inner_grad = (
        jnp.dot(target, down_weight.T, preferred_element_type=jnp.float32) * inner_slope
    ).astype(jnp.bfloat16)
    up_part = jnp.dot(first_act.T, inner_grad, preferred_element_type=jnp.float32)
    hidden_grad = (
        jnp.dot(inner_grad, up_weight.T, preferred_element_type=jnp.float32) * first_slope
    ).astype(jnp.bfloat16)
    return (hidden_grad, up_part, down_part)


def summed_over(x, axis):
    n = lax.axis_size(axis)
    flat = x.reshape(n, -1)
    mine = lax.all_to_all(flat, axis, 0, 0, tiled=True).reshape(n, -1).sum(axis=0)
    spread_back = lax.all_to_all(jnp.broadcast_to(mine[None], (n, mine.size)), axis, 0, 0, tiled=True)
    return spread_back.reshape(x.shape)


def gathered_over(x, axis, dim):
    n = lax.axis_size(axis)
    pieces = lax.all_to_all(jnp.broadcast_to(x[None], (n, *x.shape)), axis, 0, 0, tiled=True)
    pieces = jnp.moveaxis(pieces, 0, dim)
    shape = pieces.shape
    return pieces.reshape(*shape[:dim], shape[dim] * shape[dim + 1], *shape[dim + 2 :])


def agg_kernel(agg_scale, k_total, nt, tiles_ref, emb_ref, rows_ref, mask_ref, counts_ref, agg_ref, acc_ref):
    k = pl.program_id(1)

    @pl.when(k == 0)
    def _():
        acc_ref[...] = jnp.zeros_like(acc_ref)

    msk = mask_ref[0, 0].astype(jnp.bfloat16)
    rows = rows_ref[0, 0]
    local_iota = lax.broadcasted_iota(jnp.int32, (CS, TD), 0).astype(jnp.bfloat16)
    one = jnp.ones((CS, TD), jnp.bfloat16)
    zero = jnp.zeros((CS, TD), jnp.bfloat16)

    def chunk(c, carry):
        start = pl.multiple_of(c * CS, CS)
        local = (rows - start).astype(jnp.float32)
        cnt = zero
        for j in range(NB):
            here = local[j : j + 1, :].astype(jnp.bfloat16)
            cnt = cnt + jnp.where(here == local_iota, one, zero)
        counts_ref[0, 0, pl.ds(start, CS), :] = cnt * msk
        return carry

    lax.fori_loop(0, TS // CS, chunk, 0)
    acc_ref[...] += jnp.dot(emb_ref[...], counts_ref[0, 0], preferred_element_type=jnp.float32)

    @pl.when(k == k_total - 1)
    def _():
        agg_ref[...] = (acc_ref[...] * agg_scale).astype(jnp.bfloat16)


def aggregate(embedding, tiles_flat, neighbor_rows, slot_mask, agg_scale):
    columns, source_total = embedding.shape
    k_total, nb, dest_total = neighbor_rows.shape
    nt = dest_total // TD
    mask4 = slot_mask.reshape(k_total, 1, 1, dest_total)
    rows4 = neighbor_rows.reshape(k_total, 1, nb, dest_total)
    grid_spec = pltpu.PrefetchScalarGridSpec(
        num_scalar_prefetch=1,
        grid=(nt, k_total),
        in_specs=[
            pl.BlockSpec((columns, TS), lambda t, k, tiles: (0, tiles[k * nt + t])),
            pl.BlockSpec((1, 1, nb, TD), lambda t, k, tiles: (k, 0, 0, t)),
            pl.BlockSpec((1, 1, 1, TD), lambda t, k, tiles: (k, 0, 0, t)),
        ],
        out_specs=[
            pl.BlockSpec((1, 1, TS, TD), lambda t, k, tiles: (k, t, 0, 0)),
            pl.BlockSpec((columns, TD), lambda t, k, tiles: (0, t)),
        ],
        scratch_shapes=[pltpu.VMEM((columns, TD), jnp.float32)],
    )
    work = k_total * dest_total * TS
    return pl.pallas_call(
        functools.partial(agg_kernel, agg_scale, k_total, nt),
        grid_spec=grid_spec,
        out_shape=[
            jax.ShapeDtypeStruct((k_total, nt, TS, TD), jnp.bfloat16),
            jax.ShapeDtypeStruct((columns, dest_total), jnp.bfloat16),
        ],
        compiler_params=pltpu.CompilerParams(dimension_semantics=("arbitrary", "arbitrary")),
        cost_estimate=pl.CostEstimate(
            flops=2 * columns * work + 4 * nb * work,
            bytes_accessed=2 * work + 2 * columns * source_total,
            transcendentals=0,
        ),
    )(tiles_flat, embedding, rows4, mask4)


def spread_kernel(agg_scale, k_total, nt, tiles_ref, counts_ref, back_ref, tg_in_ref, tg_ref):
    t = pl.program_id(0)
    k = pl.program_id(1)

    @pl.when((t == 0) & (k == 0))
    def _():
        tg_ref[...] = tg_in_ref[...]

    tile = tiles_ref[k * nt + t]
    start = pl.multiple_of(tile * TS, TS)
    part = lax.dot_general(
        back_ref[...], counts_ref[0, 0], (((1,), (1,)), ((), ())), preferred_element_type=jnp.float32
    )
    tg_ref[:, pl.ds(start, TS)] += part * agg_scale


def spread(counts, back, tiles_flat, table_grad, agg_scale):
    k_total, nt = counts.shape[:2]
    columns, source_total = table_grad.shape
    grid_spec = pltpu.PrefetchScalarGridSpec(
        num_scalar_prefetch=1,
        grid=(nt, k_total),
        in_specs=[
            pl.BlockSpec((1, 1, TS, TD), lambda t, k, tiles: (k, t, 0, 0)),
            pl.BlockSpec((columns, TD), lambda t, k, tiles: (0, t)),
            pl.BlockSpec((columns, source_total), lambda t, k, tiles: (0, 0)),
        ],
        out_specs=pl.BlockSpec((columns, source_total), lambda t, k, tiles: (0, 0)),
    )
    work = k_total * nt * TD * TS
    return pl.pallas_call(
        functools.partial(spread_kernel, agg_scale, k_total, nt),
        grid_spec=grid_spec,
        out_shape=jax.ShapeDtypeStruct((columns, source_total), jnp.float32),
        input_output_aliases={3: 0},
        compiler_params=pltpu.CompilerParams(
            dimension_semantics=("arbitrary", "arbitrary"),
            vmem_limit_bytes=48 * 1024 * 1024,
        ),
        cost_estimate=pl.CostEstimate(
            flops=2 * columns * work,
            bytes_accessed=2 * work + 8 * source_total * columns,
            transcendentals=0,
        ),
    )(tiles_flat, counts, back, table_grad)


def local(
    embedding,
    self_weight,
    neighbor_weight,
    up_weight,
    down_weight,
    source_tiles,
    neighbor_rows,
    slot_mask,
    dest_rows,
    owner_order,
    output_grad,
):
    batch_total = lax.axis_size("batch")
    columns, source_total = embedding.shape
    micro_total = source_tiles.shape[0]
    dest_total = dest_rows.shape[1]
    agg_scale = 1.0 / math.sqrt(K * NB)
    norm_factor = 1.0 / math.sqrt(micro_total * dest_total * batch_total)
    tiles_all = source_tiles.reshape(micro_total, -1)

    target_all = gathered_over(output_grad, "feat", 1)
    table = embedding.T
    counts_all, own_all, hidden_all = [], [], []
    for m in range(micro_total):
        counts, agg_t = aggregate(embedding, tiles_all[m], neighbor_rows[m], slot_mask[m], agg_scale)
        own = table[dest_rows[m]]
        partial = jnp.dot(own, self_weight, preferred_element_type=jnp.float32) + lax.dot_general(
            agg_t, neighbor_weight, (((0,), (0,)), ((), ())), preferred_element_type=jnp.float32
        )
        counts_all.append((counts, agg_t))
        own_all.append(own)
        hidden_all.append(summed_over(partial, "feat"))

    up_sum = jnp.zeros(up_weight.shape, jnp.float32)
    down_sum = jnp.zeros(down_weight.shape, jnp.float32)
    self_sum = jnp.zeros((columns, H), jnp.float32)
    neighbor_sum = jnp.zeros((columns, H), jnp.float32)
    table_grad = jnp.zeros((columns, source_total), jnp.float32)
    pending = []
    for m in range(micro_total):
        hidden = hidden_all[m]
        if m > 0:
            hidden, table_grad = lax.optimization_barrier((hidden, table_grad))
        agg_t = counts_all[m][1]
        row_order = owner_order[m, 0]
        target = jnp.zeros(target_all.shape[1:], target_all.dtype).at[row_order].set(target_all[m])
        hidden_grad, up_part, down_part = mlp_pass(hidden, target, up_weight, down_weight)
        up_sum = up_sum + up_part
        down_sum = down_sum + down_part
        self_sum = self_sum + jnp.dot(own_all[m].T, hidden_grad, preferred_element_type=jnp.float32)
        neighbor_sum = neighbor_sum + jnp.dot(agg_t, hidden_grad, preferred_element_type=jnp.float32)
        back = lax.dot_general(
            neighbor_weight, hidden_grad, (((1,), (1,)), ((), ())), preferred_element_type=jnp.float32
        ).astype(jnp.bfloat16)
        own_grad = lax.dot_general(
            self_weight, hidden_grad, (((1,), (1,)), ((), ())), preferred_element_type=jnp.float32
        )
        if m + 1 < micro_total:
            table_grad = spread(counts_all[m][0], back, tiles_all[m], table_grad, agg_scale)
            table_grad = table_grad.at[:, dest_rows[m]].add(own_grad)
        else:
            pending.append((m, back, own_grad))

    sizes = [up_sum.size, down_sum.size, self_sum.size, neighbor_sum.size]
    line = jnp.concatenate([up_sum.ravel(), down_sum.ravel(), self_sum.ravel(), neighbor_sum.ravel()])
    line = summed_over(line, "batch")
    ends = [0]
    for s in sizes:
        ends.append(ends[-1] + s)
    up_sum = line[ends[0] : ends[1]].reshape(up_weight.shape)
    down_sum = line[ends[1] : ends[2]].reshape(down_weight.shape)
    self_sum = line[ends[2] : ends[3]].reshape(columns, H)
    neighbor_sum = line[ends[3] : ends[4]].reshape(columns, H)

    for m, back, own_grad in pending:
        table_grad = spread(counts_all[m][0], back, tiles_all[m], table_grad, agg_scale)
        table_grad = table_grad.at[:, dest_rows[m]].add(own_grad)
    return (
        table_grad,
        self_sum * norm_factor,
        neighbor_sum * norm_factor,
        up_sum * norm_factor,
        down_sum * norm_factor,
    )


def solution(mesh):
    in_specs = (
        P("feat", "batch"),
        P("feat", None),
        P("feat", None),
        P(),
        P(),
        P(None, None, "batch"),
        P(None, None, None, "batch"),
        P(None, None, "batch"),
        P(None, "batch"),
        P(None, "batch", None),
        P(None, ("batch", "feat"), None),
    )
    out_specs = (P("feat", "batch"), P("feat", None), P("feat", None), P(), P())
    return jax.shard_map(local, mesh=mesh, in_specs=in_specs, out_specs=out_specs, check_vma=False)
```

```python
import functools
import math

import jax
import jax.numpy as jnp
from jax import lax
from jax.experimental import pallas as pl
from jax.experimental.pallas import tpu as pltpu
from jax.sharding import PartitionSpec as P

H = 128
TD = 256
TS = 1024
K = 8
NB = 16
CS = 256


def gelu_slope(values):
    result, pullback = jax.vjp(jax.nn.gelu, values)
    return (result, pullback(jnp.ones_like(values))[0])


def mlp_pass(hidden, target, up_weight, down_weight):
    first_value, first_slope = gelu_slope(hidden)
    first_act = first_value.astype(jnp.bfloat16)
    inner_pre = jnp.dot(first_act, up_weight, preferred_element_type=jnp.float32)
    inner_value, inner_slope = gelu_slope(inner_pre)
    inner_act = inner_value.astype(jnp.bfloat16)
    down_part = jnp.dot(inner_act.T, target, preferred_element_type=jnp.float32)
    inner_grad = (
        jnp.dot(target, down_weight.T, preferred_element_type=jnp.float32) * inner_slope
    ).astype(jnp.bfloat16)
    up_part = jnp.dot(first_act.T, inner_grad, preferred_element_type=jnp.float32)
    hidden_grad = (
        jnp.dot(inner_grad, up_weight.T, preferred_element_type=jnp.float32) * first_slope
    ).astype(jnp.bfloat16)
    return (hidden_grad, up_part, down_part)


def summed_over(x, axis):
    n = lax.axis_size(axis)
    flat = x.reshape(n, -1)
    mine = lax.all_to_all(flat, axis, 0, 0, tiled=True).reshape(n, -1).sum(axis=0)
    spread_back = lax.all_to_all(jnp.broadcast_to(mine[None], (n, mine.size)), axis, 0, 0, tiled=True)
    return spread_back.reshape(x.shape)


def gathered_over(x, axis, dim):
    n = lax.axis_size(axis)
    pieces = lax.all_to_all(jnp.broadcast_to(x[None], (n, *x.shape)), axis, 0, 0, tiled=True)
    pieces = jnp.moveaxis(pieces, 0, dim)
    shape = pieces.shape
    return pieces.reshape(*shape[:dim], shape[dim] * shape[dim + 1], *shape[dim + 2 :])


def agg_kernel(agg_scale, k_total, nt, tiles_ref, emb_ref, rows_ref, mask_ref, counts_ref, agg_ref, acc_ref):
    k = pl.program_id(1)

    @pl.when(k == 0)
    def _():
        acc_ref[...] = jnp.zeros_like(acc_ref)

    msk = mask_ref[0, 0].astype(jnp.bfloat16)
    rows = rows_ref[0, 0]
    local_iota = lax.broadcasted_iota(jnp.int32, (CS, TD), 0).astype(jnp.bfloat16)
    one = jnp.ones((CS, TD), jnp.bfloat16)
    zero = jnp.zeros((CS, TD), jnp.bfloat16)

    def chunk(c, carry):
        start = pl.multiple_of(c * CS, CS)
        local = (rows - start).astype(jnp.float32)
        cnt = zero
        for j in range(NB):
            here = local[j : j + 1, :].astype(jnp.bfloat16)
            cnt = cnt + jnp.where(here == local_iota, one, zero)
        counts_ref[0, 0, pl.ds(start, CS), :] = cnt * msk
        return carry

    lax.fori_loop(0, TS // CS, chunk, 0)
    acc_ref[...] += jnp.dot(emb_ref[...], counts_ref[0, 0], preferred_element_type=jnp.float32)

    @pl.when(k == k_total - 1)
    def _():
        agg_ref[...] = (acc_ref[...] * agg_scale).astype(jnp.bfloat16)


def aggregate(embedding, tiles_flat, neighbor_rows, slot_mask, agg_scale):
    columns, source_total = embedding.shape
    k_total, nb, dest_total = neighbor_rows.shape
    nt = dest_total // TD
    mask4 = slot_mask.reshape(k_total, 1, 1, dest_total)
    rows4 = neighbor_rows.reshape(k_total, 1, nb, dest_total)
    grid_spec = pltpu.PrefetchScalarGridSpec(
        num_scalar_prefetch=1,
        grid=(nt, k_total),
        in_specs=[
            pl.BlockSpec((columns, TS), lambda t, k, tiles: (0, tiles[k * nt + t])),
            pl.BlockSpec((1, 1, nb, TD), lambda t, k, tiles: (k, 0, 0, t)),
            pl.BlockSpec((1, 1, 1, TD), lambda t, k, tiles: (k, 0, 0, t)),
        ],
        out_specs=[
            pl.BlockSpec((1, 1, TS, TD), lambda t, k, tiles: (k, t, 0, 0)),
            pl.BlockSpec((columns, TD), lambda t, k, tiles: (0, t)),
        ],
        scratch_shapes=[pltpu.VMEM((columns, TD), jnp.float32)],
    )
    work = k_total * dest_total * TS
    return pl.pallas_call(
        functools.partial(agg_kernel, agg_scale, k_total, nt),
        grid_spec=grid_spec,
        out_shape=[
            jax.ShapeDtypeStruct((k_total, nt, TS, TD), jnp.bfloat16),
            jax.ShapeDtypeStruct((columns, dest_total), jnp.bfloat16),
        ],
        compiler_params=pltpu.CompilerParams(dimension_semantics=("arbitrary", "arbitrary")),
        cost_estimate=pl.CostEstimate(
            flops=2 * columns * work + 4 * nb * work,
            bytes_accessed=2 * work + 2 * columns * source_total,
            transcendentals=0,
        ),
    )(tiles_flat, embedding, rows4, mask4)


def spread_kernel(agg_scale, k_total, nt, tiles_ref, counts_ref, back_ref, own_ref, tg_in_ref, tg_ref):
    t = pl.program_id(0)
    k = pl.program_id(1)

    @pl.when((t == 0) & (k == 0))
    def _():
        tg_ref[...] = tg_in_ref[...]

    tile = tiles_ref[k * nt + t]
    start = pl.multiple_of(tile * TS, TS)
    part = jnp.dot(counts_ref[0, 0], back_ref[...], preferred_element_type=jnp.float32)
    tg_ref[pl.ds(start, TS), :] += part * agg_scale

    @pl.when((t == nt - 1) & (k == k_total - 1))
    def _():
        base = k_total * nt

        def one_row(d, carry):
            row = tiles_ref[base + d]
            tg_ref[pl.ds(row, 1), :] += own_ref[pl.ds(d, 1), :]
            return carry

        lax.fori_loop(0, own_ref.shape[0], one_row, 0, unroll=8)


def spread(counts, back, own_grad, dest, tiles_flat, table_grad, agg_scale):
    k_total, nt = counts.shape[:2]
    source_total, columns = table_grad.shape
    prefetch = jnp.concatenate([tiles_flat, dest])
    grid_spec = pltpu.PrefetchScalarGridSpec(
        num_scalar_prefetch=1,
        grid=(nt, k_total),
        in_specs=[
            pl.BlockSpec((1, 1, TS, TD), lambda t, k, tiles: (k, t, 0, 0)),
            pl.BlockSpec((TD, columns), lambda t, k, tiles: (t, 0)),
            pl.BlockSpec(own_grad.shape, lambda t, k, tiles: (0, 0)),
            pl.BlockSpec((source_total, columns), lambda t, k, tiles: (0, 0)),
        ],
        out_specs=pl.BlockSpec((source_total, columns), lambda t, k, tiles: (0, 0)),
    )
    work = k_total * nt * TD * TS
    return pl.pallas_call(
        functools.partial(spread_kernel, agg_scale, k_total, nt),
        grid_spec=grid_spec,
        out_shape=jax.ShapeDtypeStruct((source_total, columns), jnp.float32),
        input_output_aliases={4: 0},
        compiler_params=pltpu.CompilerParams(
            dimension_semantics=("arbitrary", "arbitrary"),
            vmem_limit_bytes=48 * 1024 * 1024,
        ),
        cost_estimate=pl.CostEstimate(
            flops=2 * columns * work,
            bytes_accessed=2 * work + 8 * source_total * columns,
            transcendentals=0,
        ),
    )(prefetch, counts, back, own_grad, table_grad)


def local(
    embedding,
    self_weight,
    neighbor_weight,
    up_weight,
    down_weight,
    source_tiles,
    neighbor_rows,
    slot_mask,
    dest_rows,
    owner_order,
    output_grad,
):
    batch_total = lax.axis_size("batch")
    columns, source_total = embedding.shape
    micro_total = source_tiles.shape[0]
    dest_total = dest_rows.shape[1]
    agg_scale = 1.0 / math.sqrt(K * NB)
    norm_factor = 1.0 / math.sqrt(micro_total * dest_total * batch_total)
    tiles_all = source_tiles.reshape(micro_total, -1)

    target_all = gathered_over(output_grad, "feat", 1)
    table = embedding.T
    counts_all, own_all, hidden_all = [], [], []
    for m in range(micro_total):
        counts, agg_t = aggregate(embedding, tiles_all[m], neighbor_rows[m], slot_mask[m], agg_scale)
        own = table[dest_rows[m]]
        partial = jnp.dot(own, self_weight, preferred_element_type=jnp.float32) + lax.dot_general(
            agg_t, neighbor_weight, (((0,), (0,)), ((), ())), preferred_element_type=jnp.float32
        )
        counts_all.append((counts, agg_t))
        own_all.append(own)
        hidden_all.append(summed_over(partial, "feat"))

    up_sum = jnp.zeros(up_weight.shape, jnp.float32)
    down_sum = jnp.zeros(down_weight.shape, jnp.float32)
    self_sum = jnp.zeros((columns, H), jnp.float32)
    neighbor_sum = jnp.zeros((columns, H), jnp.float32)
    table_grad = jnp.zeros((source_total, columns), jnp.float32)
    pending = []
    for m in range(micro_total):
        hidden = hidden_all[m]
        if m > 0:
            hidden, table_grad = lax.optimization_barrier((hidden, table_grad))
        agg_t = counts_all[m][1]
        row_order = owner_order[m, 0]
        target = jnp.zeros(target_all.shape[1:], target_all.dtype).at[row_order].set(target_all[m])
        hidden_grad, up_part, down_part = mlp_pass(hidden, target, up_weight, down_weight)
        up_sum = up_sum + up_part
        down_sum = down_sum + down_part
        self_sum = self_sum + jnp.dot(own_all[m].T, hidden_grad, preferred_element_type=jnp.float32)
        neighbor_sum = neighbor_sum + jnp.dot(agg_t, hidden_grad, preferred_element_type=jnp.float32)
        back = jnp.dot(hidden_grad, neighbor_weight.T, preferred_element_type=jnp.float32).astype(jnp.bfloat16)
        own_grad = jnp.dot(hidden_grad, self_weight.T, preferred_element_type=jnp.float32)
        if m + 1 < micro_total:
            table_grad = spread(
                counts_all[m][0], back, own_grad, dest_rows[m], tiles_all[m], table_grad, agg_scale
            )
        else:
            pending.append((m, back, own_grad))

    sizes = [up_sum.size, down_sum.size, self_sum.size, neighbor_sum.size]
    line = jnp.concatenate([up_sum.ravel(), down_sum.ravel(), self_sum.ravel(), neighbor_sum.ravel()])
    line = summed_over(line, "batch")
    ends = [0]
    for s in sizes:
        ends.append(ends[-1] + s)
    up_sum = line[ends[0] : ends[1]].reshape(up_weight.shape)
    down_sum = line[ends[1] : ends[2]].reshape(down_weight.shape)
    self_sum = line[ends[2] : ends[3]].reshape(columns, H)
    neighbor_sum = line[ends[3] : ends[4]].reshape(columns, H)

    for m, back, own_grad in pending:
        table_grad = spread(
            counts_all[m][0], back, own_grad, dest_rows[m], tiles_all[m], table_grad, agg_scale
        )
    return (
        table_grad.T,
        self_sum * norm_factor,
        neighbor_sum * norm_factor,
        up_sum * norm_factor,
        down_sum * norm_factor,
    )


def solution(mesh):
    in_specs = (
        P("feat", "batch"),
        P("feat", None),
        P("feat", None),
        P(),
        P(),
        P(None, None, "batch"),
        P(None, None, None, "batch"),
        P(None, None, "batch"),
        P(None, "batch"),
        P(None, "batch", None),
        P(None, ("batch", "feat"), None),
    )
    out_specs = (P("feat", "batch"), P("feat", None), P("feat", None), P(), P())
    return jax.shard_map(local, mesh=mesh, in_specs=in_specs, out_specs=out_specs, check_vma=False)
```

```python
import functools
import math

import jax
import jax.numpy as jnp
from jax import lax
from jax.experimental import pallas as pl
from jax.experimental.pallas import tpu as pltpu
from jax.sharding import PartitionSpec as P

H = 128
TD = 256
TS = 1024
K = 8
NB = 16
CS = 256


def gelu_slope(values):
    result, pullback = jax.vjp(jax.nn.gelu, values)
    return (result, pullback(jnp.ones_like(values))[0])


def mlp_pass(hidden, target, up_weight, down_weight):
    first_value, first_slope = gelu_slope(hidden)
    first_act = first_value.astype(jnp.bfloat16)
    inner_pre = jnp.dot(first_act, up_weight, preferred_element_type=jnp.float32)
    inner_value, inner_slope = gelu_slope(inner_pre)
    inner_act = inner_value.astype(jnp.bfloat16)
    down_part = jnp.dot(inner_act.T, target, preferred_element_type=jnp.float32)
    inner_grad = (
        jnp.dot(target, down_weight.T, preferred_element_type=jnp.float32) * inner_slope
    ).astype(jnp.bfloat16)
    up_part = jnp.dot(first_act.T, inner_grad, preferred_element_type=jnp.float32)
    hidden_grad = (
        jnp.dot(inner_grad, up_weight.T, preferred_element_type=jnp.float32) * first_slope
    ).astype(jnp.bfloat16)
    return (hidden_grad, up_part, down_part)


def summed_over(x, axis):
    n = lax.axis_size(axis)
    flat = x.reshape(n, -1)
    mine = lax.all_to_all(flat, axis, 0, 0, tiled=True).reshape(n, -1).sum(axis=0)
    spread_back = lax.all_to_all(jnp.broadcast_to(mine[None], (n, mine.size)), axis, 0, 0, tiled=True)
    return spread_back.reshape(x.shape)


def gathered_over(x, axis, dim):
    n = lax.axis_size(axis)
    pieces = lax.all_to_all(jnp.broadcast_to(x[None], (n, *x.shape)), axis, 0, 0, tiled=True)
    pieces = jnp.moveaxis(pieces, 0, dim)
    shape = pieces.shape
    return pieces.reshape(*shape[:dim], shape[dim] * shape[dim + 1], *shape[dim + 2 :])


def agg_kernel(agg_scale, k_total, nt, tiles_ref, emb_ref, rows_ref, mask_ref, counts_ref, agg_ref, acc_ref):
    k = pl.program_id(1)

    @pl.when(k == 0)
    def _():
        acc_ref[...] = jnp.zeros_like(acc_ref)

    msk = mask_ref[0, 0].astype(jnp.bfloat16)
    rows = rows_ref[0, 0]
    local_iota = lax.broadcasted_iota(jnp.int32, (CS, TD), 0).astype(jnp.bfloat16)
    one = jnp.ones((CS, TD), jnp.bfloat16)
    zero = jnp.zeros((CS, TD), jnp.bfloat16)

    def chunk(c, carry):
        start = pl.multiple_of(c * CS, CS)
        local = (rows - start).astype(jnp.float32)
        cnt = zero
        for j in range(0, NB, 2):
            here = local[j : j + 1, :].astype(jnp.bfloat16)
            there = local[j + 1 : j + 2, :].astype(jnp.bfloat16)
            cnt = cnt + (jnp.where(here == local_iota, one, zero) + jnp.where(there == local_iota, one, zero))
        counts_ref[0, 0, pl.ds(start, CS), :] = cnt * msk
        return carry

    lax.fori_loop(0, TS // CS, chunk, 0)
    acc_ref[...] += jnp.dot(emb_ref[...], counts_ref[0, 0], preferred_element_type=jnp.float32)

    @pl.when(k == k_total - 1)
    def _():
        agg_ref[...] = (acc_ref[...] * agg_scale).astype(jnp.bfloat16)


def aggregate(embedding, tiles_flat, neighbor_rows, slot_mask, agg_scale):
    columns, source_total = embedding.shape
    k_total, nb, dest_total = neighbor_rows.shape
    nt = dest_total // TD
    mask4 = slot_mask.reshape(k_total, 1, 1, dest_total)
    rows4 = neighbor_rows.reshape(k_total, 1, nb, dest_total)
    grid_spec = pltpu.PrefetchScalarGridSpec(
        num_scalar_prefetch=1,
        grid=(nt, k_total),
        in_specs=[
            pl.BlockSpec((columns, TS), lambda t, k, tiles: (0, tiles[k * nt + t])),
            pl.BlockSpec((1, 1, nb, TD), lambda t, k, tiles: (k, 0, 0, t)),
            pl.BlockSpec((1, 1, 1, TD), lambda t, k, tiles: (k, 0, 0, t)),
        ],
        out_specs=[
            pl.BlockSpec((1, 1, TS, TD), lambda t, k, tiles: (k, t, 0, 0)),
            pl.BlockSpec((columns, TD), lambda t, k, tiles: (0, t)),
        ],
        scratch_shapes=[pltpu.VMEM((columns, TD), jnp.float32)],
    )
    work = k_total * dest_total * TS
    return pl.pallas_call(
        functools.partial(agg_kernel, agg_scale, k_total, nt),
        grid_spec=grid_spec,
        out_shape=[
            jax.ShapeDtypeStruct((k_total, nt, TS, TD), jnp.bfloat16),
            jax.ShapeDtypeStruct((columns, dest_total), jnp.bfloat16),
        ],
        compiler_params=pltpu.CompilerParams(dimension_semantics=("arbitrary", "arbitrary")),
        cost_estimate=pl.CostEstimate(
            flops=2 * columns * work + 4 * nb * work,
            bytes_accessed=2 * work + 2 * columns * source_total,
            transcendentals=0,
        ),
    )(tiles_flat, embedding, rows4, mask4)


def spread_kernel(agg_scale, k_total, nt, tiles_ref, counts_ref, back_ref, own_ref, tg_in_ref, tg_ref):
    t = pl.program_id(0)
    k = pl.program_id(1)

    @pl.when((t == 0) & (k == 0))
    def _():
        tg_ref[...] = tg_in_ref[...]

    tile = tiles_ref[k * nt + t]
    start = pl.multiple_of(tile * TS, TS)
    part = jnp.dot(counts_ref[0, 0], back_ref[...], preferred_element_type=jnp.float32)
    tg_ref[pl.ds(start, TS), :] += part * agg_scale

    @pl.when((t == nt - 1) & (k == k_total - 1))
    def _():
        base = k_total * nt

        def one_row(d, carry):
            row = tiles_ref[base + d]
            tg_ref[pl.ds(row, 1), :] += own_ref[pl.ds(d, 1), :]
            return carry

        lax.fori_loop(0, own_ref.shape[0], one_row, 0, unroll=8)


def spread(counts, back, own_grad, dest, tiles_flat, table_grad, agg_scale):
    k_total, nt = counts.shape[:2]
    source_total, columns = table_grad.shape
    prefetch = jnp.concatenate([tiles_flat, dest])
    grid_spec = pltpu.PrefetchScalarGridSpec(
        num_scalar_prefetch=1,
        grid=(nt, k_total),
        in_specs=[
            pl.BlockSpec((1, 1, TS, TD), lambda t, k, tiles: (k, t, 0, 0)),
            pl.BlockSpec((TD, columns), lambda t, k, tiles: (t, 0)),
            pl.BlockSpec(own_grad.shape, lambda t, k, tiles: (0, 0)),
            pl.BlockSpec((source_total, columns), lambda t, k, tiles: (0, 0)),
        ],
        out_specs=pl.BlockSpec((source_total, columns), lambda t, k, tiles: (0, 0)),
    )
    work = k_total * nt * TD * TS
    return pl.pallas_call(
        functools.partial(spread_kernel, agg_scale, k_total, nt),
        grid_spec=grid_spec,
        out_shape=jax.ShapeDtypeStruct((source_total, columns), jnp.float32),
        input_output_aliases={4: 0},
        compiler_params=pltpu.CompilerParams(
            dimension_semantics=("arbitrary", "arbitrary"),
            vmem_limit_bytes=48 * 1024 * 1024,
        ),
        cost_estimate=pl.CostEstimate(
            flops=2 * columns * work,
            bytes_accessed=2 * work + 8 * source_total * columns,
            transcendentals=0,
        ),
    )(prefetch, counts, back, own_grad, table_grad)


def local(
    embedding,
    self_weight,
    neighbor_weight,
    up_weight,
    down_weight,
    source_tiles,
    neighbor_rows,
    slot_mask,
    dest_rows,
    owner_order,
    output_grad,
):
    batch_total = lax.axis_size("batch")
    columns, source_total = embedding.shape
    micro_total = source_tiles.shape[0]
    dest_total = dest_rows.shape[1]
    agg_scale = 1.0 / math.sqrt(K * NB)
    norm_factor = 1.0 / math.sqrt(micro_total * dest_total * batch_total)
    tiles_all = source_tiles.reshape(micro_total, -1)

    target_all = gathered_over(output_grad, "feat", 1)
    table = embedding.T
    counts_all, own_all, hidden_all = [], [], []
    for m in range(micro_total):
        counts, agg_t = aggregate(embedding, tiles_all[m], neighbor_rows[m], slot_mask[m], agg_scale)
        own = table[dest_rows[m]]
        partial = jnp.dot(own, self_weight, preferred_element_type=jnp.float32) + lax.dot_general(
            agg_t, neighbor_weight, (((0,), (0,)), ((), ())), preferred_element_type=jnp.float32
        )
        counts_all.append((counts, agg_t))
        own_all.append(own)
        hidden_all.append(summed_over(partial, "feat"))

    up_sum = jnp.zeros(up_weight.shape, jnp.float32)
    down_sum = jnp.zeros(down_weight.shape, jnp.float32)
    self_sum = jnp.zeros((columns, H), jnp.float32)
    neighbor_sum = jnp.zeros((columns, H), jnp.float32)
    table_grad = jnp.zeros((source_total, columns), jnp.float32)
    pending = []
    for m in range(micro_total):
        hidden = hidden_all[m]
        if m > 0:
            hidden, table_grad = lax.optimization_barrier((hidden, table_grad))
        agg_t = counts_all[m][1]
        row_order = owner_order[m, 0]
        target = jnp.zeros(target_all.shape[1:], target_all.dtype).at[row_order].set(target_all[m])
        hidden_grad, up_part, down_part = mlp_pass(hidden, target, up_weight, down_weight)
        up_sum = up_sum + up_part
        down_sum = down_sum + down_part
        self_sum = self_sum + jnp.dot(own_all[m].T, hidden_grad, preferred_element_type=jnp.float32)
        neighbor_sum = neighbor_sum + jnp.dot(agg_t, hidden_grad, preferred_element_type=jnp.float32)
        back = jnp.dot(hidden_grad, neighbor_weight.T, preferred_element_type=jnp.float32).astype(jnp.bfloat16)
        own_grad = jnp.dot(hidden_grad, self_weight.T, preferred_element_type=jnp.float32)
        if m + 1 < micro_total:
            table_grad = spread(
                counts_all[m][0], back, own_grad, dest_rows[m], tiles_all[m], table_grad, agg_scale
            )
        else:
            pending.append((m, back, own_grad))

    sizes = [up_sum.size, down_sum.size, self_sum.size, neighbor_sum.size]
    line = jnp.concatenate([up_sum.ravel(), down_sum.ravel(), self_sum.ravel(), neighbor_sum.ravel()])
    line = summed_over(line, "batch")
    ends = [0]
    for s in sizes:
        ends.append(ends[-1] + s)
    up_sum = line[ends[0] : ends[1]].reshape(up_weight.shape)
    down_sum = line[ends[1] : ends[2]].reshape(down_weight.shape)
    self_sum = line[ends[2] : ends[3]].reshape(columns, H)
    neighbor_sum = line[ends[3] : ends[4]].reshape(columns, H)

    for m, back, own_grad in pending:
        table_grad = spread(
            counts_all[m][0], back, own_grad, dest_rows[m], tiles_all[m], table_grad, agg_scale
        )
    return (
        table_grad.T,
        self_sum * norm_factor,
        neighbor_sum * norm_factor,
        up_sum * norm_factor,
        down_sum * norm_factor,
    )


def solution(mesh):
    in_specs = (
        P("feat", "batch"),
        P("feat", None),
        P("feat", None),
        P(),
        P(),
        P(None, None, "batch"),
        P(None, None, None, "batch"),
        P(None, None, "batch"),
        P(None, "batch"),
        P(None, "batch", None),
        P(None, ("batch", "feat"), None),
    )
    out_specs = (P("feat", "batch"), P("feat", None), P("feat", None), P(), P())
    return jax.shard_map(local, mesh=mesh, in_specs=in_specs, out_specs=out_specs, check_vma=False)
```

```python
import functools
import math

import jax
import jax.numpy as jnp
from jax import lax
from jax.experimental import pallas as pl
from jax.experimental.pallas import tpu as pltpu
from jax.sharding import PartitionSpec as P

H = 128
TD = 256
TS = 1024
K = 8
NB = 16
CS = 256


def gelu_slope(values):
    result, pullback = jax.vjp(jax.nn.gelu, values)
    return (result, pullback(jnp.ones_like(values))[0])


def mlp_pass(hidden, target, up_weight, down_weight):
    first_value, first_slope = gelu_slope(hidden)
    first_act = first_value.astype(jnp.bfloat16)
    inner_pre = jnp.dot(first_act, up_weight, preferred_element_type=jnp.float32)
    inner_value, inner_slope = gelu_slope(inner_pre)
    inner_act = inner_value.astype(jnp.bfloat16)
    down_part = jnp.dot(inner_act.T, target, preferred_element_type=jnp.float32)
    inner_grad = (
        jnp.dot(target, down_weight.T, preferred_element_type=jnp.float32) * inner_slope
    ).astype(jnp.bfloat16)
    up_part = jnp.dot(first_act.T, inner_grad, preferred_element_type=jnp.float32)
    hidden_grad = (
        jnp.dot(inner_grad, up_weight.T, preferred_element_type=jnp.float32) * first_slope
    ).astype(jnp.bfloat16)
    return (hidden_grad, up_part, down_part)


def summed_over(x, axis):
    n = lax.axis_size(axis)
    flat = x.reshape(n, -1)
    mine = lax.all_to_all(flat, axis, 0, 0, tiled=True).reshape(n, -1).sum(axis=0)
    spread_back = lax.all_to_all(jnp.broadcast_to(mine[None], (n, mine.size)), axis, 0, 0, tiled=True)
    return spread_back.reshape(x.shape)


def gathered_over(x, axis, dim):
    n = lax.axis_size(axis)
    pieces = lax.all_to_all(jnp.broadcast_to(x[None], (n, *x.shape)), axis, 0, 0, tiled=True)
    pieces = jnp.moveaxis(pieces, 0, dim)
    shape = pieces.shape
    return pieces.reshape(*shape[:dim], shape[dim] * shape[dim + 1], *shape[dim + 2 :])


def agg_kernel(agg_scale, k_total, nt, tiles_ref, emb_ref, rows_ref, mask_ref, counts_ref, agg_ref, acc_ref):
    k = pl.program_id(1)

    @pl.when(k == 0)
    def _():
        acc_ref[...] = jnp.zeros_like(acc_ref)

    msk = mask_ref[0, 0].astype(jnp.bfloat16)
    rows = rows_ref[0, 0]
    local_iota = lax.broadcasted_iota(jnp.int32, (CS, TD), 0).astype(jnp.bfloat16)
    one = jnp.ones((CS, TD), jnp.bfloat16)
    zero = jnp.zeros((CS, TD), jnp.bfloat16)

    def chunk(c, carry):
        start = pl.multiple_of(c * CS, CS)
        local = (rows - start).astype(jnp.float32)
        cnt = zero
        for j in range(0, NB, 2):
            here = local[j : j + 1, :].astype(jnp.bfloat16)
            there = local[j + 1 : j + 2, :].astype(jnp.bfloat16)
            cnt = cnt + (jnp.where(here == local_iota, one, zero) + jnp.where(there == local_iota, one, zero))
        counts_ref[0, 0, pl.ds(start, CS), :] = cnt * msk
        return carry

    lax.fori_loop(0, TS // CS, chunk, 0)
    acc_ref[...] += jnp.dot(emb_ref[...], counts_ref[0, 0], preferred_element_type=jnp.float32)

    @pl.when(k == k_total - 1)
    def _():
        agg_ref[...] = (acc_ref[...] * agg_scale).astype(jnp.bfloat16)


def aggregate(embedding, tiles_flat, neighbor_rows, slot_mask, agg_scale):
    columns, source_total = embedding.shape
    k_total, nb, dest_total = neighbor_rows.shape
    nt = dest_total // TD
    mask4 = slot_mask.reshape(k_total, 1, 1, dest_total)
    rows4 = neighbor_rows.reshape(k_total, 1, nb, dest_total)
    grid_spec = pltpu.PrefetchScalarGridSpec(
        num_scalar_prefetch=1,
        grid=(nt, k_total),
        in_specs=[
            pl.BlockSpec((columns, TS), lambda t, k, tiles: (0, tiles[k * nt + t])),
            pl.BlockSpec((1, 1, nb, TD), lambda t, k, tiles: (k, 0, 0, t)),
            pl.BlockSpec((1, 1, 1, TD), lambda t, k, tiles: (k, 0, 0, t)),
        ],
        out_specs=[
            pl.BlockSpec((1, 1, TS, TD), lambda t, k, tiles: (k, t, 0, 0)),
            pl.BlockSpec((columns, TD), lambda t, k, tiles: (0, t)),
        ],
        scratch_shapes=[pltpu.VMEM((columns, TD), jnp.float32)],
    )
    work = k_total * dest_total * TS
    return pl.pallas_call(
        functools.partial(agg_kernel, agg_scale, k_total, nt),
        grid_spec=grid_spec,
        out_shape=[
            jax.ShapeDtypeStruct((k_total, nt, TS, TD), jnp.bfloat16),
            jax.ShapeDtypeStruct((columns, dest_total), jnp.bfloat16),
        ],
        compiler_params=pltpu.CompilerParams(dimension_semantics=("arbitrary", "arbitrary")),
        cost_estimate=pl.CostEstimate(
            flops=2 * columns * work + 4 * nb * work,
            bytes_accessed=2 * work + 2 * columns * source_total,
            transcendentals=0,
        ),
    )(tiles_flat, embedding, rows4, mask4)


def spread_kernel(agg_scale, k_total, nt, tiles_ref, counts_ref, back_ref, own_ref, *refs):
    tg_ref = refs[-1]
    t = pl.program_id(0)
    k = pl.program_id(1)

    @pl.when((t == 0) & (k == 0))
    def _():
        if len(refs) == 2:
            tg_ref[...] = refs[0][...]
        else:
            tg_ref[...] = jnp.zeros_like(tg_ref)

    tile = tiles_ref[k * nt + t]
    start = pl.multiple_of(tile * TS, TS)
    part = jnp.dot(counts_ref[0, 0], back_ref[...], preferred_element_type=jnp.float32)
    tg_ref[pl.ds(start, TS), :] += part * agg_scale

    @pl.when((t == nt - 1) & (k == k_total - 1))
    def _():
        base = k_total * nt

        def one_row(d, carry):
            row = tiles_ref[base + d]
            tg_ref[pl.ds(row, 1), :] += own_ref[pl.ds(d, 1), :]
            return carry

        lax.fori_loop(0, own_ref.shape[0], one_row, 0, unroll=8)


def spread(counts, back, own_grad, dest, tiles_flat, table_grad, agg_scale, source_total):
    k_total, nt = counts.shape[:2]
    columns = back.shape[1]
    prefetch = jnp.concatenate([tiles_flat, dest])
    in_specs = [
        pl.BlockSpec((1, 1, TS, TD), lambda t, k, tiles: (k, t, 0, 0)),
        pl.BlockSpec((TD, columns), lambda t, k, tiles: (t, 0)),
        pl.BlockSpec(own_grad.shape, lambda t, k, tiles: (0, 0)),
    ]
    operands = [prefetch, counts, back, own_grad]
    aliases = {}
    if table_grad is not None:
        in_specs.append(pl.BlockSpec((source_total, columns), lambda t, k, tiles: (0, 0)))
        operands.append(table_grad)
        aliases = {4: 0}
    grid_spec = pltpu.PrefetchScalarGridSpec(
        num_scalar_prefetch=1,
        grid=(nt, k_total),
        in_specs=in_specs,
        out_specs=pl.BlockSpec((source_total, columns), lambda t, k, tiles: (0, 0)),
    )
    work = k_total * nt * TD * TS
    return pl.pallas_call(
        functools.partial(spread_kernel, agg_scale, k_total, nt),
        grid_spec=grid_spec,
        out_shape=jax.ShapeDtypeStruct((source_total, columns), jnp.float32),
        input_output_aliases=aliases,
        compiler_params=pltpu.CompilerParams(
            dimension_semantics=("arbitrary", "arbitrary"),
            vmem_limit_bytes=48 * 1024 * 1024,
        ),
        cost_estimate=pl.CostEstimate(
            flops=2 * columns * work,
            bytes_accessed=2 * work + 8 * source_total * columns,
            transcendentals=0,
        ),
    )(*operands)


def local(
    embedding,
    self_weight,
    neighbor_weight,
    up_weight,
    down_weight,
    source_tiles,
    neighbor_rows,
    slot_mask,
    dest_rows,
    owner_order,
    output_grad,
):
    batch_total = lax.axis_size("batch")
    columns, source_total = embedding.shape
    micro_total = source_tiles.shape[0]
    dest_total = dest_rows.shape[1]
    agg_scale = 1.0 / math.sqrt(K * NB)
    norm_factor = 1.0 / math.sqrt(micro_total * dest_total * batch_total)
    tiles_all = source_tiles.reshape(micro_total, -1)

    target_all = gathered_over(output_grad, "feat", 1)
    table = embedding.T
    counts_all, own_all, hidden_all = [], [], []
    for m in range(micro_total):
        counts, agg_t = aggregate(embedding, tiles_all[m], neighbor_rows[m], slot_mask[m], agg_scale)
        own = table[dest_rows[m]]
        partial = jnp.dot(own, self_weight, preferred_element_type=jnp.float32) + lax.dot_general(
            agg_t, neighbor_weight, (((0,), (0,)), ((), ())), preferred_element_type=jnp.float32
        )
        counts_all.append((counts, agg_t))
        own_all.append(own)
        hidden_all.append(summed_over(partial, "feat"))

    up_sum = jnp.zeros(up_weight.shape, jnp.float32)
    down_sum = jnp.zeros(down_weight.shape, jnp.float32)
    self_sum = jnp.zeros((columns, H), jnp.float32)
    neighbor_sum = jnp.zeros((columns, H), jnp.float32)
    table_grad = None
    pending = []
    for m in range(micro_total):
        hidden = hidden_all[m]
        if m > 0:
            hidden, table_grad = lax.optimization_barrier((hidden, table_grad))
        agg_t = counts_all[m][1]
        row_order = owner_order[m, 0]
        target = jnp.zeros(target_all.shape[1:], target_all.dtype).at[row_order].set(target_all[m])
        hidden_grad, up_part, down_part = mlp_pass(hidden, target, up_weight, down_weight)
        up_sum = up_sum + up_part
        down_sum = down_sum + down_part
        self_sum = self_sum + jnp.dot(own_all[m].T, hidden_grad, preferred_element_type=jnp.float32)
        neighbor_sum = neighbor_sum + jnp.dot(agg_t, hidden_grad, preferred_element_type=jnp.float32)
        back = jnp.dot(hidden_grad, neighbor_weight.T, preferred_element_type=jnp.float32).astype(jnp.bfloat16)
        own_grad = jnp.dot(hidden_grad, self_weight.T, preferred_element_type=jnp.float32)
        if m + 1 < micro_total:
            table_grad = spread(
                counts_all[m][0], back, own_grad, dest_rows[m], tiles_all[m], table_grad, agg_scale, source_total
            )
        else:
            pending.append((m, back, own_grad))

    sizes = [up_sum.size, down_sum.size, self_sum.size, neighbor_sum.size]
    line = jnp.concatenate([up_sum.ravel(), down_sum.ravel(), self_sum.ravel(), neighbor_sum.ravel()])
    line = summed_over(line, "batch")
    ends = [0]
    for s in sizes:
        ends.append(ends[-1] + s)
    up_sum = line[ends[0] : ends[1]].reshape(up_weight.shape)
    down_sum = line[ends[1] : ends[2]].reshape(down_weight.shape)
    self_sum = line[ends[2] : ends[3]].reshape(columns, H)
    neighbor_sum = line[ends[3] : ends[4]].reshape(columns, H)

    for m, back, own_grad in pending:
        table_grad = spread(
            counts_all[m][0], back, own_grad, dest_rows[m], tiles_all[m], table_grad, agg_scale, source_total
        )
    return (
        table_grad.T,
        self_sum * norm_factor,
        neighbor_sum * norm_factor,
        up_sum * norm_factor,
        down_sum * norm_factor,
    )


def solution(mesh):
    in_specs = (
        P("feat", "batch"),
        P("feat", None),
        P("feat", None),
        P(),
        P(),
        P(None, None, "batch"),
        P(None, None, None, "batch"),
        P(None, None, "batch"),
        P(None, "batch"),
        P(None, "batch", None),
        P(None, ("batch", "feat"), None),
    )
    out_specs = (P("feat", "batch"), P("feat", None), P("feat", None), P(), P())
    return jax.shard_map(local, mesh=mesh, in_specs=in_specs, out_specs=out_specs, check_vma=False)
```

```python
import functools
import math

import jax
import jax.numpy as jnp
from jax import lax
from jax.experimental import pallas as pl
from jax.experimental.pallas import tpu as pltpu
from jax.sharding import PartitionSpec as P

H = 128
TD = 256
TS = 1024
K = 8
NB = 16
CS = 256


def gelu_slope(values):
    result, pullback = jax.vjp(jax.nn.gelu, values)
    return (result, pullback(jnp.ones_like(values))[0])


def mlp_pass(hidden, target, up_weight, down_weight):
    first_value, first_slope = gelu_slope(hidden)
    first_act = first_value.astype(jnp.bfloat16)
    inner_pre = jnp.dot(first_act, up_weight, preferred_element_type=jnp.float32)
    inner_value, inner_slope = gelu_slope(inner_pre)
    inner_act = inner_value.astype(jnp.bfloat16)
    down_part = jnp.dot(inner_act.T, target, preferred_element_type=jnp.float32)
    inner_grad = (
        jnp.dot(target, down_weight.T, preferred_element_type=jnp.float32) * inner_slope
    ).astype(jnp.bfloat16)
    up_part = jnp.dot(first_act.T, inner_grad, preferred_element_type=jnp.float32)
    hidden_grad = (
        jnp.dot(inner_grad, up_weight.T, preferred_element_type=jnp.float32) * first_slope
    ).astype(jnp.bfloat16)
    return (hidden_grad, up_part, down_part)


def summed_over(x, axis):
    n = lax.axis_size(axis)
    flat = x.reshape(n, -1)
    mine = lax.all_to_all(flat, axis, 0, 0, tiled=True).reshape(n, -1).sum(axis=0)
    spread_back = lax.all_to_all(jnp.broadcast_to(mine[None], (n, mine.size)), axis, 0, 0, tiled=True)
    return spread_back.reshape(x.shape)


def gathered_over(x, axis, dim):
    n = lax.axis_size(axis)
    pieces = lax.all_to_all(jnp.broadcast_to(x[None], (n, *x.shape)), axis, 0, 0, tiled=True)
    pieces = jnp.moveaxis(pieces, 0, dim)
    shape = pieces.shape
    return pieces.reshape(*shape[:dim], shape[dim] * shape[dim + 1], *shape[dim + 2 :])


def agg_kernel(agg_scale, k_total, nt, tiles_ref, emb_ref, rows_ref, mask_ref, counts_ref, agg_ref, acc_ref):
    k = pl.program_id(1)

    @pl.when(k == 0)
    def _():
        acc_ref[...] = jnp.zeros_like(acc_ref)

    msk = mask_ref[0, 0].astype(jnp.bfloat16)
    rows = rows_ref[0, 0]
    local_iota = lax.broadcasted_iota(jnp.int32, (CS, TD), 0).astype(jnp.bfloat16)
    one = jnp.ones((CS, TD), jnp.bfloat16)
    zero = jnp.zeros((CS, TD), jnp.bfloat16)

    def chunk(c, carry):
        start = pl.multiple_of(c * CS, CS)
        local = (rows - start).astype(jnp.float32)
        cnt = zero
        for j in range(0, NB, 2):
            here = local[j : j + 1, :].astype(jnp.bfloat16)
            there = local[j + 1 : j + 2, :].astype(jnp.bfloat16)
            cnt = cnt + (jnp.where(here == local_iota, one, zero) + jnp.where(there == local_iota, one, zero))
        counts_ref[0, 0, pl.ds(start, CS), :] = cnt * msk
        return carry

    lax.fori_loop(0, TS // CS, chunk, 0)
    acc_ref[...] += jnp.dot(emb_ref[...], counts_ref[0, 0], preferred_element_type=jnp.float32)

    @pl.when(k == k_total - 1)
    def _():
        agg_ref[...] = (acc_ref[...] * agg_scale).astype(jnp.bfloat16)


def aggregate(embedding, tiles_flat, neighbor_rows, slot_mask, agg_scale):
    columns, source_total = embedding.shape
    k_total, nb, dest_total = neighbor_rows.shape
    nt = dest_total // TD
    mask4 = slot_mask.reshape(k_total, 1, 1, dest_total)
    rows4 = neighbor_rows.reshape(k_total, 1, nb, dest_total)
    grid_spec = pltpu.PrefetchScalarGridSpec(
        num_scalar_prefetch=1,
        grid=(nt, k_total),
        in_specs=[
            pl.BlockSpec((columns, TS), lambda t, k, tiles: (0, tiles[k * nt + t])),
            pl.BlockSpec((1, 1, nb, TD), lambda t, k, tiles: (k, 0, 0, t)),
            pl.BlockSpec((1, 1, 1, TD), lambda t, k, tiles: (k, 0, 0, t)),
        ],
        out_specs=[
            pl.BlockSpec((1, 1, TS, TD), lambda t, k, tiles: (k, t, 0, 0)),
            pl.BlockSpec((columns, TD), lambda t, k, tiles: (0, t)),
        ],
        scratch_shapes=[pltpu.VMEM((columns, TD), jnp.float32)],
    )
    work = k_total * dest_total * TS
    return pl.pallas_call(
        functools.partial(agg_kernel, agg_scale, k_total, nt),
        grid_spec=grid_spec,
        out_shape=[
            jax.ShapeDtypeStruct((k_total, nt, TS, TD), jnp.bfloat16),
            jax.ShapeDtypeStruct((columns, dest_total), jnp.bfloat16),
        ],
        compiler_params=pltpu.CompilerParams(dimension_semantics=("arbitrary", "arbitrary")),
        cost_estimate=pl.CostEstimate(
            flops=2 * columns * work + 4 * nb * work,
            bytes_accessed=2 * work + 2 * columns * source_total,
            transcendentals=0,
        ),
    )(tiles_flat, embedding, rows4, mask4)


def spread_kernel(agg_scale, k_total, nt, final, tiles_ref, counts_ref, back_ref, own_ref, *refs):
    tg_ref = refs[-1]
    t = pl.program_id(0)
    k = pl.program_id(1)

    @pl.when((t == 0) & (k == 0))
    def _():
        if len(refs) >= 2:
            tg_ref[...] = refs[0][...]
        else:
            tg_ref[...] = jnp.zeros_like(tg_ref)

    tile = tiles_ref[k * nt + t]
    start = pl.multiple_of(tile * TS, TS)
    part = jnp.dot(counts_ref[0, 0], back_ref[...], preferred_element_type=jnp.float32)
    tg_ref[pl.ds(start, TS), :] += part * agg_scale

    @pl.when((t == nt - 1) & (k == k_total - 1))
    def _():
        base = k_total * nt

        def one_row(d, carry):
            row = tiles_ref[base + d]
            tg_ref[pl.ds(row, 1), :] += own_ref[pl.ds(d, 1), :]
            return carry

        lax.fori_loop(0, own_ref.shape[0], one_row, 0, unroll=8)
        if final:
            out_ref = refs[1]
            for i in range(tg_ref.shape[0] // TS):
                out_ref[:, i * TS : (i + 1) * TS] = tg_ref[i * TS : (i + 1) * TS, :].T


def spread(counts, back, own_grad, dest, tiles_flat, table_grad, agg_scale, source_total, final=False):
    k_total, nt = counts.shape[:2]
    columns = back.shape[1]
    prefetch = jnp.concatenate([tiles_flat, dest])
    in_specs = [
        pl.BlockSpec((1, 1, TS, TD), lambda t, k, tiles: (k, t, 0, 0)),
        pl.BlockSpec((TD, columns), lambda t, k, tiles: (t, 0)),
        pl.BlockSpec(own_grad.shape, lambda t, k, tiles: (0, 0)),
    ]
    operands = [prefetch, counts, back, own_grad]
    aliases = {}
    if table_grad is not None:
        in_specs.append(pl.BlockSpec((source_total, columns), lambda t, k, tiles: (0, 0)))
        operands.append(table_grad)
        aliases = {} if final else {4: 0}
    grid_spec = pltpu.PrefetchScalarGridSpec(
        num_scalar_prefetch=1,
        grid=(nt, k_total),
        in_specs=in_specs,
        out_specs=(
            pl.BlockSpec((columns, source_total), lambda t, k, tiles: (0, 0))
            if final
            else pl.BlockSpec((source_total, columns), lambda t, k, tiles: (0, 0))
        ),
        scratch_shapes=[pltpu.VMEM((source_total, columns), jnp.float32)] if final else [],
    )
    work = k_total * nt * TD * TS
    return pl.pallas_call(
        functools.partial(spread_kernel, agg_scale, k_total, nt, final),
        grid_spec=grid_spec,
        out_shape=jax.ShapeDtypeStruct(
            (columns, source_total) if final else (source_total, columns), jnp.float32
        ),
        input_output_aliases=aliases,
        compiler_params=pltpu.CompilerParams(
            dimension_semantics=("arbitrary", "arbitrary"),
            vmem_limit_bytes=48 * 1024 * 1024,
        ),
        cost_estimate=pl.CostEstimate(
            flops=2 * columns * work,
            bytes_accessed=2 * work + 8 * source_total * columns,
            transcendentals=0,
        ),
    )(*operands)


def local(
    embedding,
    self_weight,
    neighbor_weight,
    up_weight,
    down_weight,
    source_tiles,
    neighbor_rows,
    slot_mask,
    dest_rows,
    owner_order,
    output_grad,
):
    batch_total = lax.axis_size("batch")
    columns, source_total = embedding.shape
    micro_total = source_tiles.shape[0]
    dest_total = dest_rows.shape[1]
    agg_scale = 1.0 / math.sqrt(K * NB)
    norm_factor = 1.0 / math.sqrt(micro_total * dest_total * batch_total)
    tiles_all = source_tiles.reshape(micro_total, -1)

    target_all = gathered_over(output_grad, "feat", 1)
    table = embedding.T
    counts_all, own_all, hidden_all = [], [], []
    for m in range(micro_total):
        counts, agg_t = aggregate(embedding, tiles_all[m], neighbor_rows[m], slot_mask[m], agg_scale)
        own = table[dest_rows[m]]
        partial = jnp.dot(own, self_weight, preferred_element_type=jnp.float32) + lax.dot_general(
            agg_t, neighbor_weight, (((0,), (0,)), ((), ())), preferred_element_type=jnp.float32
        )
        counts_all.append((counts, agg_t))
        own_all.append(own)
        hidden_all.append(summed_over(partial, "feat"))

    up_sum = jnp.zeros(up_weight.shape, jnp.float32)
    down_sum = jnp.zeros(down_weight.shape, jnp.float32)
    self_sum = jnp.zeros((columns, H), jnp.float32)
    neighbor_sum = jnp.zeros((columns, H), jnp.float32)
    table_grad = None
    pending = []
    for m in range(micro_total):
        hidden = hidden_all[m]
        if m > 0:
            hidden, table_grad = lax.optimization_barrier((hidden, table_grad))
        agg_t = counts_all[m][1]
        row_order = owner_order[m, 0]
        target = jnp.zeros(target_all.shape[1:], target_all.dtype).at[row_order].set(target_all[m])
        hidden_grad, up_part, down_part = mlp_pass(hidden, target, up_weight, down_weight)
        up_sum = up_sum + up_part
        down_sum = down_sum + down_part
        self_sum = self_sum + jnp.dot(own_all[m].T, hidden_grad, preferred_element_type=jnp.float32)
        neighbor_sum = neighbor_sum + jnp.dot(agg_t, hidden_grad, preferred_element_type=jnp.float32)
        back = jnp.dot(hidden_grad, neighbor_weight.T, preferred_element_type=jnp.float32).astype(jnp.bfloat16)
        own_grad = jnp.dot(hidden_grad, self_weight.T, preferred_element_type=jnp.float32)
        if m + 1 < micro_total:
            table_grad = spread(
                counts_all[m][0], back, own_grad, dest_rows[m], tiles_all[m], table_grad, agg_scale, source_total
            )
        else:
            pending.append((m, back, own_grad))

    sizes = [up_sum.size, down_sum.size, self_sum.size, neighbor_sum.size]
    line = jnp.concatenate([up_sum.ravel(), down_sum.ravel(), self_sum.ravel(), neighbor_sum.ravel()])
    line = summed_over(line, "batch")
    ends = [0]
    for s in sizes:
        ends.append(ends[-1] + s)
    up_sum = line[ends[0] : ends[1]].reshape(up_weight.shape)
    down_sum = line[ends[1] : ends[2]].reshape(down_weight.shape)
    self_sum = line[ends[2] : ends[3]].reshape(columns, H)
    neighbor_sum = line[ends[3] : ends[4]].reshape(columns, H)

    for m, back, own_grad in pending:
        table_grad = spread(
            counts_all[m][0], back, own_grad, dest_rows[m], tiles_all[m], table_grad, agg_scale, source_total,
            final=True,
        )
    return (
        table_grad,
        self_sum * norm_factor,
        neighbor_sum * norm_factor,
        up_sum * norm_factor,
        down_sum * norm_factor,
    )


def solution(mesh):
    in_specs = (
        P("feat", "batch"),
        P("feat", None),
        P("feat", None),
        P(),
        P(),
        P(None, None, "batch"),
        P(None, None, None, "batch"),
        P(None, None, "batch"),
        P(None, "batch"),
        P(None, "batch", None),
        P(None, ("batch", "feat"), None),
    )
    out_specs = (P("feat", "batch"), P("feat", None), P("feat", None), P(), P())
    return jax.shard_map(local, mesh=mesh, in_specs=in_specs, out_specs=out_specs, check_vma=False)
```

```python
import functools
import math

import jax
import jax.numpy as jnp
from jax import lax
from jax.experimental import pallas as pl
from jax.experimental.pallas import tpu as pltpu
from jax.sharding import PartitionSpec as P

H = 128
TD = 256
TS = 1024
K = 8
NB = 16
CS = 256


def gelu_slope(values):
    result, pullback = jax.vjp(jax.nn.gelu, values)
    return (result, pullback(jnp.ones_like(values))[0])


def mlp_pass(hidden, target, up_weight, down_weight):
    first_value, first_slope = gelu_slope(hidden)
    first_act = first_value.astype(jnp.bfloat16)
    inner_pre = jnp.dot(first_act, up_weight, preferred_element_type=jnp.float32)
    inner_value, inner_slope = gelu_slope(inner_pre)
    inner_act = inner_value.astype(jnp.bfloat16)
    down_part = jnp.dot(inner_act.T, target, preferred_element_type=jnp.float32)
    inner_grad = (
        jnp.dot(target, down_weight.T, preferred_element_type=jnp.float32) * inner_slope
    ).astype(jnp.bfloat16)
    up_part = jnp.dot(first_act.T, inner_grad, preferred_element_type=jnp.float32)
    hidden_grad = (
        jnp.dot(inner_grad, up_weight.T, preferred_element_type=jnp.float32) * first_slope
    ).astype(jnp.bfloat16)
    return (hidden_grad, up_part, down_part)


def summed_over(x, axis):
    n = lax.axis_size(axis)
    flat = x.reshape(n, -1)
    mine = lax.all_to_all(flat, axis, 0, 0, tiled=True).reshape(n, -1).sum(axis=0)
    spread_back = lax.all_to_all(jnp.broadcast_to(mine[None], (n, mine.size)), axis, 0, 0, tiled=True)
    return spread_back.reshape(x.shape)


def gathered_over(x, axis, dim):
    n = lax.axis_size(axis)
    pieces = lax.all_to_all(jnp.broadcast_to(x[None], (n, *x.shape)), axis, 0, 0, tiled=True)
    pieces = jnp.moveaxis(pieces, 0, dim)
    shape = pieces.shape
    return pieces.reshape(*shape[:dim], shape[dim] * shape[dim + 1], *shape[dim + 2 :])


def agg_kernel(agg_scale, k_total, nt, tiles_ref, emb_ref, rows_ref, mask_ref, counts_ref, agg_ref, acc_ref):
    k = pl.program_id(1)

    @pl.when(k == 0)
    def _():
        acc_ref[...] = jnp.zeros_like(acc_ref)

    msk = mask_ref[0, 0].astype(jnp.bfloat16)
    rows = rows_ref[0, 0]
    local_iota = lax.broadcasted_iota(jnp.int32, (CS, TD), 0).astype(jnp.bfloat16)
    one = jnp.ones((CS, TD), jnp.bfloat16)
    zero = jnp.zeros((CS, TD), jnp.bfloat16)

    def chunk(c, carry):
        start = pl.multiple_of(c * CS, CS)
        local = (rows - start).astype(jnp.float32)
        cnt = zero
        for j in range(0, NB, 2):
            here = local[j : j + 1, :].astype(jnp.bfloat16)
            there = local[j + 1 : j + 2, :].astype(jnp.bfloat16)
            cnt = cnt + (jnp.where(here == local_iota, one, zero) + jnp.where(there == local_iota, one, zero))
        counts_ref[0, 0, pl.ds(start, CS), :] = cnt * msk
        return carry

    lax.fori_loop(0, TS // CS, chunk, 0)
    acc_ref[...] += jnp.dot(emb_ref[...], counts_ref[0, 0], preferred_element_type=jnp.float32)

    @pl.when(k == k_total - 1)
    def _():
        agg_ref[...] = (acc_ref[...] * agg_scale).astype(jnp.bfloat16)


def aggregate(embedding, tiles_flat, neighbor_rows, slot_mask, agg_scale):
    columns, source_total = embedding.shape
    k_total, nb, dest_total = neighbor_rows.shape
    nt = dest_total // TD
    mask4 = slot_mask.reshape(k_total, 1, 1, dest_total)
    rows4 = neighbor_rows.reshape(k_total, 1, nb, dest_total)
    grid_spec = pltpu.PrefetchScalarGridSpec(
        num_scalar_prefetch=1,
        grid=(nt, k_total),
        in_specs=[
            pl.BlockSpec((columns, TS), lambda t, k, tiles: (0, tiles[k * nt + t])),
            pl.BlockSpec((1, 1, nb, TD), lambda t, k, tiles: (k, 0, 0, t)),
            pl.BlockSpec((1, 1, 1, TD), lambda t, k, tiles: (k, 0, 0, t)),
        ],
        out_specs=[
            pl.BlockSpec((1, 1, TS, TD), lambda t, k, tiles: (k, t, 0, 0)),
            pl.BlockSpec((columns, TD), lambda t, k, tiles: (0, t)),
        ],
        scratch_shapes=[pltpu.VMEM((columns, TD), jnp.float32)],
    )
    work = k_total * dest_total * TS
    return pl.pallas_call(
        functools.partial(agg_kernel, agg_scale, k_total, nt),
        grid_spec=grid_spec,
        out_shape=[
            jax.ShapeDtypeStruct((k_total, nt, TS, TD), jnp.bfloat16),
            jax.ShapeDtypeStruct((columns, dest_total), jnp.bfloat16),
        ],
        compiler_params=pltpu.CompilerParams(dimension_semantics=("arbitrary", "arbitrary")),
        cost_estimate=pl.CostEstimate(
            flops=2 * columns * work + 4 * nb * work,
            bytes_accessed=2 * work + 2 * columns * source_total,
            transcendentals=0,
        ),
    )(tiles_flat, embedding, rows4, mask4)


def spread_kernel(agg_scale, k_total, nt, final, tiles_ref, counts_ref, back_ref, own_ref, *refs):
    tg_ref = refs[-1]
    t = pl.program_id(0)
    k = pl.program_id(1)

    @pl.when((t == 0) & (k == 0))
    def _():
        if len(refs) >= 2:
            tg_ref[...] = refs[0][...]
        else:
            tg_ref[...] = jnp.zeros_like(tg_ref)

    tile = tiles_ref[k * nt + t]
    start = pl.multiple_of(tile * TS, TS)
    part = jnp.dot(counts_ref[0, 0], back_ref[...], preferred_element_type=jnp.float32)
    tg_ref[pl.ds(start, TS), :] += part * agg_scale

    @pl.when((t == nt - 1) & (k == k_total - 1))
    def _():
        base = k_total * nt

        def one_row(d, carry):
            row = tiles_ref[base + d]
            tg_ref[pl.ds(row, 1), :] += own_ref[pl.ds(d, 1), :]
            return carry

        lax.fori_loop(0, own_ref.shape[0], one_row, 0, unroll=8)
        if final:
            out_ref = refs[1]
            for i in range(tg_ref.shape[0] // TS):
                out_ref[:, i * TS : (i + 1) * TS] = tg_ref[i * TS : (i + 1) * TS, :].T


def spread(counts, back, own_grad, dest, tiles_flat, table_grad, agg_scale, source_total, final=False):
    k_total, nt = counts.shape[:2]
    columns = back.shape[1]
    prefetch = jnp.concatenate([tiles_flat, dest])
    in_specs = [
        pl.BlockSpec((1, 1, TS, TD), lambda t, k, tiles: (k, t, 0, 0)),
        pl.BlockSpec((TD, columns), lambda t, k, tiles: (t, 0)),
        pl.BlockSpec(own_grad.shape, lambda t, k, tiles: (0, 0)),
    ]
    operands = [prefetch, counts, back, own_grad]
    aliases = {}
    if table_grad is not None:
        in_specs.append(pl.BlockSpec((source_total, columns), lambda t, k, tiles: (0, 0)))
        operands.append(table_grad)
        aliases = {} if final else {4: 0}
    grid_spec = pltpu.PrefetchScalarGridSpec(
        num_scalar_prefetch=1,
        grid=(nt, k_total),
        in_specs=in_specs,
        out_specs=(
            pl.BlockSpec((columns, source_total), lambda t, k, tiles: (0, 0))
            if final
            else pl.BlockSpec((source_total, columns), lambda t, k, tiles: (0, 0))
        ),
        scratch_shapes=[pltpu.VMEM((source_total, columns), jnp.float32)] if final else [],
    )
    work = k_total * nt * TD * TS
    return pl.pallas_call(
        functools.partial(spread_kernel, agg_scale, k_total, nt, final),
        grid_spec=grid_spec,
        out_shape=jax.ShapeDtypeStruct(
            (columns, source_total) if final else (source_total, columns), jnp.float32
        ),
        input_output_aliases=aliases,
        compiler_params=pltpu.CompilerParams(
            dimension_semantics=("arbitrary", "arbitrary"),
            vmem_limit_bytes=48 * 1024 * 1024,
        ),
        cost_estimate=pl.CostEstimate(
            flops=2 * columns * work,
            bytes_accessed=2 * work + 8 * source_total * columns,
            transcendentals=0,
        ),
    )(*operands)


def local(
    embedding,
    self_weight,
    neighbor_weight,
    up_weight,
    down_weight,
    source_tiles,
    neighbor_rows,
    slot_mask,
    dest_rows,
    owner_order,
    output_grad,
):
    batch_total = lax.axis_size("batch")
    columns, source_total = embedding.shape
    micro_total = source_tiles.shape[0]
    dest_total = dest_rows.shape[1]
    agg_scale = 1.0 / math.sqrt(K * NB)
    norm_factor = 1.0 / math.sqrt(micro_total * dest_total * batch_total)
    tiles_all = source_tiles.reshape(micro_total, -1)

    target_all = gathered_over(output_grad, "feat", 1)
    counts_all, own_all, hidden_all = [], [], []
    for m in range(micro_total):
        counts, agg_t = aggregate(embedding, tiles_all[m], neighbor_rows[m], slot_mask[m], agg_scale)
        own = jnp.take(embedding, dest_rows[m], axis=1)
        partial = lax.dot_general(
            own, self_weight, (((0,), (0,)), ((), ())), preferred_element_type=jnp.float32
        ) + lax.dot_general(
            agg_t, neighbor_weight, (((0,), (0,)), ((), ())), preferred_element_type=jnp.float32
        )
        counts_all.append((counts, agg_t))
        own_all.append(own)
        hidden_all.append(summed_over(partial, "feat"))

    up_sum = jnp.zeros(up_weight.shape, jnp.float32)
    down_sum = jnp.zeros(down_weight.shape, jnp.float32)
    self_sum = jnp.zeros((columns, H), jnp.float32)
    neighbor_sum = jnp.zeros((columns, H), jnp.float32)
    table_grad = None
    pending = []
    for m in range(micro_total):
        hidden = hidden_all[m]
        if m > 0:
            hidden, table_grad = lax.optimization_barrier((hidden, table_grad))
        agg_t = counts_all[m][1]
        row_order = owner_order[m, 0]
        target = jnp.zeros(target_all.shape[1:], target_all.dtype).at[row_order].set(target_all[m])
        hidden_grad, up_part, down_part = mlp_pass(hidden, target, up_weight, down_weight)
        up_sum = up_sum + up_part
        down_sum = down_sum + down_part
        self_sum = self_sum + jnp.dot(own_all[m], hidden_grad, preferred_element_type=jnp.float32)
        neighbor_sum = neighbor_sum + jnp.dot(agg_t, hidden_grad, preferred_element_type=jnp.float32)
        back = jnp.dot(hidden_grad, neighbor_weight.T, preferred_element_type=jnp.float32).astype(jnp.bfloat16)
        own_grad = jnp.dot(hidden_grad, self_weight.T, preferred_element_type=jnp.float32)
        if m + 1 < micro_total:
            table_grad = spread(
                counts_all[m][0], back, own_grad, dest_rows[m], tiles_all[m], table_grad, agg_scale, source_total
            )
        else:
            pending.append((m, back, own_grad))

    sizes = [up_sum.size, down_sum.size, self_sum.size, neighbor_sum.size]
    line = jnp.concatenate([up_sum.ravel(), down_sum.ravel(), self_sum.ravel(), neighbor_sum.ravel()])
    line = summed_over(line, "batch")
    ends = [0]
    for s in sizes:
        ends.append(ends[-1] + s)
    up_sum = line[ends[0] : ends[1]].reshape(up_weight.shape)
    down_sum = line[ends[1] : ends[2]].reshape(down_weight.shape)
    self_sum = line[ends[2] : ends[3]].reshape(columns, H)
    neighbor_sum = line[ends[3] : ends[4]].reshape(columns, H)

    for m, back, own_grad in pending:
        table_grad = spread(
            counts_all[m][0], back, own_grad, dest_rows[m], tiles_all[m], table_grad, agg_scale, source_total,
            final=True,
        )
    return (
        table_grad,
        self_sum * norm_factor,
        neighbor_sum * norm_factor,
        up_sum * norm_factor,
        down_sum * norm_factor,
    )


def solution(mesh):
    in_specs = (
        P("feat", "batch"),
        P("feat", None),
        P("feat", None),
        P(),
        P(),
        P(None, None, "batch"),
        P(None, None, None, "batch"),
        P(None, None, "batch"),
        P(None, "batch"),
        P(None, "batch", None),
        P(None, ("batch", "feat"), None),
    )
    out_specs = (P("feat", "batch"), P("feat", None), P("feat", None), P(), P())
    return jax.shard_map(local, mesh=mesh, in_specs=in_specs, out_specs=out_specs, check_vma=False)
```

```python
import functools
import math

import jax
import jax.numpy as jnp
from jax import lax
from jax.experimental import pallas as pl
from jax.experimental.pallas import tpu as pltpu
from jax.sharding import PartitionSpec as P

H = 128
TD = 256
TS = 1024
K = 8
NB = 16
CS = 256


def gelu_slope(values):
    result, pullback = jax.vjp(jax.nn.gelu, values)
    return (result, pullback(jnp.ones_like(values))[0])


def mlp_pass(hidden, target, up_weight, down_weight):
    first_value, first_slope = gelu_slope(hidden)
    first_act = first_value.astype(jnp.bfloat16)
    inner_pre = jnp.dot(first_act, up_weight, preferred_element_type=jnp.float32)
    inner_value, inner_slope = gelu_slope(inner_pre)
    inner_act = inner_value.astype(jnp.bfloat16)
    down_part = jnp.dot(inner_act.T, target, preferred_element_type=jnp.float32)
    inner_grad = (
        jnp.dot(target, down_weight.T, preferred_element_type=jnp.float32) * inner_slope
    ).astype(jnp.bfloat16)
    up_part = jnp.dot(first_act.T, inner_grad, preferred_element_type=jnp.float32)
    hidden_grad = (
        jnp.dot(inner_grad, up_weight.T, preferred_element_type=jnp.float32) * first_slope
    ).astype(jnp.bfloat16)
    return (hidden_grad, up_part, down_part)


def summed_over(x, axis):
    n = lax.axis_size(axis)
    flat = x.reshape(n, -1)
    mine = lax.all_to_all(flat, axis, 0, 0, tiled=True).reshape(n, -1).sum(axis=0)
    spread_back = lax.all_to_all(jnp.broadcast_to(mine[None], (n, mine.size)), axis, 0, 0, tiled=True)
    return spread_back.reshape(x.shape)


def gathered_over(x, axis, dim):
    n = lax.axis_size(axis)
    pieces = lax.all_to_all(jnp.broadcast_to(x[None], (n, *x.shape)), axis, 0, 0, tiled=True)
    pieces = jnp.moveaxis(pieces, 0, dim)
    shape = pieces.shape
    return pieces.reshape(*shape[:dim], shape[dim] * shape[dim + 1], *shape[dim + 2 :])


def agg_kernel(agg_scale, k_total, nt, tiles_ref, emb_ref, rows_ref, mask_ref, counts_ref, agg_ref, acc_ref):
    k = pl.program_id(1)

    @pl.when(k == 0)
    def _():
        acc_ref[...] = jnp.zeros_like(acc_ref)

    msk = mask_ref[0, 0].astype(jnp.bfloat16)
    rows = rows_ref[0, 0]
    local_iota = lax.broadcasted_iota(jnp.int32, (CS, TD), 0).astype(jnp.bfloat16)
    one = jnp.ones((CS, TD), jnp.bfloat16)
    zero = jnp.zeros((CS, TD), jnp.bfloat16)

    def chunk(c, carry):
        start = pl.multiple_of(c * CS, CS)
        local = (rows - start).astype(jnp.float32)
        cnt = zero
        for j in range(0, NB, 2):
            here = local[j : j + 1, :].astype(jnp.bfloat16)
            there = local[j + 1 : j + 2, :].astype(jnp.bfloat16)
            cnt = cnt + ((here == local_iota).astype(jnp.bfloat16) + (there == local_iota).astype(jnp.bfloat16))
        counts_ref[0, 0, pl.ds(start, CS), :] = cnt * msk
        return carry

    lax.fori_loop(0, TS // CS, chunk, 0)
    acc_ref[...] += jnp.dot(emb_ref[...], counts_ref[0, 0], preferred_element_type=jnp.float32)

    @pl.when(k == k_total - 1)
    def _():
        agg_ref[...] = (acc_ref[...] * agg_scale).astype(jnp.bfloat16)


def aggregate(embedding, tiles_flat, neighbor_rows, slot_mask, agg_scale):
    columns, source_total = embedding.shape
    k_total, nb, dest_total = neighbor_rows.shape
    nt = dest_total // TD
    mask4 = slot_mask.reshape(k_total, 1, 1, dest_total)
    rows4 = neighbor_rows.reshape(k_total, 1, nb, dest_total)
    grid_spec = pltpu.PrefetchScalarGridSpec(
        num_scalar_prefetch=1,
        grid=(nt, k_total),
        in_specs=[
            pl.BlockSpec((columns, TS), lambda t, k, tiles: (0, tiles[k * nt + t])),
            pl.BlockSpec((1, 1, nb, TD), lambda t, k, tiles: (k, 0, 0, t)),
            pl.BlockSpec((1, 1, 1, TD), lambda t, k, tiles: (k, 0, 0, t)),
        ],
        out_specs=[
            pl.BlockSpec((1, 1, TS, TD), lambda t, k, tiles: (k, t, 0, 0)),
            pl.BlockSpec((columns, TD), lambda t, k, tiles: (0, t)),
        ],
        scratch_shapes=[pltpu.VMEM((columns, TD), jnp.float32)],
    )
    work = k_total * dest_total * TS
    return pl.pallas_call(
        functools.partial(agg_kernel, agg_scale, k_total, nt),
        grid_spec=grid_spec,
        out_shape=[
            jax.ShapeDtypeStruct((k_total, nt, TS, TD), jnp.bfloat16),
            jax.ShapeDtypeStruct((columns, dest_total), jnp.bfloat16),
        ],
        compiler_params=pltpu.CompilerParams(dimension_semantics=("arbitrary", "arbitrary")),
        cost_estimate=pl.CostEstimate(
            flops=2 * columns * work + 4 * nb * work,
            bytes_accessed=2 * work + 2 * columns * source_total,
            transcendentals=0,
        ),
    )(tiles_flat, embedding, rows4, mask4)


def spread_kernel(agg_scale, k_total, nt, final, tiles_ref, counts_ref, back_ref, own_ref, *refs):
    tg_ref = refs[-1]
    t = pl.program_id(0)
    k = pl.program_id(1)

    @pl.when((t == 0) & (k == 0))
    def _():
        if len(refs) >= 2:
            tg_ref[...] = refs[0][...]
        else:
            tg_ref[...] = jnp.zeros_like(tg_ref)

    tile = tiles_ref[k * nt + t]
    start = pl.multiple_of(tile * TS, TS)
    part = jnp.dot(counts_ref[0, 0], back_ref[...], preferred_element_type=jnp.float32)
    tg_ref[pl.ds(start, TS), :] += part * agg_scale

    @pl.when((t == nt - 1) & (k == k_total - 1))
    def _():
        base = k_total * nt

        def one_row(d, carry):
            row = tiles_ref[base + d]
            tg_ref[pl.ds(row, 1), :] += own_ref[pl.ds(d, 1), :]
            return carry

        lax.fori_loop(0, own_ref.shape[0], one_row, 0, unroll=8)
        if final:
            out_ref = refs[1]
            for i in range(tg_ref.shape[0] // TS):
                out_ref[:, i * TS : (i + 1) * TS] = tg_ref[i * TS : (i + 1) * TS, :].T


def spread(counts, back, own_grad, dest, tiles_flat, table_grad, agg_scale, source_total, final=False):
    k_total, nt = counts.shape[:2]
    columns = back.shape[1]
    prefetch = jnp.concatenate([tiles_flat, dest])
    in_specs = [
        pl.BlockSpec((1, 1, TS, TD), lambda t, k, tiles: (k, t, 0, 0)),
        pl.BlockSpec((TD, columns), lambda t, k, tiles: (t, 0)),
        pl.BlockSpec(own_grad.shape, lambda t, k, tiles: (0, 0)),
    ]
    operands = [prefetch, counts, back, own_grad]
    aliases = {}
    if table_grad is not None:
        in_specs.append(pl.BlockSpec((source_total, columns), lambda t, k, tiles: (0, 0)))
        operands.append(table_grad)
        aliases = {} if final else {4: 0}
    grid_spec = pltpu.PrefetchScalarGridSpec(
        num_scalar_prefetch=1,
        grid=(nt, k_total),
        in_specs=in_specs,
        out_specs=(
            pl.BlockSpec((columns, source_total), lambda t, k, tiles: (0, 0))
            if final
            else pl.BlockSpec((source_total, columns), lambda t, k, tiles: (0, 0))
        ),
        scratch_shapes=[pltpu.VMEM((source_total, columns), jnp.float32)] if final else [],
    )
    work = k_total * nt * TD * TS
    return pl.pallas_call(
        functools.partial(spread_kernel, agg_scale, k_total, nt, final),
        grid_spec=grid_spec,
        out_shape=jax.ShapeDtypeStruct(
            (columns, source_total) if final else (source_total, columns), jnp.float32
        ),
        input_output_aliases=aliases,
        compiler_params=pltpu.CompilerParams(
            dimension_semantics=("arbitrary", "arbitrary"),
            vmem_limit_bytes=48 * 1024 * 1024,
        ),
        cost_estimate=pl.CostEstimate(
            flops=2 * columns * work,
            bytes_accessed=2 * work + 8 * source_total * columns,
            transcendentals=0,
        ),
    )(*operands)


def local(
    embedding,
    self_weight,
    neighbor_weight,
    up_weight,
    down_weight,
    source_tiles,
    neighbor_rows,
    slot_mask,
    dest_rows,
    owner_order,
    output_grad,
):
    batch_total = lax.axis_size("batch")
    columns, source_total = embedding.shape
    micro_total = source_tiles.shape[0]
    dest_total = dest_rows.shape[1]
    agg_scale = 1.0 / math.sqrt(K * NB)
    norm_factor = 1.0 / math.sqrt(micro_total * dest_total * batch_total)
    tiles_all = source_tiles.reshape(micro_total, -1)

    target_all = gathered_over(output_grad, "feat", 1)
    table = embedding.T
    counts_all, own_all, hidden_all = [], [], []
    for m in range(micro_total):
        counts, agg_t = aggregate(embedding, tiles_all[m], neighbor_rows[m], slot_mask[m], agg_scale)
        own = table[dest_rows[m]]
        partial = jnp.dot(own, self_weight, preferred_element_type=jnp.float32) + lax.dot_general(
            agg_t, neighbor_weight, (((0,), (0,)), ((), ())), preferred_element_type=jnp.float32
        )
        counts_all.append((counts, agg_t))
        own_all.append(own)
        hidden_all.append(summed_over(partial, "feat"))

    up_sum = jnp.zeros(up_weight.shape, jnp.float32)
    down_sum = jnp.zeros(down_weight.shape, jnp.float32)
    self_sum = jnp.zeros((columns, H), jnp.float32)
    neighbor_sum = jnp.zeros((columns, H), jnp.float32)
    table_grad = None
    pending = []
    for m in range(micro_total):
        hidden = hidden_all[m]
        if m > 0:
            hidden, table_grad = lax.optimization_barrier((hidden, table_grad))
        agg_t = counts_all[m][1]
        row_order = owner_order[m, 0]
        target = jnp.zeros(target_all.shape[1:], target_all.dtype).at[row_order].set(target_all[m])
        hidden_grad, up_part, down_part = mlp_pass(hidden, target, up_weight, down_weight)
        up_sum = up_sum + up_part
        down_sum = down_sum + down_part
        self_sum = self_sum + jnp.dot(own_all[m].T, hidden_grad, preferred_element_type=jnp.float32)
        neighbor_sum = neighbor_sum + jnp.dot(agg_t, hidden_grad, preferred_element_type=jnp.float32)
        back = jnp.dot(hidden_grad, neighbor_weight.T, preferred_element_type=jnp.float32).astype(jnp.bfloat16)
        own_grad = jnp.dot(hidden_grad, self_weight.T, preferred_element_type=jnp.float32)
        if m + 1 < micro_total:
            table_grad = spread(
                counts_all[m][0], back, own_grad, dest_rows[m], tiles_all[m], table_grad, agg_scale, source_total
            )
        else:
            pending.append((m, back, own_grad))

    sizes = [up_sum.size, down_sum.size, self_sum.size, neighbor_sum.size]
    line = jnp.concatenate([up_sum.ravel(), down_sum.ravel(), self_sum.ravel(), neighbor_sum.ravel()])
    line = summed_over(line, "batch")
    ends = [0]
    for s in sizes:
        ends.append(ends[-1] + s)
    up_sum = line[ends[0] : ends[1]].reshape(up_weight.shape)
    down_sum = line[ends[1] : ends[2]].reshape(down_weight.shape)
    self_sum = line[ends[2] : ends[3]].reshape(columns, H)
    neighbor_sum = line[ends[3] : ends[4]].reshape(columns, H)

    for m, back, own_grad in pending:
        table_grad = spread(
            counts_all[m][0], back, own_grad, dest_rows[m], tiles_all[m], table_grad, agg_scale, source_total,
            final=True,
        )
    return (
        table_grad,
        self_sum * norm_factor,
        neighbor_sum * norm_factor,
        up_sum * norm_factor,
        down_sum * norm_factor,
    )


def solution(mesh):
    in_specs = (
        P("feat", "batch"),
        P("feat", None),
        P("feat", None),
        P(),
        P(),
        P(None, None, "batch"),
        P(None, None, None, "batch"),
        P(None, None, "batch"),
        P(None, "batch"),
        P(None, "batch", None),
        P(None, ("batch", "feat"), None),
    )
    out_specs = (P("feat", "batch"), P("feat", None), P("feat", None), P(), P())
    return jax.shard_map(local, mesh=mesh, in_specs=in_specs, out_specs=out_specs, check_vma=False)
```

```python
import functools
import math

import jax
import jax.numpy as jnp
from jax import lax
from jax.experimental import pallas as pl
from jax.experimental.pallas import tpu as pltpu
from jax.sharding import PartitionSpec as P

H = 128
TD = 256
TS = 1024
K = 8
NB = 16
CS = 256


def gelu_slope(values):
    result, pullback = jax.vjp(jax.nn.gelu, values)
    return (result, pullback(jnp.ones_like(values))[0])


def mlp_pass(hidden, target, up_weight, down_weight):
    first_value, first_slope = gelu_slope(hidden)
    first_act = first_value.astype(jnp.bfloat16)
    inner_pre = jnp.dot(first_act, up_weight, preferred_element_type=jnp.float32)
    inner_value, inner_slope = gelu_slope(inner_pre)
    inner_act = inner_value.astype(jnp.bfloat16)
    down_part = jnp.dot(inner_act.T, target, preferred_element_type=jnp.float32)
    inner_grad = (
        jnp.dot(target, down_weight.T, preferred_element_type=jnp.float32) * inner_slope
    ).astype(jnp.bfloat16)
    up_part = jnp.dot(first_act.T, inner_grad, preferred_element_type=jnp.float32)
    hidden_grad = (
        jnp.dot(inner_grad, up_weight.T, preferred_element_type=jnp.float32) * first_slope
    ).astype(jnp.bfloat16)
    return (hidden_grad, up_part, down_part)


def summed_over(x, axis):
    n = lax.axis_size(axis)
    flat = x.reshape(n, -1)
    mine = lax.all_to_all(flat, axis, 0, 0, tiled=True).reshape(n, -1).sum(axis=0)
    spread_back = lax.all_to_all(jnp.broadcast_to(mine[None], (n, mine.size)), axis, 0, 0, tiled=True)
    return spread_back.reshape(x.shape)


def gathered_over(x, axis, dim):
    n = lax.axis_size(axis)
    pieces = lax.all_to_all(jnp.broadcast_to(x[None], (n, *x.shape)), axis, 0, 0, tiled=True)
    pieces = jnp.moveaxis(pieces, 0, dim)
    shape = pieces.shape
    return pieces.reshape(*shape[:dim], shape[dim] * shape[dim + 1], *shape[dim + 2 :])


def agg_kernel(agg_scale, k_total, nt, tiles_ref, emb_ref, rows_ref, mask_ref, counts_ref, agg_ref, acc_ref):
    k = pl.program_id(1)

    @pl.when(k == 0)
    def _():
        acc_ref[...] = jnp.zeros_like(acc_ref)

    msk = mask_ref[0, 0].astype(jnp.bfloat16)
    rows = rows_ref[0, 0]
    local_iota = lax.broadcasted_iota(jnp.int32, (CS, TD), 0).astype(jnp.bfloat16)
    one = jnp.ones((CS, TD), jnp.bfloat16)
    zero = jnp.zeros((CS, TD), jnp.bfloat16)

    def chunk(c, carry):
        start = pl.multiple_of(c * CS, CS)
        local = (rows - start).astype(jnp.float32)
        cnt = zero
        for j in range(0, NB, 2):
            here = local[j : j + 1, :].astype(jnp.bfloat16)
            there = local[j + 1 : j + 2, :].astype(jnp.bfloat16)
            cnt = cnt + (jnp.where(here == local_iota, one, zero) + jnp.where(there == local_iota, one, zero))
        counts_ref[0, 0, pl.ds(start, CS), :] = cnt * msk
        return carry

    lax.fori_loop(0, TS // CS, chunk, 0)
    acc_ref[...] += jnp.dot(emb_ref[...], counts_ref[0, 0], preferred_element_type=jnp.float32)

    @pl.when(k == k_total - 1)
    def _():
        agg_ref[...] = (acc_ref[...] * agg_scale).astype(jnp.bfloat16)


def aggregate(embedding, tiles_flat, neighbor_rows, slot_mask, agg_scale):
    columns, source_total = embedding.shape
    k_total, nb, dest_total = neighbor_rows.shape
    nt = dest_total // TD
    mask4 = slot_mask.reshape(k_total, 1, 1, dest_total)
    rows4 = neighbor_rows.reshape(k_total, 1, nb, dest_total)
    grid_spec = pltpu.PrefetchScalarGridSpec(
        num_scalar_prefetch=1,
        grid=(nt, k_total),
        in_specs=[
            pl.BlockSpec((columns, TS), lambda t, k, tiles: (0, tiles[k * nt + t])),
            pl.BlockSpec((1, 1, nb, TD), lambda t, k, tiles: (k, 0, 0, t)),
            pl.BlockSpec((1, 1, 1, TD), lambda t, k, tiles: (k, 0, 0, t)),
        ],
        out_specs=[
            pl.BlockSpec((1, 1, TS, TD), lambda t, k, tiles: (k, t, 0, 0)),
            pl.BlockSpec((columns, TD), lambda t, k, tiles: (0, t)),
        ],
        scratch_shapes=[pltpu.VMEM((columns, TD), jnp.float32)],
    )
    work = k_total * dest_total * TS
    return pl.pallas_call(
        functools.partial(agg_kernel, agg_scale, k_total, nt),
        grid_spec=grid_spec,
        out_shape=[
            jax.ShapeDtypeStruct((k_total, nt, TS, TD), jnp.bfloat16),
            jax.ShapeDtypeStruct((columns, dest_total), jnp.bfloat16),
        ],
        compiler_params=pltpu.CompilerParams(dimension_semantics=("arbitrary", "arbitrary")),
        cost_estimate=pl.CostEstimate(
            flops=2 * columns * work + 4 * nb * work,
            bytes_accessed=2 * work + 2 * columns * source_total,
            transcendentals=0,
        ),
    )(tiles_flat, embedding, rows4, mask4)


def spread_kernel(agg_scale, k_total, nt, final, tiles_ref, counts_ref, back_ref, own_ref, *refs):
    tg_ref = refs[-1]
    t = pl.program_id(0)
    k = pl.program_id(1)

    @pl.when((t == 0) & (k == 0))
    def _():
        if len(refs) >= 2:
            tg_ref[...] = refs[0][...]
        else:
            tg_ref[...] = jnp.zeros_like(tg_ref)

    tile = tiles_ref[k * nt + t]
    start = pl.multiple_of(tile * TS, TS)
    part = jnp.dot(counts_ref[0, 0], back_ref[...], preferred_element_type=jnp.float32)
    tg_ref[pl.ds(start, TS), :] += part * agg_scale

    @pl.when((t == nt - 1) & (k == k_total - 1))
    def _():
        base = k_total * nt

        def one_row(d, carry):
            row = tiles_ref[base + d]
            tg_ref[pl.ds(row, 1), :] += own_ref[pl.ds(d, 1), :]
            return carry

        lax.fori_loop(0, own_ref.shape[0], one_row, 0, unroll=32)
        if final:
            out_ref = refs[1]
            for i in range(tg_ref.shape[0] // TS):
                out_ref[:, i * TS : (i + 1) * TS] = tg_ref[i * TS : (i + 1) * TS, :].T


def spread(counts, back, own_grad, dest, tiles_flat, table_grad, agg_scale, source_total, final=False):
    k_total, nt = counts.shape[:2]
    columns = back.shape[1]
    prefetch = jnp.concatenate([tiles_flat, dest])
    in_specs = [
        pl.BlockSpec((1, 1, TS, TD), lambda t, k, tiles: (k, t, 0, 0)),
        pl.BlockSpec((TD, columns), lambda t, k, tiles: (t, 0)),
        pl.BlockSpec(own_grad.shape, lambda t, k, tiles: (0, 0)),
    ]
    operands = [prefetch, counts, back, own_grad]
    aliases = {}
    if table_grad is not None:
        in_specs.append(pl.BlockSpec((source_total, columns), lambda t, k, tiles: (0, 0)))
        operands.append(table_grad)
        aliases = {} if final else {4: 0}
    grid_spec = pltpu.PrefetchScalarGridSpec(
        num_scalar_prefetch=1,
        grid=(nt, k_total),
        in_specs=in_specs,
        out_specs=(
            pl.BlockSpec((columns, source_total), lambda t, k, tiles: (0, 0))
            if final
            else pl.BlockSpec((source_total, columns), lambda t, k, tiles: (0, 0))
        ),
        scratch_shapes=[pltpu.VMEM((source_total, columns), jnp.float32)] if final else [],
    )
    work = k_total * nt * TD * TS
    return pl.pallas_call(
        functools.partial(spread_kernel, agg_scale, k_total, nt, final),
        grid_spec=grid_spec,
        out_shape=jax.ShapeDtypeStruct(
            (columns, source_total) if final else (source_total, columns), jnp.float32
        ),
        input_output_aliases=aliases,
        compiler_params=pltpu.CompilerParams(
            dimension_semantics=("arbitrary", "arbitrary"),
            vmem_limit_bytes=48 * 1024 * 1024,
        ),
        cost_estimate=pl.CostEstimate(
            flops=2 * columns * work,
            bytes_accessed=2 * work + 8 * source_total * columns,
            transcendentals=0,
        ),
    )(*operands)


def local(
    embedding,
    self_weight,
    neighbor_weight,
    up_weight,
    down_weight,
    source_tiles,
    neighbor_rows,
    slot_mask,
    dest_rows,
    owner_order,
    output_grad,
):
    batch_total = lax.axis_size("batch")
    columns, source_total = embedding.shape
    micro_total = source_tiles.shape[0]
    dest_total = dest_rows.shape[1]
    agg_scale = 1.0 / math.sqrt(K * NB)
    norm_factor = 1.0 / math.sqrt(micro_total * dest_total * batch_total)
    tiles_all = source_tiles.reshape(micro_total, -1)

    target_all = gathered_over(output_grad, "feat", 1)
    table = embedding.T
    counts_all, own_all, hidden_all = [], [], []
    for m in range(micro_total):
        counts, agg_t = aggregate(embedding, tiles_all[m], neighbor_rows[m], slot_mask[m], agg_scale)
        own = table[dest_rows[m]]
        partial = jnp.dot(own, self_weight, preferred_element_type=jnp.float32) + lax.dot_general(
            agg_t, neighbor_weight, (((0,), (0,)), ((), ())), preferred_element_type=jnp.float32
        )
        counts_all.append((counts, agg_t))
        own_all.append(own)
        hidden_all.append(summed_over(partial, "feat"))

    up_sum = jnp.zeros(up_weight.shape, jnp.float32)
    down_sum = jnp.zeros(down_weight.shape, jnp.float32)
    self_sum = jnp.zeros((columns, H), jnp.float32)
    neighbor_sum = jnp.zeros((columns, H), jnp.float32)
    table_grad = None
    pending = []
    for m in range(micro_total):
        hidden = hidden_all[m]
        if m > 0:
            hidden, table_grad = lax.optimization_barrier((hidden, table_grad))
        agg_t = counts_all[m][1]
        row_order = owner_order[m, 0]
        target = jnp.zeros(target_all.shape[1:], target_all.dtype).at[row_order].set(target_all[m])
        hidden_grad, up_part, down_part = mlp_pass(hidden, target, up_weight, down_weight)
        up_sum = up_sum + up_part
        down_sum = down_sum + down_part
        self_sum = self_sum + jnp.dot(own_all[m].T, hidden_grad, preferred_element_type=jnp.float32)
        neighbor_sum = neighbor_sum + jnp.dot(agg_t, hidden_grad, preferred_element_type=jnp.float32)
        back = jnp.dot(hidden_grad, neighbor_weight.T, preferred_element_type=jnp.float32).astype(jnp.bfloat16)
        own_grad = jnp.dot(hidden_grad, self_weight.T, preferred_element_type=jnp.float32)
        if m + 1 < micro_total:
            table_grad = spread(
                counts_all[m][0], back, own_grad, dest_rows[m], tiles_all[m], table_grad, agg_scale, source_total
            )
        else:
            pending.append((m, back, own_grad))

    sizes = [up_sum.size, down_sum.size, self_sum.size, neighbor_sum.size]
    line = jnp.concatenate([up_sum.ravel(), down_sum.ravel(), self_sum.ravel(), neighbor_sum.ravel()])
    line = summed_over(line, "batch")
    ends = [0]
    for s in sizes:
        ends.append(ends[-1] + s)
    up_sum = line[ends[0] : ends[1]].reshape(up_weight.shape)
    down_sum = line[ends[1] : ends[2]].reshape(down_weight.shape)
    self_sum = line[ends[2] : ends[3]].reshape(columns, H)
    neighbor_sum = line[ends[3] : ends[4]].reshape(columns, H)

    for m, back, own_grad in pending:
        table_grad = spread(
            counts_all[m][0], back, own_grad, dest_rows[m], tiles_all[m], table_grad, agg_scale, source_total,
            final=True,
        )
    return (
        table_grad,
        self_sum * norm_factor,
        neighbor_sum * norm_factor,
        up_sum * norm_factor,
        down_sum * norm_factor,
    )


def solution(mesh):
    in_specs = (
        P("feat", "batch"),
        P("feat", None),
        P("feat", None),
        P(),
        P(),
        P(None, None, "batch"),
        P(None, None, None, "batch"),
        P(None, None, "batch"),
        P(None, "batch"),
        P(None, "batch", None),
        P(None, ("batch", "feat"), None),
    )
    out_specs = (P("feat", "batch"), P("feat", None), P("feat", None), P(), P())
    return jax.shard_map(local, mesh=mesh, in_specs=in_specs, out_specs=out_specs, check_vma=False)
```
